32 devices in a mesh: depth: 4 (over z), dp: 8 (over y, x, core).
Axes of the slice: x: 2, y: 2, z: 4, core: 2. Of those that a mesh axis runs over, the one named last changes fastest.
Arguments:
- layer_inputs: float32 [4, 3072, 2048], P('depth', 'dp'), may hold values from -6 to 6
- weights: float32 [4, 2048, 2048], P('depth', 'dp'), may hold values from -6 to 6
- offsets: float32 [4, 2048], P('depth', 'dp'), may hold values from -3 to 3
- layer_outputs: float32 [4, 3072, 2048], P('depth', 'dp'), may hold values from 0 to 2
- multipliers: float32 [4, 3072, 2048], P('depth', 'dp'), may hold values from -3 to 3
Outputs:
- new_inputs: float32 [4, 3072, 2048], P('depth', 'dp')
- new_weights: float32 [4, 2048, 2048], P('depth', 'dp')
- new_offsets: float32 [4, 2048], P('depth', 'dp')
- new_outputs: float32 [4, 3072, 2048], P('depth', 'dp')
- new_multipliers: float32 [4, 3072, 2048], P('depth', 'dp')
The draws below stay inside these ranges and needn't reach their ends.
All inputs are finite; a program needn't handle non-finite values.
Results may differ from the reference program's by a relative error of at most 0.00008.
Values sent between devices are 32-bit elements; how exact they have to be, the bound alone decides.
A program may use at most 128 MiB of HBM per device.

```python
import math
import jax
import jax.numpy as jnp
from jax import lax

D = 2048
LAYERS = 4
SAMPLES = 3072


def block_scale(key, extent, pieces, smallest, high):
    level = 1.0
    for position, parts in pieces:
        draws = jax.random.uniform(jax.random.fold_in(jax.random.fold_in(key, 6), position), (parts,), jnp.float32, smallest / len(pieces), high / len(pieces))
        level = level * jnp.repeat(jnp.exp(draws), extent[position] // parts).reshape((-1,) + (1,) * (len(extent) - 1 - position))
    return level


def centred(key, shape, spread, most, shards=(), held_as=jnp.bfloat16):
    result = jax.random.normal(key, shape, jnp.float32) * spread
    if len(shards) > 0:
        result = block_scale(key, shape, shards, -0.22, 0.18) * result
    return jnp.clip(result, min=-most, max=most).astype(held_as)


def setup_inputs(seed: int = 0) -> dict:
    streams_of = jax.random.split(jax.random.key(seed), 6)
    return {
        "layer_inputs": centred(streams_of[0], (LAYERS, SAMPLES, D), 1.0, 6.0, ((0, 4), (1, 8)), jnp.float32),
        "weights": centred(streams_of[1], (LAYERS, D, D), 1.0, 6.0, ((0, 4), (1, 8)), jnp.float32),
        "offsets": centred(streams_of[2], (LAYERS, D), 0.5, 3.0, ((0, 4), (1, 8)), jnp.float32),
        "layer_outputs": jnp.clip(2.0 * jax.random.uniform(streams_of[3], (LAYERS, SAMPLES, D), jnp.float32) ** block_scale(streams_of[3], (LAYERS, SAMPLES, D), ((0, 4), (1, 8)), -0.2, 0.2), 0.0, 2.0),
        "multipliers": centred(streams_of[4], (LAYERS, SAMPLES, D), 0.5, 3.0, ((0, 4), (1, 8)), jnp.float32),
    }


fit_weight = 1.0
penalty = 1.0
step_input = 0.5

def reference(layer_inputs, weights, offsets, layer_outputs, multipliers):
    highest = lax.Precision.HIGHEST
    scaling = 1.0 / math.sqrt(D)
    samples = layer_inputs.shape[1]
    step_weight = 8.0 / math.sqrt(samples)
    step_offset = 0.5 / math.sqrt(samples)
    affine = scaling * jnp.einsum('lsd,lkd->lsk', layer_inputs, weights, precision=highest) + offsets[:, None, :]
    misfit = affine - layer_outputs
    pulled = scaling * jnp.einsum('lsk,lkd->lsd', misfit, weights, precision=highest)
    zero_layer = jnp.zeros_like(layer_inputs[:1])
    prev_outputs = jnp.concatenate([zero_layer, layer_outputs[:-1]], axis=0)
    prev_multipliers = jnp.concatenate([zero_layer, multipliers[:-1]], axis=0)
    gradient = fit_weight * pulled + prev_multipliers + penalty * (layer_inputs - prev_outputs)
    stepped = layer_inputs - step_input * gradient
    layer_ids = jnp.arange(layer_inputs.shape[0])[:, None, None]
    new_inputs = jnp.where(layer_ids == 0, layer_inputs, stepped)
    weight_grad = fit_weight * scaling * jnp.einsum('lsk,lsd->lkd', misfit, layer_inputs, precision=highest)
    new_weights = weights - step_weight * weight_grad
    new_offsets = offsets - step_offset * fit_weight * lax.optimization_barrier(jnp.sum(misfit, axis=1))
    next_inputs = jnp.concatenate([new_inputs[1:], zero_layer], axis=0)
    is_last = layer_ids == layer_inputs.shape[0] - 1
    coupled = jnp.maximum(0.0, (fit_weight * affine + penalty * next_inputs + multipliers) / (fit_weight + penalty))
    new_outputs = jnp.where(is_last, jnp.maximum(0.0, affine), coupled)
    new_multipliers = jnp.where(is_last, multipliers, multipliers + penalty * (next_inputs - new_outputs))
    return (new_inputs, new_weights, new_offsets, new_outputs, new_multipliers)
```

```python
import functools
import math

import jax
import jax.numpy as jnp
from jax import lax
from jax.experimental import pallas as pl
from jax.experimental.pallas import tpu as pltpu
from jax.sharding import PartitionSpec as P

fit_weight = 1.0
penalty = 1.0
step_input = 0.5
PRECISION = lax.Precision.HIGH


def passed_along(block, axis, distance):
    devices = range(lax.axis_size(axis))
    route = [(i - distance, i) for i in devices if i - distance in devices]
    return lax.ppermute(block, axis, route)


def swapped(block, bit):
    route = [(i, i ^ bit) for i in range(lax.axis_size("dp"))]
    return lax.ppermute(block, "dp", route)


def dot(a, b, dims):
    return lax.dot_general(a, b, (dims, ((), ())), precision=PRECISION)


def times_transposed(a, b):
    return dot(a, b, ((1,), (1,)))


def times(a, b):
    return dot(a, b, ((1,), (0,)))


def transposed_times(a, b):
    return dot(a, b, ((0,), (0,)))


def finish(inputs, outputs, mults, drive, prev_drive, affine, pulled_step, next_step):
    layer_index = lax.axis_index("depth")
    is_first = layer_index == 0
    is_last = layer_index == lax.axis_size("depth") - 1
    inputs_new = jnp.where(is_first, inputs, pulled_step - step_input * prev_drive)
    next_inputs = next_step - step_input * drive
    coupled = jnp.maximum(
        0.0, (fit_weight * affine + penalty * next_inputs + mults) / (fit_weight + penalty)
    )
    outputs_new = jnp.where(is_last, jnp.maximum(0.0, affine), coupled)
    mults_new = jnp.where(is_last, mults, mults + penalty * (next_inputs - outputs_new))
    return inputs_new, outputs_new, mults_new


def body_general(layer_inputs, weights, offsets, layer_outputs, multipliers):
    inputs, outputs, mults = layer_inputs[0], layer_outputs[0], multipliers[0]
    scaling = 1.0 / math.sqrt(inputs.shape[1])
    samples = inputs.shape[0] * lax.axis_size("dp")
    step_weight = 8.0 / math.sqrt(samples)
    step_offset = 0.5 / math.sqrt(samples)
    drive = mults - penalty * outputs
    prev_drive = passed_along(drive, "depth", 1)
    weight = lax.all_gather(weights[0], "dp", axis=0, tiled=True)
    offset = lax.all_gather(offsets, "dp", axis=1, tiled=True)
    affine = scaling * times_transposed(inputs, weight) + offset
    misfit = affine - outputs
    weight_grad = fit_weight * scaling * transposed_times(misfit, inputs)
    weight_sum = lax.psum_scatter(weight_grad, "dp", scatter_dimension=0, tiled=True)
    offset_sum = lax.psum_scatter(
        fit_weight * jnp.sum(misfit, axis=0), "dp", scatter_dimension=0, tiled=True
    )
    pulled = scaling * times(misfit, weight)
    pulled_step = inputs - step_input * (fit_weight * pulled + penalty * inputs)
    next_step = passed_along(pulled_step, "depth", -1)
    inputs_new, outputs_new, mults_new = finish(
        inputs, outputs, mults, drive, prev_drive, affine, pulled_step, next_step
    )
    weights_new = weights - step_weight * weight_sum[None]
    offsets_new = offsets - step_offset * offset_sum[None]
    return inputs_new[None], weights_new, offsets_new, outputs_new[None], mults_new[None]


def body_square(layer_inputs, weights, offsets, layer_outputs, multipliers):
    inputs, outputs, mults = layer_inputs[0], layer_outputs[0], multipliers[0]
    rows, width = inputs.shape
    units = weights.shape[1]
    half = units // 2
    scaling = 1.0 / math.sqrt(width)
    samples = rows * lax.axis_size("dp")
    step_weight = 8.0 / math.sqrt(samples)
    step_offset = 0.5 / math.sqrt(samples)
    me = lax.axis_index("dp")

    w_own = weights[0]
    low_own, high_own = w_own[:half], w_own[half:]
    low_own, high_own, inputs = lax.optimization_barrier((low_own, high_own, inputs))
    low_x, high_y = swapped(low_own, 2), swapped(high_own, 4)
    inputs_other = swapped(inputs, 1)
    inputs_other, outputs_late = lax.optimization_barrier((inputs_other, outputs))
    drive = mults - penalty * outputs
    prev_drive = passed_along(drive, "depth", 1)
    b_own = offsets
    b_x, b_y, b_d = swapped(b_own, 2), swapped(b_own, 4), swapped(b_own, 6)

    def columns(array, index):
        return lax.dynamic_slice(array, (0, index * units), (rows, units))

    def arranged(own, x, y, d):
        joined_a = jnp.concatenate([x[:, :half], y[:, half:]], axis=1)
        joined_b = jnp.concatenate([x[:, half:], y[:, :half]], axis=1)
        return own, joined_a, d, joined_b

    flips = (0, 2, 4, 6)
    out_mine = arranged(*[columns(outputs_late, me ^ f) for f in flips])
    out_sent = arranged(*[columns(outputs_late, me ^ f ^ 1) for f in flips])
    out_other = swapped(jnp.concatenate(out_sent, axis=1), 1)
    biases = arranged(b_own, b_x, b_y, b_d)
    both = jnp.concatenate([inputs, inputs_other], axis=0)

    def layer(n, w):
        affine = scaling * times_transposed(both, w) + biases[n]
        target = jnp.concatenate([out_mine[n], out_other[:, n * units : (n + 1) * units]], axis=0)
        return affine, affine - target

    affine_own, m = layer(0, w_own)
    g_own = transposed_times(m, both)
    o_own = jnp.sum(m, axis=0, keepdims=True)
    pulled = times(m, w_own)
    low_x, high_y, g_own, pulled, o_own = lax.optimization_barrier(
        (low_x, high_y, g_own, pulled, o_own)
    )

    low_d, high_d = swapped(low_x, 4), swapped(high_y, 2)
    w_a = jnp.concatenate([low_x, high_y], axis=0)
    affine_a, m = layer(1, w_a)
    g_a = transposed_times(m, both)
    o_a = jnp.sum(m, axis=0, keepdims=True)
    pulled = pulled + times(m, w_a)
    low_d, high_d, g_a, pulled, o_a, low_own, high_own = lax.optimization_barrier(
        (low_d, high_d, g_a, pulled, o_a, low_own, high_own)
    )

    high_x, low_y = swapped(high_own, 2), swapped(low_own, 4)
    w_d = jnp.concatenate([low_d, high_d], axis=0)
    affine_d, m = layer(2, w_d)
    g_d = transposed_times(m, both)
    o_d = jnp.sum(m, axis=0, keepdims=True)
    pulled = pulled + times(m, w_d)
    high_x, low_y, g_a, g_d, pulled, o_d, prev_drive = lax.optimization_barrier(
        (high_x, low_y, g_a, g_d, pulled, o_d, prev_drive)
    )

    x_low, y_high = swapped(g_a[:half], 2), swapped(g_a[half:], 4)
    from_x, from_y = swapped(g_d[:half], 2), swapped(g_d[half:], 4)
    w_b = jnp.concatenate([high_x, low_y], axis=0)
    affine_b, m = layer(3, w_b)
    pulled_other = swapped(pulled[rows:] + times(m[rows:], w_b), 1)
    pulled_mine = pulled[:rows] + times(m[:rows], w_b)
    pulled_all = scaling * (pulled_mine + pulled_other)
    pulled_step = inputs - step_input * (fit_weight * pulled_all + penalty * inputs)
    m, pulled_step = lax.optimization_barrier((m, pulled_step))
    next_step = passed_along(pulled_step, "depth", -1)
    g_b = transposed_times(m, both)
    o_b = jnp.sum(m, axis=0, keepdims=True)

    x_high = swapped(g_b[:half] + from_y, 2)
    y_low = swapped(g_b[half:] + from_x, 4)
    sum_low = g_own[:half] + x_low + y_low
    sum_high = g_own[half:] + x_high + y_high
    weight_step = step_weight * fit_weight * scaling
    weights_new = w_own - weight_step * jnp.concatenate([sum_low, sum_high], axis=0)
    o_x = jnp.concatenate([o_a[:, :half], o_b[:, :half]], axis=1)
    o_y = jnp.concatenate([o_b[:, half:], o_a[:, half:]], axis=1)
    offset_sum = o_own + swapped(o_x, 2) + swapped(o_y, 4) + swapped(o_d, 6)
    offsets_new = offsets - step_offset * fit_weight * offset_sum

    affines = (affine_own, affine_a, affine_d, affine_b)
    affine_other = swapped(jnp.concatenate([a[rows:] for a in affines], axis=1), 1)

    def by_owner(own, a, d, b):
        x = jnp.concatenate([a[:, :half], b[:, :half]], axis=1)
        y = jnp.concatenate([b[:, half:], a[:, half:]], axis=1)
        return own, x, y, d

    mine = by_owner(*[a[:rows] for a in affines])
    other = by_owner(*[affine_other[:, n * units : (n + 1) * units] for n in range(len(flips))])
    affine = jnp.zeros_like(outputs)
    for n, f in enumerate(flips):
        affine = lax.dynamic_update_slice(affine, mine[n], (0, (me ^ f) * units))
        affine = lax.dynamic_update_slice(affine, other[n], (0, (me ^ f ^ 1) * units))
    inputs_new, outputs_new, mults_new = finish(
        inputs, outputs, mults, drive, prev_drive, affine, pulled_step, next_step
    )
    return (
        inputs_new[None],
        weights_new[None],
        offsets_new,
        outputs_new[None],
        mults_new[None],
    )


MESH = pl.DeviceIdType.MESH
VMEM_BYTES = 67043328
OWNERS = ((0, 0), (2, 4), (4, 2), (6, 6))
X, Y, DIAGONAL, PARTNER = 2, 4, 6, 1
ROW_TILE = 128
COLUMN_TILE = 256
LINK_CHUNKS = 4
PULL_CHUNKS = 6


def fused_shapes(rows, width, units):
    f32, bf16 = jnp.float32, jnp.bfloat16
    return dict(
        pull=((2 * rows, width), f32),
        x_high=((2 * rows, width), bf16),
        x_low=((2 * rows, width), bf16),
        w=((4 * units, width), f32),
        w_high=((units, width), bf16),
        w_low=((units, width), bf16),
        target=((4, 2 * rows, units), f32),
        m_high=((2 * rows, units), bf16),
        m_low=((2 * rows, units), bf16),
        mt_high=((units, 2 * rows), bf16),
        mt_low=((units, 2 * rows), bf16),
        affine=((rows, width), f32),
        pull_in=((rows, width), f32),
        grad=((4 * units, width), f32),
        direct_in=((units, width), f32),
        relay_in=((units, width), f32),
        merged_in=((units, width), f32),
        drive=((rows, width), f32),
        prev_in=((rows, width), f32),
        next_in=((rows, width), f32),
        bias=((4, 8, units), f32),
        osum=((4, 8, units), f32),
        osend=((3, 8, units), f32),
        orecv=((3, 8, units), f32),
    )


def fused_bytes(rows, width, units):
    shapes = fused_shapes(rows, width, units).values()
    return sum(math.prod(shape) * jnp.dtype(dtype).itemsize for shape, dtype in shapes)


def fused_kernel(
    names, samples, x_ref, w_ref, b_ref, q_ref, u_ref, p_new, w_new, b_new, q_new, u_new, *scratch
):
    ref = dict(zip(names, scratch))
    send_sem, recv_sem, local_sem = scratch[len(names) :]
    pull, x_high, x_low, w = ref["pull"], ref["x_high"], ref["x_low"], ref["w"]
    w_high, w_low, target = ref["w_high"], ref["w_low"], ref["target"]
    m_high, m_low, mt_high, mt_low = ref["m_high"], ref["m_low"], ref["mt_high"], ref["mt_low"]
    affine, pull_in, grad = ref["affine"], ref["pull_in"], ref["grad"]
    direct_in, relay_in, merged_in = ref["direct_in"], ref["relay_in"], ref["merged_in"]
    drive, prev_in, next_in = ref["drive"], ref["prev_in"], ref["next_in"]
    bias, osum, osend, orecv = ref["bias"], ref["osum"], ref["osend"], ref["orecv"]

    rows, width = affine.shape
    units = w_high.shape[0]
    half = units // 2
    scaling = 1.0 / math.sqrt(width)
    step_weight = 8.0 / math.sqrt(samples)
    step_offset = 0.5 / math.sqrt(samples)
    pull_factor = step_input * fit_weight * scaling
    keep_factor = 1.0 - step_input * penalty

    me, z = lax.axis_index("dp"), lax.axis_index("depth")
    has_prev, has_next = z > 0, z < lax.axis_size("depth") - 1
    bits = (me % 2, (me // 2) % 2, me // 4)

    def index_of(flip):
        return sum(((1 - b) if flip >> i & 1 else b) * 2**i for i, b in enumerate(bits))

    def device(flip):
        return (z, index_of(flip))

    above, below = (z + 1, me), (z - 1, me)
    remote_count, local_count = [0], [0]

    def remote(src, dst, to):
        i = remote_count[0]
        remote_count[0] += 1
        return pltpu.make_async_remote_copy(
            src_ref=src,
            dst_ref=dst,
            send_sem=send_sem.at[i],
            recv_sem=recv_sem.at[i],
            device_id=to,
            device_id_type=MESH,
        )

    def local(src, dst):
        i = local_count[0]
        local_count[0] += 1
        return pltpu.make_async_copy(src, dst, local_sem.at[i])

    def columns(flip, h):
        return pl.ds(pl.multiple_of(index_of(flip) * units + h * half, half), half)

    def halves(h):
        return pl.ds(h * half, half)

    bias[0] = jnp.broadcast_to(b_ref[...], (8, units))

    barrier = pltpu.get_barrier_semaphore()
    for flip in (PARTNER, X, Y, DIAGONAL):
        pl.semaphore_signal(barrier, inc=1, device_id=device(flip), device_id_type=MESH)

    @pl.when(has_prev)
    def _():
        pl.semaphore_signal(barrier, inc=1, device_id=below, device_id_type=MESH)

    @pl.when(has_next)
    def _():
        pl.semaphore_signal(barrier, inc=1, device_id=above, device_id_type=MESH)

    x_in = local(x_ref.at[0], pull.at[:rows])
    x_in.start()
    w_in = local(w_ref.at[0], w.at[:units])
    w_in.start()

    depth = lax.axis_size("depth")
    pl.semaphore_wait(barrier, 4 + (z + depth - 1) // depth + 1 - (z + 1) // depth)

    gather = {}
    for piece, h, to in ((1, 0, X), (1, 1, Y), (2, 1, X), (2, 0, Y)):
        dst = w.at[pl.ds(piece * units + h * half, half)]
        gather[piece, h] = remote(w_ref.at[0, halves(h)], dst, device(to))
        gather[piece, h].start()
    x_swap = remote(x_ref.at[0], pull.at[rows:], device(PARTNER))
    x_swap.start()
    target_in, target_swap = {}, {}
    for n, owners in enumerate(OWNERS):
        for h, flip in enumerate(owners):
            src = q_ref.at[0, :, columns(flip, h)]
            target_in[n, h] = local(src, target.at[n, :rows, halves(h)])
            src = q_ref.at[0, :, columns(flip ^ PARTNER, h)]
            dst = target.at[n, rows:, halves(h)]
            target_swap[n, h] = remote(src, dst, device(PARTNER))
    for h in (0, 1):
        target_in[0, h].start()
        target_swap[0, h].start()
    bias_swap = [remote(bias.at[0], bias.at[flip // 2], device(flip)) for flip in (X, Y, DIAGONAL)]
    for copy in bias_swap:
        copy.start()
    staged = grad.at[pl.ds(units, rows)]
    q_in, u_in = local(q_ref.at[0], staged), local(u_ref.at[0], drive)
    q_in.start()
    u_in.start()
    for n in (1, 2, 3):
        for h in (0, 1):
            target_in[n, h].start()
            target_swap[n, h].start()

    def split(value):
        high = value.astype(jnp.bfloat16)
        return high, (value - high.astype(jnp.float32)).astype(jnp.bfloat16)

    def split_rows(src, start, high, low, to, count):
        @pl.loop(0, count // 16)
        def _(i):
            offset = pl.multiple_of(i * 16, 16)
            high_part, low_part = split(src[pl.ds(start + offset, 16), :])
            high[pl.ds(to + offset, 16), :] = high_part
            low[pl.ds(to + offset, 16), :] = low_part

    def dot(a, b, contract):
        return lax.dot_general(a, b, (contract, ((), ())), preferred_element_type=jnp.float32)

    def dot3(a, b, contract):
        return (
            dot(a[0], b[0], contract) + dot(a[1], b[0], contract) + dot(a[0], b[1], contract)
        )

    def product(n):
        split_rows(w, n * units, w_high, w_low, 0, units)
        owners = OWNERS[n]
        shift = [bias[owners[h] // 2, 0:1, h * half : (h + 1) * half] for h in (0, 1)]
        shift = jnp.concatenate(shift, axis=1)
        osum[n] = jnp.zeros((8, units), jnp.float32)

        def tile(offset, mine):
            at = pl.ds(offset, ROW_TILE)
            value = dot3((x_high[at, :], x_low[at, :]), (w_high[...], w_low[...]), ((1,), (1,)))
            value = scaling * value + shift
            m = value - target[n, at, :]
            if mine:
                for h, flip in enumerate(owners):
                    affine[at, columns(flip, h)] = value[:, h * half : (h + 1) * half]
            else:
                target[n, at, :] = value
            osum[n] += jnp.sum(m.reshape(ROW_TILE // 8, 8, units), axis=0)
            m_high[at, :], m_low[at, :] = split(m)
            mt_high[:, at], mt_low[:, at] = split(m.T)

        for side in (1, 0):

            @pl.loop(0, rows // ROW_TILE)
            def _(i):
                tile(pl.multiple_of(side * rows + i * ROW_TILE, ROW_TILE), side == 0)

    def pull_tile(at, cols):
        a = (m_high[at, :], m_low[at, :])
        return dot3(a, (w_high[:, cols], w_low[:, cols]), ((1,), (0,)))

    def column_loop(body):
        @pl.loop(0, width // COLUMN_TILE)
        def _(c):
            body(pl.ds(pl.multiple_of(c * COLUMN_TILE, COLUMN_TILE), COLUMN_TILE))

    def pull_add(n):
        for side in (1, 0):
            at = pl.ds(side * rows, rows)

            def body(cols):
                value = pull_tile(at, cols)
                if n > 0:
                    value += pull[at, cols]
                elif side == 0:
                    value -= (keep_factor / pull_factor) * pull[at, cols]
                pull[at, cols] = value

            column_loop(body)

    def gradient(n):
        def body(cols):
            b = (x_high[:, cols], x_low[:, cols])
            value = dot3((mt_high[...], mt_low[...]), b, ((1,), (0,)))
            grad[pl.ds(n * units, units), cols] = value

        column_loop(body)

    affine_swap = {}

    def send_affine(n):
        for h, flip in enumerate(OWNERS[n]):
            src = target.at[n, rows:, halves(h)]
            affine_swap[n, h] = remote(src, affine.at[:, columns(flip, h)], device(PARTNER))
            affine_swap[n, h].start()

    def wait_targets(n):
        for h in (0, 1):
            target_in[n, h].wait()
            target_swap[n, h].wait_recv()

    x_in.wait()
    split_rows(pull, 0, x_high, x_low, 0, rows)
    x_swap.wait_recv()
    split_rows(pull, rows, x_high, x_low, rows, rows)
    w_in.wait()
    wait_targets(0)
    product(0)
    q_in.wait()
    u_in.wait()

    @pl.loop(0, rows // 16)
    def _(i):
        offset = pl.multiple_of(i * 16, 16)
        at = pl.ds(offset, 16)
        drive[at, :] = drive[at, :] - penalty * grad[pl.ds(units + offset, 16), :]

    pull_add(0)
    drive_up = remote(drive, prev_in, above)

    @pl.when(has_next)
    def _():
        drive_up.start()

    send_affine(0)
    gradient(0)

    for copy in bias_swap:
        copy.wait_recv()
    gather[1, 0].wait_recv()
    gather[1, 1].wait_recv()
    for h, to in ((1, X), (0, Y)):
        src = w.at[pl.ds(units + h * half, half)]
        dst = w.at[pl.ds(3 * units + h * half, half)]
        gather[3, h] = remote(src, dst, device(to))
        gather[3, h].start()
    wait_targets(1)
    product(1)
    gradient(1)
    pull_add(1)
    send_affine(1)
    direct = []
    for h, to in ((0, X), (1, Y)):
        src = grad.at[pl.ds(units + h * half, half)]
        direct.append(remote(src, direct_in.at[halves(h)], device(to)))
        direct[h].start()

    gather[2, 0].wait_recv()
    gather[2, 1].wait_recv()
    wait_targets(2)
    product(2)
    gradient(2)
    pull_add(2)
    send_affine(2)

    gather[3, 0].wait_recv()
    gather[3, 1].wait_recv()
    wait_targets(3)
    product(3)
    pull_swap, step_down = [], []
    blocks = rows // ROW_TILE
    for i in range(blocks):
        at = pl.ds(rows + i * ROW_TILE, ROW_TILE)

        def body(cols):
            pull[at, cols] = pull[at, cols] + pull_tile(at, cols)

        column_loop(body)
        pull_swap.append(remote(pull.at[at], pull_in.at[pl.ds(i * ROW_TILE, ROW_TILE)], device(PARTNER)))
        pull_swap[i].start()
    send_affine(3)
    pull_rows = rows // PULL_CHUNKS
    for i in range(PULL_CHUNKS):
        at = pl.ds(i * pull_rows, pull_rows)
        step_down.append(remote(pull.at[at], next_in.at[at], below))
    per_block = PULL_CHUNKS // blocks
    for i in range(blocks):
        at = pl.ds(i * ROW_TILE, ROW_TILE)
        pull_swap[i].wait_recv()

        def body(cols):
            value = pull[at, cols] + pull_tile(at, cols) + pull_in[at, cols]
            pull[at, cols] = -pull_factor * value

        column_loop(body)

        @pl.when(has_prev)
        def _():
            for k in range(per_block):
                step_down[i * per_block + k].start()

    gradient(3)
    link_rows = half // LINK_CHUNKS
    relay, merged = {}, {}

    def link_part(h, c):
        return pl.ds(h * half + c * link_rows, link_rows)

    for c in range(LINK_CHUNKS):
        for h, to in ((0, X), (1, Y)):
            at = link_part(h, c)
            src = grad.at[pl.ds(3 * units + h * half + c * link_rows, link_rows)]
            relay[h, c] = remote(src, relay_in.at[at], device(to))
            relay[h, c].start()
    for c in range(LINK_CHUNKS):
        for h, to in ((1, X), (0, Y)):
            src = grad.at[pl.ds(2 * units + h * half + c * link_rows, link_rows)]
            merged[h, c] = remote(src, merged_in.at[link_part(h, c)], device(to))

    for k, (low, high) in enumerate(((1, 2), (2, 1), (3, 3))):
        osend[k, :, :half] = osum[low, :, :half]
        osend[k, :, half:] = osum[high, :, half:]
    sums = [remote(osend.at[k], orecv.at[k], device(flip)) for k, flip in enumerate((X, Y, DIAGONAL))]

    outs = []
    p_out = local(prev_in, p_new.at[0])

    @pl.when(has_prev)
    def _():
        drive_up.wait_recv()

        @pl.loop(0, rows // 16)
        def _(i):
            at = pl.ds(pl.multiple_of(i * 16, 16), 16)
            prev_in[at, :] = pull[at, :] - step_input * prev_in[at, :]

    p_copy = local(x_ref.at[0], prev_in)

    @pl.when(jnp.logical_not(has_prev))
    def _():
        p_copy.start()
        p_copy.wait()

    for copy in sums:
        copy.start()
    for copy in pull_swap:
        copy.wait_send()
    u_late = local(u_ref.at[0], pull.at[rows:])
    u_late.start()
    p_out.start()
    outs.append(p_out)

    @pl.when(has_next)
    def _():
        drive_up.wait_send()

    for n in range(4):
        for h in (0, 1):
            affine_swap[n, h].wait_recv()
    u_late.wait()
    q_out, u_out = [], []
    for i in range(PULL_CHUNKS):
        at = pl.ds(i * pull_rows, pull_rows)
        q_out.append(local(affine.at[at], q_new.at[0, at]))
        u_out.append(local(drive.at[at], u_new.at[0, at]))

    def finish_rows(i):
        @pl.when(has_next)
        def _():
            step_down[i].wait_recv()

            @pl.loop(0, pull_rows // 8)
            def _(j):
                offset = pl.multiple_of(i * pull_rows + j * 8, 8)
                at = pl.ds(offset, 8)
                mults = pull[pl.ds(rows + offset, 8), :]
                following = next_in[at, :] - step_input * drive[at, :]
                total = fit_weight * affine[at, :] + penalty * following + mults
                fresh = jnp.maximum(0.0, total / (fit_weight + penalty))
                affine[at, :] = fresh
                drive[at, :] = mults + penalty * (following - fresh)

        @pl.when(jnp.logical_not(has_next))
        def _():
            @pl.loop(0, pull_rows // 8)
            def _(j):
                offset = pl.multiple_of(i * pull_rows + j * 8, 8)
                at = pl.ds(offset, 8)
                affine[at, :] = jnp.maximum(0.0, affine[at, :])
                drive[at, :] = pull[pl.ds(rows + offset, 8), :]

        if i > 0:
            q_out[i - 1].start()
            u_out[i - 1].start()

    def merge(c):
        for h in (1, 0):
            relay[h, c].wait_recv()
            start = 2 * units + h * half + c * link_rows
            at = pl.ds(start, link_rows)
            grad[at, :] = grad[at, :] + relay_in[link_part(h, c), :]
        for h in (1, 0):
            merged[h, c].start()

    w_out = {}

    def finish_weights(c):
        for h in (0, 1):
            merged[h, c].wait_recv()
            at = link_part(h, c)
            total = grad[at, :] + direct_in[at, :] + merged_in[at, :]
            grad[at, :] = w[at, :] - (step_weight * fit_weight * scaling) * total
        for h in (0, 1):
            at = link_part(h, c)
            w_out[h, c] = local(grad.at[at], w_new.at[0, at])
            w_out[h, c].start()

    finish_rows(0)
    finish_rows(1)
    merge(0)
    merge(1)
    merge(2)
    finish_rows(2)
    merge(3)
    for copy in sums:
        copy.wait_recv()
    total = osum[0] + orecv[0] + orecv[1] + orecv[2]
    total = jnp.sum(total, axis=0, keepdims=True)
    b_new[...] = b_ref[...] - (step_offset * fit_weight) * total
    finish_rows(3)
    for copy in direct:
        copy.wait_recv()
    finish_weights(0)
    finish_weights(1)
    finish_weights(2)
    finish_rows(4)
    finish_weights(3)
    finish_rows(5)
    q_out[-1].start()
    u_out[-1].start()

    for copies in (gather, target_swap, affine_swap, relay, merged):
        for copy in copies.values():
            copy.wait_send()
    for copy in (x_swap, *bias_swap, *direct, *sums):
        copy.wait_send()

    @pl.when(has_prev)
    def _():
        for copy in step_down:
            copy.wait_send()

    for copy in (*outs, *q_out, *u_out, *w_out.values()):
        copy.wait()


def body_fused(layer_inputs, weights, offsets, layer_outputs, multipliers):
    _, rows, width = layer_inputs.shape
    units = weights.shape[1]
    shapes = fused_shapes(rows, width, units)
    samples = rows * lax.axis_size("dp")
    anywhere = pl.BlockSpec(memory_space=pl.ANY)
    vmem = pl.BlockSpec(memory_space=pltpu.VMEM)
    args = (layer_inputs, weights, offsets, layer_outputs, multipliers)
    return pl.pallas_call(
        functools.partial(fused_kernel, tuple(shapes), samples),
        out_shape=tuple(jax.ShapeDtypeStruct(a.shape, a.dtype) for a in args),
        in_specs=[anywhere, anywhere, vmem, anywhere, anywhere],
        out_specs=[anywhere, anywhere, vmem, anywhere, anywhere],
        scratch_shapes=[pltpu.VMEM(shape, dtype) for shape, dtype in shapes.values()]
        + [
            pltpu.SemaphoreType.DMA((64,)),
            pltpu.SemaphoreType.DMA((64,)),
            pltpu.SemaphoreType.DMA((48,)),
        ],
        compiler_params=pltpu.CompilerParams(
            collective_id=0, has_side_effects=True, vmem_limit_bytes=VMEM_BYTES
        ),
        name="iteration",
    )(*args)


def choose(mesh, layer_inputs, weights, *rest):
    if mesh.shape["dp"] != 8:
        return body_general(layer_inputs, weights, *rest)
    rows, width, units = layer_inputs.shape[1], layer_inputs.shape[2], weights.shape[1]
    tiles = rows % (16 * PULL_CHUNKS), width % COLUMN_TILE, units % 256, rows % ROW_TILE
    if any(tiles) or fused_bytes(rows, width, units) > VMEM_BYTES - 2**21:
        return body_square(layer_inputs, weights, *rest)
    return body_fused(layer_inputs, weights, *rest)


def solution(mesh):
    specs = (
        P("depth", "dp", None),
        P("depth", "dp", None),
        P("depth", "dp"),
        P("depth", "dp", None),
        P("depth", "dp", None),
    )
    body = functools.partial(choose, mesh)
    return jax.shard_map(body, mesh=mesh, in_specs=specs, out_specs=specs, check_vma=False)
```

```python
import functools
import math

import jax
import jax.numpy as jnp
from jax import lax
from jax.experimental import pallas as pl
from jax.experimental.pallas import tpu as pltpu
from jax.sharding import PartitionSpec as P

fit_weight = 1.0
penalty = 1.0
step_input = 0.5
PRECISION = lax.Precision.HIGH


def passed_along(block, axis, distance):
    devices = range(lax.axis_size(axis))
    route = [(i - distance, i) for i in devices if i - distance in devices]
    return lax.ppermute(block, axis, route)


def swapped(block, bit):
    route = [(i, i ^ bit) for i in range(lax.axis_size("dp"))]
    return lax.ppermute(block, "dp", route)


def dot(a, b, dims):
    return lax.dot_general(a, b, (dims, ((), ())), precision=PRECISION)


def times_transposed(a, b):
    return dot(a, b, ((1,), (1,)))


def times(a, b):
    return dot(a, b, ((1,), (0,)))


def transposed_times(a, b):
    return dot(a, b, ((0,), (0,)))


def finish(inputs, outputs, mults, drive, prev_drive, affine, pulled_step, next_step):
    layer_index = lax.axis_index("depth")
    is_first = layer_index == 0
    is_last = layer_index == lax.axis_size("depth") - 1
    inputs_new = jnp.where(is_first, inputs, pulled_step - step_input * prev_drive)
    next_inputs = next_step - step_input * drive
    coupled = jnp.maximum(
        0.0, (fit_weight * affine + penalty * next_inputs + mults) / (fit_weight + penalty)
    )
    outputs_new = jnp.where(is_last, jnp.maximum(0.0, affine), coupled)
    mults_new = jnp.where(is_last, mults, mults + penalty * (next_inputs - outputs_new))
    return inputs_new, outputs_new, mults_new


def body_general(layer_inputs, weights, offsets, layer_outputs, multipliers):
    inputs, outputs, mults = layer_inputs[0], layer_outputs[0], multipliers[0]
    scaling = 1.0 / math.sqrt(inputs.shape[1])
    samples = inputs.shape[0] * lax.axis_size("dp")
    step_weight = 8.0 / math.sqrt(samples)
    step_offset = 0.5 / math.sqrt(samples)
    drive = mults - penalty * outputs
    prev_drive = passed_along(drive, "depth", 1)
    weight = lax.all_gather(weights[0], "dp", axis=0, tiled=True)
    offset = lax.all_gather(offsets, "dp", axis=1, tiled=True)
    affine = scaling * times_transposed(inputs, weight) + offset
    misfit = affine - outputs
    weight_grad = fit_weight * scaling * transposed_times(misfit, inputs)
    weight_sum = lax.psum_scatter(weight_grad, "dp", scatter_dimension=0, tiled=True)
    offset_sum = lax.psum_scatter(
        fit_weight * jnp.sum(misfit, axis=0), "dp", scatter_dimension=0, tiled=True
    )
    pulled = scaling * times(misfit, weight)
    pulled_step = inputs - step_input * (fit_weight * pulled + penalty * inputs)
    next_step = passed_along(pulled_step, "depth", -1)
    inputs_new, outputs_new, mults_new = finish(
        inputs, outputs, mults, drive, prev_drive, affine, pulled_step, next_step
    )
    weights_new = weights - step_weight * weight_sum[None]
    offsets_new = offsets - step_offset * offset_sum[None]
    return inputs_new[None], weights_new, offsets_new, outputs_new[None], mults_new[None]


def body_square(layer_inputs, weights, offsets, layer_outputs, multipliers):
    inputs, outputs, mults = layer_inputs[0], layer_outputs[0], multipliers[0]
    rows, width = inputs.shape
    units = weights.shape[1]
    half = units // 2
    scaling = 1.0 / math.sqrt(width)
    samples = rows * lax.axis_size("dp")
    step_weight = 8.0 / math.sqrt(samples)
    step_offset = 0.5 / math.sqrt(samples)
    me = lax.axis_index("dp")

    w_own = weights[0]
    low_own, high_own = w_own[:half], w_own[half:]
    low_own, high_own, inputs = lax.optimization_barrier((low_own, high_own, inputs))
    low_x, high_y = swapped(low_own, 2), swapped(high_own, 4)
    inputs_other = swapped(inputs, 1)
    inputs_other, outputs_late = lax.optimization_barrier((inputs_other, outputs))
    drive = mults - penalty * outputs
    prev_drive = passed_along(drive, "depth", 1)
    b_own = offsets
    b_x, b_y, b_d = swapped(b_own, 2), swapped(b_own, 4), swapped(b_own, 6)

    def columns(array, index):
        return lax.dynamic_slice(array, (0, index * units), (rows, units))

    def arranged(own, x, y, d):
        joined_a = jnp.concatenate([x[:, :half], y[:, half:]], axis=1)
        joined_b = jnp.concatenate([x[:, half:], y[:, :half]], axis=1)
        return own, joined_a, d, joined_b

    flips = (0, 2, 4, 6)
    out_mine = arranged(*[columns(outputs_late, me ^ f) for f in flips])
    out_sent = arranged(*[columns(outputs_late, me ^ f ^ 1) for f in flips])
    out_other = swapped(jnp.concatenate(out_sent, axis=1), 1)
    biases = arranged(b_own, b_x, b_y, b_d)
    both = jnp.concatenate([inputs, inputs_other], axis=0)

    def layer(n, w):
        affine = scaling * times_transposed(both, w) + biases[n]
        target = jnp.concatenate([out_mine[n], out_other[:, n * units : (n + 1) * units]], axis=0)
        return affine, affine - target

    affine_own, m = layer(0, w_own)
    g_own = transposed_times(m, both)
    o_own = jnp.sum(m, axis=0, keepdims=True)
    pulled = times(m, w_own)
    low_x, high_y, g_own, pulled, o_own = lax.optimization_barrier(
        (low_x, high_y, g_own, pulled, o_own)
    )

    low_d, high_d = swapped(low_x, 4), swapped(high_y, 2)
    w_a = jnp.concatenate([low_x, high_y], axis=0)
    affine_a, m = layer(1, w_a)
    g_a = transposed_times(m, both)
    o_a = jnp.sum(m, axis=0, keepdims=True)
    pulled = pulled + times(m, w_a)
    low_d, high_d, g_a, pulled, o_a, low_own, high_own = lax.optimization_barrier(
        (low_d, high_d, g_a, pulled, o_a, low_own, high_own)
    )

    high_x, low_y = swapped(high_own, 2), swapped(low_own, 4)
    w_d = jnp.concatenate([low_d, high_d], axis=0)
    affine_d, m = layer(2, w_d)
    g_d = transposed_times(m, both)
    o_d = jnp.sum(m, axis=0, keepdims=True)
    pulled = pulled + times(m, w_d)
    high_x, low_y, g_a, g_d, pulled, o_d, prev_drive = lax.optimization_barrier(
        (high_x, low_y, g_a, g_d, pulled, o_d, prev_drive)
    )

    x_low, y_high = swapped(g_a[:half], 2), swapped(g_a[half:], 4)
    from_x, from_y = swapped(g_d[:half], 2), swapped(g_d[half:], 4)
    w_b = jnp.concatenate([high_x, low_y], axis=0)
    affine_b, m = layer(3, w_b)
    pulled_other = swapped(pulled[rows:] + times(m[rows:], w_b), 1)
    pulled_mine = pulled[:rows] + times(m[:rows], w_b)
    pulled_all = scaling * (pulled_mine + pulled_other)
    pulled_step = inputs - step_input * (fit_weight * pulled_all + penalty * inputs)
    m, pulled_step = lax.optimization_barrier((m, pulled_step))
    next_step = passed_along(pulled_step, "depth", -1)
    g_b = transposed_times(m, both)
    o_b = jnp.sum(m, axis=0, keepdims=True)

    x_high = swapped(g_b[:half] + from_y, 2)
    y_low = swapped(g_b[half:] + from_x, 4)
    sum_low = g_own[:half] + x_low + y_low
    sum_high = g_own[half:] + x_high + y_high
    weight_step = step_weight * fit_weight * scaling
    weights_new = w_own - weight_step * jnp.concatenate([sum_low, sum_high], axis=0)
    o_x = jnp.concatenate([o_a[:, :half], o_b[:, :half]], axis=1)
    o_y = jnp.concatenate([o_b[:, half:], o_a[:, half:]], axis=1)
    offset_sum = o_own + swapped(o_x, 2) + swapped(o_y, 4) + swapped(o_d, 6)
    offsets_new = offsets - step_offset * fit_weight * offset_sum

    affines = (affine_own, affine_a, affine_d, affine_b)
    affine_other = swapped(jnp.concatenate([a[rows:] for a in affines], axis=1), 1)

    def by_owner(own, a, d, b):
        x = jnp.concatenate([a[:, :half], b[:, :half]], axis=1)
        y = jnp.concatenate([b[:, half:], a[:, half:]], axis=1)
        return own, x, y, d

    mine = by_owner(*[a[:rows] for a in affines])
    other = by_owner(*[affine_other[:, n * units : (n + 1) * units] for n in range(len(flips))])
    affine = jnp.zeros_like(outputs)
    for n, f in enumerate(flips):
        affine = lax.dynamic_update_slice(affine, mine[n], (0, (me ^ f) * units))
        affine = lax.dynamic_update_slice(affine, other[n], (0, (me ^ f ^ 1) * units))
    inputs_new, outputs_new, mults_new = finish(
        inputs, outputs, mults, drive, prev_drive, affine, pulled_step, next_step
    )
    return (
        inputs_new[None],
        weights_new[None],
        offsets_new,
        outputs_new[None],
        mults_new[None],
    )


MESH = pl.DeviceIdType.MESH
VMEM_BYTES = 67043328
SPARE_BYTES = 2**22
OWNERS = ((0, 0), (2, 4), (4, 2), (6, 6))
X, Y, DIAGONAL, PARTNER = 2, 4, 6, 1
ROW_TILE = 128
COLUMN_TILE = 256
LINK_CHUNKS = 4
EARLY_PART = 0.75


def fused_shapes(rows, width, units):
    f32, bf16 = jnp.float32, jnp.bfloat16
    return dict(
        pull=((2 * rows, width), f32),
        x_high=((2 * rows, width), bf16),
        x_low=((2 * rows, width), bf16),
        w=((4 * units, width), f32),
        w_high=((units, width), bf16),
        w_low=((units, width), bf16),
        target=((4, 2 * rows, units), f32),
        m_high=((2 * rows, units), bf16),
        m_low=((2 * rows, units), bf16),
        mt_high=((units, 2 * rows), bf16),
        mt_low=((units, 2 * rows), bf16),
        product=((2 * rows, units), f32),
        pull_in=((rows, width), f32),
        grad=((3 * units, width), f32),
        direct_in=((units, width), f32),
        relay_in=((units, width), f32),
        merged_in=((units, width), f32),
        next_in=((rows, width), f32),
        bias=((4, 8, units), f32),
        osum=((4, 8, units), f32),
        osend=((3, 8, units), f32),
        orecv=((3, 8, units), f32),
    )


def fused_bytes(rows, width, units):
    shapes = fused_shapes(rows, width, units).values()
    return sum(math.prod(shape) * jnp.dtype(dtype).itemsize for shape, dtype in shapes)


def fused_kernel(
    names, samples, x_ref, w_ref, b_ref, q_ref, u_ref, p_new, w_new, b_new, q_new, u_new, *scratch
):
    ref = dict(zip(names, scratch))
    send_sem, recv_sem, local_sem = scratch[len(names) :]
    pull, x_high, x_low, w = ref["pull"], ref["x_high"], ref["x_low"], ref["w"]
    w_high, w_low, target = ref["w_high"], ref["w_low"], ref["target"]
    m_high, m_low, mt_high, mt_low = ref["m_high"], ref["m_low"], ref["mt_high"], ref["mt_low"]
    pull_in, grad, partial = ref["pull_in"], ref["grad"], ref["product"]
    direct_in, relay_in, merged_in = ref["direct_in"], ref["relay_in"], ref["merged_in"]
    next_in = ref["next_in"]
    prev_in, own_grad, affine, drive = p_new.at[0], w_new.at[0], q_new.at[0], u_new.at[0]
    bias, osum, osend, orecv = ref["bias"], ref["osum"], ref["osend"], ref["orecv"]

    rows, width = affine.shape
    units = w_high.shape[0]
    half = units // 2
    scaling = 1.0 / math.sqrt(width)
    step_weight = 8.0 / math.sqrt(samples)
    step_offset = 0.5 / math.sqrt(samples)
    pull_factor = step_input * fit_weight * scaling
    keep_factor = 1.0 - step_input * penalty

    me, z = lax.axis_index("dp"), lax.axis_index("depth")
    has_prev, has_next = z > 0, z < lax.axis_size("depth") - 1
    bits = (me % 2, (me // 2) % 2, me // 4)

    def index_of(flip):
        return sum(((1 - b) if flip >> i & 1 else b) * 2**i for i, b in enumerate(bits))

    def device(flip):
        return (z, index_of(flip))

    above, below = (z + 1, me), (z - 1, me)
    remote_count, local_count = [0], [0]

    def remote(src, dst, to):
        i = remote_count[0]
        remote_count[0] += 1
        return pltpu.make_async_remote_copy(
            src_ref=src,
            dst_ref=dst,
            send_sem=send_sem.at[i],
            recv_sem=recv_sem.at[i],
            device_id=to,
            device_id_type=MESH,
        )

    def local(src, dst):
        i = local_count[0]
        local_count[0] += 1
        return pltpu.make_async_copy(src, dst, local_sem.at[i])

    def columns(flip, h):
        return pl.ds(pl.multiple_of(index_of(flip) * units + h * half, half), half)

    def halves(h):
        return pl.ds(h * half, half)

    bias[0] = jnp.broadcast_to(b_ref[...], (8, units))

    barrier = pltpu.get_barrier_semaphore()
    for flip in (PARTNER, X, Y, DIAGONAL):
        pl.semaphore_signal(barrier, inc=1, device_id=device(flip), device_id_type=MESH)

    @pl.when(has_prev)
    def _():
        pl.semaphore_signal(barrier, inc=1, device_id=below, device_id_type=MESH)

    @pl.when(has_next)
    def _():
        pl.semaphore_signal(barrier, inc=1, device_id=above, device_id_type=MESH)

    x_in = local(x_ref.at[0], pull.at[:rows])
    x_in.start()
    w_in = local(w_ref.at[0], w.at[:units])
    w_in.start()

    depth = lax.axis_size("depth")
    pl.semaphore_wait(barrier, 4 + (z + depth - 1) // depth + 1 - (z + 1) // depth)

    bias_swap = [remote(bias.at[0], bias.at[flip // 2], device(flip)) for flip in (X, Y, DIAGONAL)]
    for copy in bias_swap:
        copy.start()
    gather = {}
    for piece, h, to in ((1, 0, X), (1, 1, Y), (2, 1, X), (2, 0, Y)):
        dst = w.at[pl.ds(piece * units + h * half, half)]
        gather[piece, h] = remote(w_ref.at[0, halves(h)], dst, device(to))
        gather[piece, h].start()
    x_swap = remote(x_ref.at[0], pull.at[rows:], device(PARTNER))
    x_swap.start()
    target_in, target_swap = {}, {}
    for n, owners in enumerate(OWNERS):
        for h, flip in enumerate(owners):
            src = q_ref.at[0, :, columns(flip, h)]
            target_in[n, h] = local(src, target.at[n, :rows, halves(h)])
            src = q_ref.at[0, :, columns(flip ^ PARTNER, h)]
            dst = target.at[n, rows:, halves(h)]
            target_swap[n, h] = remote(src, dst, device(PARTNER))
    for h in (0, 1):
        target_in[0, h].start()
        target_swap[0, h].start()
    staged = grad.at[:rows]
    q_in, u_in = local(q_ref.at[0], staged), local(u_ref.at[0], drive)
    q_in.start()
    u_in.start()
    for n in (1, 2, 3):
        for h in (0, 1):
            target_in[n, h].start()
            target_swap[n, h].start()

    def split(value):
        high = value.astype(jnp.bfloat16)
        return high, (value - high.astype(jnp.float32)).astype(jnp.bfloat16)

    def split_rows(src, start, high, low, to, count, cols=slice(None)):
        @pl.loop(0, count // 16)
        def _(i):
            offset = pl.multiple_of(i * 16, 16)
            high_part, low_part = split(src[pl.ds(start + offset, 16), cols])
            high[pl.ds(to + offset, 16), cols] = high_part
            low[pl.ds(to + offset, 16), cols] = low_part

    def dot(a, b, contract):
        return lax.dot_general(a, b, (contract, ((), ())), preferred_element_type=jnp.float32)

    def dot3(a, b, contract):
        return (
            dot(a[0], b[0], contract) + dot(a[1], b[0], contract) + dot(a[0], b[1], contract)
        )

    def product(n, parts=(slice(None),)):
        owners = OWNERS[n]
        shift = [bias[owners[h] // 2, 0:1, h * half : (h + 1) * half] for h in (0, 1)]
        shift = jnp.concatenate(shift, axis=1)
        osum[n] = jnp.zeros((8, units), jnp.float32)
        for k, cols in enumerate(parts):
            if n == 3:
                gather[3, 0, k].wait_recv()
                gather[3, 1, k].wait_recv()
            split_rows(w, n * units, w_high, w_low, 0, units, cols)
            for side in (1, 0):
                at = pl.ds(side * rows, rows)
                value = dot3(
                    (x_high[at, cols], x_low[at, cols]),
                    (w_high[:, cols], w_low[:, cols]),
                    ((1,), (1,)),
                )
                if k > 0:
                    value += partial[at, :]
                if k < len(parts) - 1:
                    partial[at, :] = value
                    continue
                value = scaling * value + shift
                m = value - target[n, at, :]
                if side == 0:
                    for h, flip in enumerate(owners):
                        affine[:, columns(flip, h)] = value[:, h * half : (h + 1) * half]
                else:
                    target[n, at, :] = value
                osum[n] += jnp.sum(m.reshape(rows // 8, 8, units), axis=0)
                m_high[at, :], m_low[at, :] = split(m)

    def pull_tile(at, cols):
        a = (m_high[at, :], m_low[at, :])
        return dot3(a, (w_high[:, cols], w_low[:, cols]), ((1,), (0,)))

    def column_loop(body):
        @pl.loop(0, width // COLUMN_TILE)
        def _(c):
            body(pl.ds(pl.multiple_of(c * COLUMN_TILE, COLUMN_TILE), COLUMN_TILE))

    def pull_add(n):
        for side in (1, 0):
            at = pl.ds(side * rows, rows)

            def body(cols):
                value = pull_tile(at, cols)
                if n > 0:
                    value += pull[at, cols]
                elif side == 0:
                    value -= (keep_factor / pull_factor) * pull[at, cols]
                pull[at, cols] = value

            column_loop(body)

    def gradient(n):
        for part, turned in ((m_high, mt_high), (m_low, mt_low)):

            @pl.loop(0, 2 * rows // ROW_TILE)
            def _(i):
                at = pl.ds(pl.multiple_of(i * ROW_TILE, ROW_TILE), ROW_TILE)
                turned[:, at] = part[at, :].astype(jnp.float32).T.astype(jnp.bfloat16)

        def body(cols):
            b = (x_high[:, cols], x_low[:, cols])
            value = dot3((mt_high[...], mt_low[...]), b, ((1,), (0,)))
            if n == 0:
                own_grad[:, cols] = value
            else:
                grad[pl.ds((n - 1) * units, units), cols] = value

        column_loop(body)

    affine_swap = {}

    def send_affine(n):
        for h, flip in enumerate(OWNERS[n]):
            src = target.at[n, rows:, halves(h)]
            affine_swap[n, h] = remote(src, affine.at[:, columns(flip, h)], device(PARTNER))
            affine_swap[n, h].start()

    def wait_targets(n):
        for h in (0, 1):
            target_in[n, h].wait()
            target_swap[n, h].wait_recv()

    x_in.wait()
    split_rows(pull, 0, x_high, x_low, 0, rows)
    x_swap.wait_recv()
    split_rows(pull, rows, x_high, x_low, rows, rows)
    w_in.wait()
    wait_targets(0)
    product(0)
    q_in.wait()
    u_in.wait()

    @pl.loop(0, rows // 16)
    def _(i):
        offset = pl.multiple_of(i * 16, 16)
        at = pl.ds(offset, 16)
        drive[at, :] = drive[at, :] - penalty * grad[pl.ds(offset, 16), :]

    pull_add(0)
    drive_up = remote(drive, prev_in, above)

    @pl.when(has_next)
    def _():
        drive_up.start()

    send_affine(0)
    gradient(0)

    for copy in bias_swap:
        copy.wait_recv()
    gather[1, 0].wait_recv()
    gather[1, 1].wait_recv()
    cut = int(width * EARLY_PART) // 128 * 128
    parts = (slice(0, cut), slice(cut, width))
    for k, cols in enumerate(parts):
        for h, to in ((1, X), (0, Y)):
            src = w.at[pl.ds(units + h * half, half), cols]
            dst = w.at[pl.ds(3 * units + h * half, half), cols]
            gather[3, h, k] = remote(src, dst, device(to))
            gather[3, h, k].start()
    wait_targets(1)
    product(1)
    gradient(1)
    pull_add(1)
    send_affine(1)
    direct = []
    for h, to in ((0, X), (1, Y)):
        src = grad.at[halves(h)]
        direct.append(remote(src, direct_in.at[halves(h)], device(to)))
        direct[h].start()

    gather[2, 0].wait_recv()
    gather[2, 1].wait_recv()
    wait_targets(2)
    product(2)
    gradient(2)
    pull_add(2)
    send_affine(2)

    wait_targets(3)
    product(3, parts)
    pull_swap, step_down = [], []
    blocks = width // COLUMN_TILE

    def block(i):
        return slice(i * COLUMN_TILE, (i + 1) * COLUMN_TILE)

    for i in range(blocks):
        src = pull.at[rows:, block(i)]
        pull_swap.append(remote(src, pull_in.at[:, block(i)], device(PARTNER)))
        src = pull.at[:rows, block(i)]
        step_down.append(remote(src, next_in.at[:, block(i)], below))

    def pull_last(i, side):
        at = pl.ds(side * rows, rows)
        pull[at, block(i)] = pull[at, block(i)] + pull_tile(at, block(i))

    def pull_done(i):
        pull_swap[i].wait_recv()
        pull[:rows, block(i)] = -pull_factor * (pull[:rows, block(i)] + pull_in[:, block(i)])

        @pl.when(has_prev)
        def _():
            step_down[i].start()

    lag = 2
    for i in range(blocks + lag):
        if i < blocks:
            pull_last(i, 1)
        if i >= lag:
            pull_done(i - lag)
        if i < blocks:
            pull_swap[i].start()
            pull_last(i, 0)
    send_affine(3)
    gradient(3)
    link_rows = half // LINK_CHUNKS
    relay, merged = {}, {}

    def link_part(h, c):
        return pl.ds(h * half + c * link_rows, link_rows)

    for c in range(LINK_CHUNKS):
        for h, to in ((0, X), (1, Y)):
            at = link_part(h, c)
            src = grad.at[pl.ds(2 * units + h * half + c * link_rows, link_rows)]
            relay[h, c] = remote(src, relay_in.at[at], device(to))
            relay[h, c].start()
    for c in range(LINK_CHUNKS):
        for h, to in ((1, X), (0, Y)):
            src = grad.at[pl.ds(units + h * half + c * link_rows, link_rows)]
            merged[h, c] = remote(src, merged_in.at[link_part(h, c)], device(to))

    for k, (low, high) in enumerate(((1, 2), (2, 1), (3, 3))):
        osend[k, :, :half] = osum[low, :, :half]
        osend[k, :, half:] = osum[high, :, half:]
    sums = [remote(osend.at[k], orecv.at[k], device(flip)) for k, flip in enumerate((X, Y, DIAGONAL))]


    @pl.when(has_prev)
    def _():
        drive_up.wait_recv()

        @pl.loop(0, rows // 16)
        def _(i):
            at = pl.ds(pl.multiple_of(i * 16, 16), 16)
            prev_in[at, :] = pull[at, :] - step_input * prev_in[at, :]

    p_copy = local(x_ref.at[0], prev_in)

    @pl.when(jnp.logical_not(has_prev))
    def _():
        p_copy.start()
        p_copy.wait()

    for copy in sums:
        copy.start()
    for copy in pull_swap:
        copy.wait_send()
    u_late = local(u_ref.at[0], pull.at[rows:])
    u_late.start()

    @pl.when(has_next)
    def _():
        drive_up.wait_send()

    for n in range(4):
        for h in (0, 1):
            affine_swap[n, h].wait_recv()
    u_late.wait()

    def finish_block(i):
        cols = block(i)

        @pl.when(has_next)
        def _():
            step_down[i].wait_recv()

            @pl.loop(0, rows // 32)
            def _(j):
                offset = pl.multiple_of(j * 32, 32)
                at = pl.ds(offset, 32)
                mults = pull[pl.ds(rows + offset, 32), cols]
                following = next_in[at, cols] - step_input * drive[at, cols]
                total = fit_weight * affine[at, cols] + penalty * following + mults
                fresh = jnp.maximum(0.0, total / (fit_weight + penalty))
                affine[at, cols] = fresh
                drive[at, cols] = mults + penalty * (following - fresh)

        @pl.when(jnp.logical_not(has_next))
        def _():
            @pl.loop(0, rows // 32)
            def _(j):
                offset = pl.multiple_of(j * 32, 32)
                at = pl.ds(offset, 32)
                affine[at, cols] = jnp.maximum(0.0, affine[at, cols])
                drive[at, cols] = pull[pl.ds(rows + offset, 32), cols]

    def merge(c):
        for h in (1, 0):
            relay[h, c].wait_recv()
            start = units + h * half + c * link_rows
            at = pl.ds(start, link_rows)
            grad[at, :] = grad[at, :] + relay_in[link_part(h, c), :]
        for h in (1, 0):
            merged[h, c].start()

    def finish_weights(c):
        for h in (0, 1):
            merged[h, c].wait_recv()
            at = link_part(h, c)
            total = own_grad[at, :] + direct_in[at, :] + merged_in[at, :]
            own_grad[at, :] = w[at, :] - (step_weight * fit_weight * scaling) * total

    blocks_done, chunks_done, chunks_merged = [0], [0], [0]

    def step_on(counter, work, count):
        for i in range(counter[0], counter[0] + count):
            work(i)
        counter[0] += count

    step_on(blocks_done, finish_block, 2)
    step_on(chunks_merged, merge, 1)
    step_on(blocks_done, finish_block, 1)
    step_on(chunks_merged, merge, 2)
    step_on(blocks_done, finish_block, 1)
    step_on(chunks_merged, merge, 1)
    for copy in sums:
        copy.wait_recv()
    total = osum[0] + orecv[0] + orecv[1] + orecv[2]
    total = jnp.sum(total, axis=0, keepdims=True)
    b_new[...] = b_ref[...] - (step_offset * fit_weight) * total
    for copy in direct:
        copy.wait_recv()
    step_on(blocks_done, finish_block, 1)
    step_on(chunks_done, finish_weights, 2)
    step_on(blocks_done, finish_block, 1)
    step_on(chunks_done, finish_weights, 1)
    step_on(blocks_done, finish_block, 1)
    step_on(chunks_done, finish_weights, 1)
    step_on(blocks_done, finish_block, 1)

    for copies in (gather, target_swap, affine_swap, relay, merged):
        for copy in copies.values():
            copy.wait_send()
    for copy in (x_swap, *bias_swap, *direct, *sums):
        copy.wait_send()

    @pl.when(has_prev)
    def _():
        for copy in step_down:
            copy.wait_send()


def write_kernel(*refs):
    values, outs, sems = refs[:5], refs[5:10], refs[10]
    copies = [pltpu.make_async_copy(*pair, sems.at[i]) for i, pair in enumerate(zip(values, outs))]
    for copy in copies:
        copy.start()
    for copy in copies:
        copy.wait()


def body_fused(layer_inputs, weights, offsets, layer_outputs, multipliers):
    _, rows, width = layer_inputs.shape
    units = weights.shape[1]
    shapes = fused_shapes(rows, width, units)
    samples = rows * lax.axis_size("dp")
    anywhere = pl.BlockSpec(memory_space=pl.ANY)
    vmem = pl.BlockSpec(memory_space=pltpu.VMEM)
    args = (layer_inputs, weights, offsets, layer_outputs, multipliers)
    results = pl.pallas_call(
        functools.partial(fused_kernel, tuple(shapes), samples),
        out_shape=tuple(pltpu.VMEM(a.shape, a.dtype) for a in args),
        in_specs=[anywhere, anywhere, vmem, anywhere, anywhere],
        out_specs=[vmem] * 5,
        scratch_shapes=[pltpu.VMEM(shape, dtype) for shape, dtype in shapes.values()]
        + [
            pltpu.SemaphoreType.DMA((72,)),
            pltpu.SemaphoreType.DMA((72,)),
            pltpu.SemaphoreType.DMA((32,)),
        ],
        compiler_params=pltpu.CompilerParams(
            collective_id=0,
            has_side_effects=True,
            vmem_limit_bytes=fused_bytes(rows, width, units) + SPARE_BYTES,
        ),
        name="iteration",
    )(*args)
    return pl.pallas_call(
        write_kernel,
        out_shape=tuple(jax.ShapeDtypeStruct(a.shape, a.dtype) for a in args),
        in_specs=[vmem] * 5,
        out_specs=[anywhere] * 5,
        scratch_shapes=[pltpu.SemaphoreType.DMA((5,))],
        compiler_params=pltpu.CompilerParams(vmem_limit_bytes=SPARE_BYTES),
        name="write",
    )(*(pltpu.with_memory_space_constraint(r, pltpu.VMEM) for r in results))


def choose(mesh, layer_inputs, weights, *rest):
    if mesh.shape["dp"] != 8:
        return body_general(layer_inputs, weights, *rest)
    rows, width, units = layer_inputs.shape[1], layer_inputs.shape[2], weights.shape[1]
    tiles = rows % ROW_TILE, width % COLUMN_TILE, units % 256
    held = 4 * (3 * rows + units) * width
    total = fused_bytes(rows, width, units) + held + SPARE_BYTES
    if any(tiles) or total > VMEM_BYTES:
        return body_square(layer_inputs, weights, *rest)
    return body_fused(layer_inputs, weights, *rest)


def solution(mesh):
    specs = (
        P("depth", "dp", None),
        P("depth", "dp", None),
        P("depth", "dp"),
        P("depth", "dp", None),
        P("depth", "dp", None),
    )
    body = functools.partial(choose, mesh)
    return jax.shard_map(body, mesh=mesh, in_specs=specs, out_specs=specs, check_vma=False)
```

```python
import functools
import math

import jax
import jax.numpy as jnp
from jax import lax
from jax.experimental import pallas as pl
from jax.experimental.pallas import tpu as pltpu
from jax.sharding import PartitionSpec as P

fit_weight = 1.0
penalty = 1.0
step_input = 0.5
PRECISION = lax.Precision.HIGH


def passed_along(block, axis, distance):
    devices = range(lax.axis_size(axis))
    route = [(i - distance, i) for i in devices if i - distance in devices]
    return lax.ppermute(block, axis, route)


def swapped(block, bit):
    route = [(i, i ^ bit) for i in range(lax.axis_size("dp"))]
    return lax.ppermute(block, "dp", route)


def dot(a, b, dims):
    return lax.dot_general(a, b, (dims, ((), ())), precision=PRECISION)


def times_transposed(a, b):
    return dot(a, b, ((1,), (1,)))


def times(a, b):
    return dot(a, b, ((1,), (0,)))


def transposed_times(a, b):
    return dot(a, b, ((0,), (0,)))


def finish(inputs, outputs, mults, drive, prev_drive, affine, pulled_step, next_step):
    layer_index = lax.axis_index("depth")
    is_first = layer_index == 0
    is_last = layer_index == lax.axis_size("depth") - 1
    inputs_new = jnp.where(is_first, inputs, pulled_step - step_input * prev_drive)
    next_inputs = next_step - step_input * drive
    coupled = jnp.maximum(
        0.0, (fit_weight * affine + penalty * next_inputs + mults) / (fit_weight + penalty)
    )
    outputs_new = jnp.where(is_last, jnp.maximum(0.0, affine), coupled)
    mults_new = jnp.where(is_last, mults, mults + penalty * (next_inputs - outputs_new))
    return inputs_new, outputs_new, mults_new


def body_general(layer_inputs, weights, offsets, layer_outputs, multipliers):
    inputs, outputs, mults = layer_inputs[0], layer_outputs[0], multipliers[0]
    scaling = 1.0 / math.sqrt(inputs.shape[1])
    samples = inputs.shape[0] * lax.axis_size("dp")
    step_weight = 8.0 / math.sqrt(samples)
    step_offset = 0.5 / math.sqrt(samples)
    drive = mults - penalty * outputs
    prev_drive = passed_along(drive, "depth", 1)
    weight = lax.all_gather(weights[0], "dp", axis=0, tiled=True)
    offset = lax.all_gather(offsets, "dp", axis=1, tiled=True)
    affine = scaling * times_transposed(inputs, weight) + offset
    misfit = affine - outputs
    weight_grad = fit_weight * scaling * transposed_times(misfit, inputs)
    weight_sum = lax.psum_scatter(weight_grad, "dp", scatter_dimension=0, tiled=True)
    offset_sum = lax.psum_scatter(
        fit_weight * jnp.sum(misfit, axis=0), "dp", scatter_dimension=0, tiled=True
    )
    pulled = scaling * times(misfit, weight)
    pulled_step = inputs - step_input * (fit_weight * pulled + penalty * inputs)
    next_step = passed_along(pulled_step, "depth", -1)
    inputs_new, outputs_new, mults_new = finish(
        inputs, outputs, mults, drive, prev_drive, affine, pulled_step, next_step
    )
    weights_new = weights - step_weight * weight_sum[None]
    offsets_new = offsets - step_offset * offset_sum[None]
    return inputs_new[None], weights_new, offsets_new, outputs_new[None], mults_new[None]


def body_square(layer_inputs, weights, offsets, layer_outputs, multipliers):
    inputs, outputs, mults = layer_inputs[0], layer_outputs[0], multipliers[0]
    rows, width = inputs.shape
    units = weights.shape[1]
    half = units // 2
    scaling = 1.0 / math.sqrt(width)
    samples = rows * lax.axis_size("dp")
    step_weight = 8.0 / math.sqrt(samples)
    step_offset = 0.5 / math.sqrt(samples)
    me = lax.axis_index("dp")

    w_own = weights[0]
    low_own, high_own = w_own[:half], w_own[half:]
    low_own, high_own, inputs = lax.optimization_barrier((low_own, high_own, inputs))
    low_x, high_y = swapped(low_own, 2), swapped(high_own, 4)
    inputs_other = swapped(inputs, 1)
    inputs_other, outputs_late = lax.optimization_barrier((inputs_other, outputs))
    drive = mults - penalty * outputs
    prev_drive = passed_along(drive, "depth", 1)
    b_own = offsets
    b_x, b_y, b_d = swapped(b_own, 2), swapped(b_own, 4), swapped(b_own, 6)

    def columns(array, index):
        return lax.dynamic_slice(array, (0, index * units), (rows, units))

    def arranged(own, x, y, d):
        joined_a = jnp.concatenate([x[:, :half], y[:, half:]], axis=1)
        joined_b = jnp.concatenate([x[:, half:], y[:, :half]], axis=1)
        return own, joined_a, d, joined_b

    flips = (0, 2, 4, 6)
    out_mine = arranged(*[columns(outputs_late, me ^ f) for f in flips])
    out_sent = arranged(*[columns(outputs_late, me ^ f ^ 1) for f in flips])
    out_other = swapped(jnp.concatenate(out_sent, axis=1), 1)
    biases = arranged(b_own, b_x, b_y, b_d)
    both = jnp.concatenate([inputs, inputs_other], axis=0)

    def layer(n, w):
        affine = scaling * times_transposed(both, w) + biases[n]
        target = jnp.concatenate([out_mine[n], out_other[:, n * units : (n + 1) * units]], axis=0)
        return affine, affine - target

    affine_own, m = layer(0, w_own)
    g_own = transposed_times(m, both)
    o_own = jnp.sum(m, axis=0, keepdims=True)
    pulled = times(m, w_own)
    low_x, high_y, g_own, pulled, o_own = lax.optimization_barrier(
        (low_x, high_y, g_own, pulled, o_own)
    )

    low_d, high_d = swapped(low_x, 4), swapped(high_y, 2)
    w_a = jnp.concatenate([low_x, high_y], axis=0)
    affine_a, m = layer(1, w_a)
    g_a = transposed_times(m, both)
    o_a = jnp.sum(m, axis=0, keepdims=True)
    pulled = pulled + times(m, w_a)
    low_d, high_d, g_a, pulled, o_a, low_own, high_own = lax.optimization_barrier(
        (low_d, high_d, g_a, pulled, o_a, low_own, high_own)
    )

    high_x, low_y = swapped(high_own, 2), swapped(low_own, 4)
    w_d = jnp.concatenate([low_d, high_d], axis=0)
    affine_d, m = layer(2, w_d)
    g_d = transposed_times(m, both)
    o_d = jnp.sum(m, axis=0, keepdims=True)
    pulled = pulled + times(m, w_d)
    high_x, low_y, g_a, g_d, pulled, o_d, prev_drive = lax.optimization_barrier(
        (high_x, low_y, g_a, g_d, pulled, o_d, prev_drive)
    )

    x_low, y_high = swapped(g_a[:half], 2), swapped(g_a[half:], 4)
    from_x, from_y = swapped(g_d[:half], 2), swapped(g_d[half:], 4)
    w_b = jnp.concatenate([high_x, low_y], axis=0)
    affine_b, m = layer(3, w_b)
    pulled_other = swapped(pulled[rows:] + times(m[rows:], w_b), 1)
    pulled_mine = pulled[:rows] + times(m[:rows], w_b)
    pulled_all = scaling * (pulled_mine + pulled_other)
    pulled_step = inputs - step_input * (fit_weight * pulled_all + penalty * inputs)
    m, pulled_step = lax.optimization_barrier((m, pulled_step))
    next_step = passed_along(pulled_step, "depth", -1)
    g_b = transposed_times(m, both)
    o_b = jnp.sum(m, axis=0, keepdims=True)

    x_high = swapped(g_b[:half] + from_y, 2)
    y_low = swapped(g_b[half:] + from_x, 4)
    sum_low = g_own[:half] + x_low + y_low
    sum_high = g_own[half:] + x_high + y_high
    weight_step = step_weight * fit_weight * scaling
    weights_new = w_own - weight_step * jnp.concatenate([sum_low, sum_high], axis=0)
    o_x = jnp.concatenate([o_a[:, :half], o_b[:, :half]], axis=1)
    o_y = jnp.concatenate([o_b[:, half:], o_a[:, half:]], axis=1)
    offset_sum = o_own + swapped(o_x, 2) + swapped(o_y, 4) + swapped(o_d, 6)
    offsets_new = offsets - step_offset * fit_weight * offset_sum

    affines = (affine_own, affine_a, affine_d, affine_b)
    affine_other = swapped(jnp.concatenate([a[rows:] for a in affines], axis=1), 1)

    def by_owner(own, a, d, b):
        x = jnp.concatenate([a[:, :half], b[:, :half]], axis=1)
        y = jnp.concatenate([b[:, half:], a[:, half:]], axis=1)
        return own, x, y, d

    mine = by_owner(*[a[:rows] for a in affines])
    other = by_owner(*[affine_other[:, n * units : (n + 1) * units] for n in range(len(flips))])
    affine = jnp.zeros_like(outputs)
    for n, f in enumerate(flips):
        affine = lax.dynamic_update_slice(affine, mine[n], (0, (me ^ f) * units))
        affine = lax.dynamic_update_slice(affine, other[n], (0, (me ^ f ^ 1) * units))
    inputs_new, outputs_new, mults_new = finish(
        inputs, outputs, mults, drive, prev_drive, affine, pulled_step, next_step
    )
    return (
        inputs_new[None],
        weights_new[None],
        offsets_new,
        outputs_new[None],
        mults_new[None],
    )


MESH = pl.DeviceIdType.MESH
VMEM_BYTES = 67043328
SPARE_BYTES = 2**22
OWNERS = ((0, 0), (2, 4), (4, 2), (6, 6))
X, Y, DIAGONAL, PARTNER = 2, 4, 6, 1
ROW_TILE = 128
COLUMN_TILE = 256
LINK_CHUNKS = 4
EARLY_PART = 0.875


def fused_shapes(rows, width, units):
    f32, bf16 = jnp.float32, jnp.bfloat16
    return dict(
        pull=((2 * rows, width), f32),
        x_high=((2 * rows, width), bf16),
        x_low=((2 * rows, width), bf16),
        w=((4 * units, width), f32),
        w_high=((units, width), bf16),
        w_low=((units, width), bf16),
        target=((4, 2 * rows, units), f32),
        m_high=((2 * rows, units), bf16),
        m_low=((2 * rows, units), bf16),
        mt_high=((units, 2 * rows), bf16),
        mt_low=((units, 2 * rows), bf16),
        product=((2 * rows, units), f32),
        pull_in=((rows, width), f32),
        grad=((3 * units, width), f32),
        direct_in=((units, width), f32),
        relay_in=((units, width), f32),
        merged_in=((units, width), f32),
        next_in=((rows, width), f32),
        bias=((4, 8, units), f32),
        osum=((4, 8, units), f32),
        osend=((3, 8, units), f32),
        orecv=((3, 8, units), f32),
    )


def fused_bytes(rows, width, units):
    shapes = fused_shapes(rows, width, units).values()
    return sum(math.prod(shape) * jnp.dtype(dtype).itemsize for shape, dtype in shapes)


def pull_blocks(width):
    narrow = COLUMN_TILE // 2
    widths = [narrow] * 2 + [COLUMN_TILE] * (width // COLUMN_TILE - 2) + [narrow] * 2
    return [slice(sum(widths[:i]), sum(widths[: i + 1])) for i in range(len(widths))]


def semaphore_counts(width):
    return 13, 18 + 2 * LINK_CHUNKS + 2 * len(pull_blocks(width)), 5


def fused_kernel(
    names, samples, x_ref, w_ref, b_ref, q_ref, u_ref, p_new, w_new, b_new, q_new, u_new, *scratch
):
    ref = dict(zip(names, scratch))
    send_sem, recv_sem, local_sem = scratch[len(names) :]
    pull, x_high, x_low, w = ref["pull"], ref["x_high"], ref["x_low"], ref["w"]
    w_high, w_low, target = ref["w_high"], ref["w_low"], ref["target"]
    m_high, m_low, mt_high, mt_low = ref["m_high"], ref["m_low"], ref["mt_high"], ref["mt_low"]
    pull_in, grad, partial = ref["pull_in"], ref["grad"], ref["product"]
    direct_in, relay_in, merged_in = ref["direct_in"], ref["relay_in"], ref["merged_in"]
    next_in = ref["next_in"]
    prev_in, own_grad, affine, drive = p_new.at[0], w_new.at[0], q_new.at[0], u_new.at[0]
    bias, osum, osend, orecv = ref["bias"], ref["osum"], ref["osend"], ref["orecv"]

    rows, width = affine.shape
    units = w_high.shape[0]
    half = units // 2
    scaling = 1.0 / math.sqrt(width)
    step_weight = 8.0 / math.sqrt(samples)
    step_offset = 0.5 / math.sqrt(samples)
    pull_factor = step_input * fit_weight * scaling
    keep_factor = 1.0 - step_input * penalty

    me, z = lax.axis_index("dp"), lax.axis_index("depth")
    has_prev, has_next = z > 0, z < lax.axis_size("depth") - 1
    bits = (me % 2, (me // 2) % 2, me // 4)

    def index_of(flip):
        return sum(((1 - b) if flip >> i & 1 else b) * 2**i for i, b in enumerate(bits))

    def device(flip):
        return (z, index_of(flip))

    above, below = (z + 1, me), (z - 1, me)
    sends, receives, locals_ = {}, {}, {}

    def slot(sems, taken, key):
        return sems.at[taken.setdefault(key, len(taken))]

    def remote(src, dst, to, sent, received):
        return pltpu.make_async_remote_copy(
            src_ref=src,
            dst_ref=dst,
            send_sem=slot(send_sem, sends, sent),
            recv_sem=slot(recv_sem, receives, received),
            device_id=to,
            device_id_type=MESH,
        )

    def local(src, dst, key):
        return pltpu.make_async_copy(src, dst, slot(local_sem, locals_, key))

    def wait_sent(key, buffer):
        pltpu.make_async_copy(buffer, buffer, slot(send_sem, sends, key)).wait()

    def wait_received(key, buffer):
        pltpu.make_async_copy(buffer, buffer, slot(recv_sem, receives, key)).wait()

    def columns(flip, h):
        return pl.ds(pl.multiple_of(index_of(flip) * units + h * half, half), half)

    def halves(h):
        return pl.ds(h * half, half)

    w_in = local(w_ref.at[0], w.at[:units], "w")
    w_in.start()
    x_in = local(x_ref.at[0], pull.at[:rows], "x")
    x_in.start()
    bias[0] = jnp.broadcast_to(b_ref[...], (8, units))

    barrier = pltpu.get_barrier_semaphore()
    for flip in (PARTNER, X, Y):
        pl.semaphore_signal(barrier, inc=1, device_id=device(flip), device_id_type=MESH)

    @pl.when(has_prev)
    def _():
        pl.semaphore_signal(barrier, inc=1, device_id=below, device_id_type=MESH)

    @pl.when(has_next)
    def _():
        pl.semaphore_signal(barrier, inc=1, device_id=above, device_id_type=MESH)


    depth = lax.axis_size("depth")
    pl.semaphore_wait(barrier, 3 + (z + depth - 1) // depth + 1 - (z + 1) // depth)

    bias_swap = [
        remote(bias.at[0], bias.at[flip // 2], device(flip), "bias", ("bias", flip))
        for flip in (X, Y)
    ]
    for copy in bias_swap:
        copy.start()
    w_in.wait()
    for piece, h, to in ((1, 0, X), (1, 1, Y), (2, 1, X), (2, 0, Y)):
        dst = w.at[pl.ds(piece * units + h * half, half)]
        remote(w.at[halves(h)], dst, device(to), "own", ("own", piece)).start()
    x_swap = remote(x_ref.at[0], pull.at[rows:], device(PARTNER), "x", "x")
    x_swap.start()

    def start_targets(n):
        for h, flip in enumerate(OWNERS[n]):
            src = q_ref.at[0, :, columns(flip, h)]
            local(src, target.at[n, :rows, halves(h)], "target").start()
            src = q_ref.at[0, :, columns(flip ^ PARTNER, h)]
            dst = target.at[n, rows:, halves(h)]
            remote(src, dst, device(PARTNER), "target", ("target", n)).start()

    start_targets(0)
    staged = grad.at[:rows]
    q_in, u_in = local(q_ref.at[0], staged, "q"), local(u_ref.at[0], drive, "u")
    q_in.start()
    u_in.start()
    for n in (1, 2, 3):
        start_targets(n)

    def split(value):
        high = value.astype(jnp.bfloat16)
        return high, (value - high.astype(jnp.float32)).astype(jnp.bfloat16)

    def split_rows(src, start, high, low, to, count, cols=slice(None)):
        step = 16 if cols == slice(None) else max(16, 16 * width // (cols.stop - cols.start) // 2)

        @pl.loop(0, count // step)
        def _(i):
            offset = pl.multiple_of(i * step, step)
            high_part, low_part = split(src[pl.ds(start + offset, step), cols])
            high[pl.ds(to + offset, step), cols] = high_part
            low[pl.ds(to + offset, step), cols] = low_part

    def dot(a, b, contract):
        return lax.dot_general(a, b, (contract, ((), ())), preferred_element_type=jnp.float32)

    def dot3(a, b, contract):
        return (
            dot(a[0], b[0], contract) + dot(a[1], b[0], contract) + dot(a[0], b[1], contract)
        )

    def product_part(side, cols, first, last, n):
        owners = OWNERS[n]
        at = pl.ds(side * rows, rows)
        value = dot3(
            (x_high[at, cols], x_low[at, cols]), (w_high[:, cols], w_low[:, cols]), ((1,), (1,))
        )
        if first:
            shift = [bias[owners[h] // 2, 0:1, h * half : (h + 1) * half] for h in (0, 1)]
            value = scaling * value + jnp.concatenate(shift, axis=1)
        if not last:
            partial[at, :] = value - target[n, at, :]
            return
        m = value - target[n, at, :] if first else scaling * value + partial[at, :]
        m_high[at, :], m_low[at, :] = split(m)
        if first:
            keep_affine(side, value, m, n)
        else:
            partial[at, :] = m

    def keep_affine(side, value, m, n):
        if side == 0:
            for h, flip in enumerate(OWNERS[n]):
                affine[:, columns(flip, h)] = value[:, h * half : (h + 1) * half]
        else:
            target[n, rows:, :] = value
        sums = jnp.sum(m.reshape(rows // 8, 8, units), axis=0)
        osum[n] = sums if side == 1 else osum[n] + sums

    def product(n):
        split_rows(w, n * units, w_high, w_low, 0, units)
        for side in (1, 0):
            product_part(side, slice(None), True, True, n)

    def pull_tile(at, cols):
        a = (m_high[at, :], m_low[at, :])
        return dot3(a, (w_high[:, cols], w_low[:, cols]), ((1,), (0,)))

    def column_loop(body):
        @pl.loop(0, width // COLUMN_TILE)
        def _(c):
            body(pl.ds(pl.multiple_of(c * COLUMN_TILE, COLUMN_TILE), COLUMN_TILE))

    def pull_add(n):
        for side in (1, 0):
            at = pl.ds(side * rows, rows)

            def body(cols):
                value = pull_tile(at, cols)
                if n > 0:
                    value += pull[at, cols]
                elif side == 0:
                    value -= (keep_factor / pull_factor) * pull[at, cols]
                pull[at, cols] = value

            column_loop(body)

    def gradient(n):
        for part, turned in ((m_high, mt_high), (m_low, mt_low)):

            @pl.loop(0, 2 * rows // ROW_TILE)
            def _(i):
                at = pl.ds(pl.multiple_of(i * ROW_TILE, ROW_TILE), ROW_TILE)
                turned[:, at] = part[at, :].astype(jnp.float32).T.astype(jnp.bfloat16)

        def body(cols):
            b = (x_high[:, cols], x_low[:, cols])
            value = dot3((mt_high[...], mt_low[...]), b, ((1,), (0,)))
            if n == 0:
                own_grad[:, cols] = value
            else:
                grad[pl.ds((n - 1) * units, units), cols] = value

        column_loop(body)

    def send_affine(n):
        for h, flip in enumerate(OWNERS[n]):
            src = target.at[n, rows:, halves(h)]
            dst = affine.at[:, columns(flip, h)]
            remote(src, dst, device(PARTNER), "affine", "affine").start()

    def wait_targets(n):
        wait_received(("target", n), target.at[n, rows:])

    x_in.wait()
    split_rows(pull, 0, x_high, x_low, 0, rows)
    x_swap.wait_recv()
    split_rows(pull, rows, x_high, x_low, rows, rows)
    whole = target.at[:, :rows]
    local(whole, whole, "target").wait()
    wait_targets(0)
    product(0)
    q_in.wait()
    u_in.wait()

    @pl.loop(0, rows // 16)
    def _(i):
        offset = pl.multiple_of(i * 16, 16)
        at = pl.ds(offset, 16)
        drive[at, :] = drive[at, :] - penalty * grad[pl.ds(offset, 16), :]

    pull_add(0)
    drive_up = remote(drive, prev_in, above, "drive", "drive")

    @pl.when(has_next)
    def _():
        drive_up.start()

    send_affine(0)
    gradient(0)

    for copy in bias_swap:
        copy.wait_recv()
    bias_on = remote(bias.at[1], bias.at[3], device(Y), "bias", ("bias", DIAGONAL))
    bias_on.start()
    wait_received(("own", 1), w.at[units : 2 * units])
    cut = int(width * EARLY_PART) // 128 * 128
    parts = (slice(0, cut), slice(cut, width))
    for k, cols in enumerate(parts):
        for h, to in ((1, X), (0, Y)):
            src = w.at[pl.ds(units + h * half, half), cols]
            dst = w.at[pl.ds(3 * units + h * half, half), cols]
            remote(src, dst, device(to), "forward", ("forward", k)).start()
    wait_targets(1)
    product(1)
    gradient(1)
    pull_add(1)
    send_affine(1)
    for h, to in ((0, X), (1, Y)):
        src = grad.at[halves(h)]
        remote(src, direct_in.at[halves(h)], device(to), "direct", "direct").start()

    wait_received(("own", 2), w.at[2 * units : 3 * units])
    wait_targets(2)
    product(2)
    gradient(2)
    pull_add(2)
    send_affine(2)

    wait_targets(3)
    early, late = parts
    bias_on.wait_recv()
    wait_received(("forward", 0), w.at[3 * units :, early])
    split_rows(w, 3 * units, w_high, w_low, 0, units, early)
    for side in (1, 0):
        product_part(side, early, True, False, 3)

    blocks = pull_blocks(width)
    pull_swap, step_down = [], []
    for i, cols in enumerate(blocks):
        ends = pull.at[rows:, cols], pull_in.at[:, cols]
        pull_swap.append(remote(*ends, device(PARTNER), "pull", ("pull", i)))
        ends = pull.at[:rows, cols], next_in.at[:, cols]
        step_down.append(remote(*ends, below, "step", ("step", i)))

    def pull_last(side, i):
        if i < len(blocks):
            at = pl.ds(side * rows, rows)
            pull[at, blocks[i]] = pull[at, blocks[i]] + pull_tile(at, blocks[i])

    def swap(i):
        if i < len(blocks):
            pull_swap[i].start()

    def pull_done(i):
        cols = blocks[i]
        pull_swap[i].wait_recv()
        pull[:rows, cols] = -pull_factor * (pull[:rows, cols] + pull_in[:, cols])

    def send_down(i):
        @pl.when(has_prev)
        def _():
            step_down[i].start()

    wait_received(("forward", 1), w.at[3 * units :, late])
    split_rows(w, 3 * units, w_high, w_low, 0, units, late)
    product_part(1, late, False, True, 3)
    pull_last(1, 0)
    swap(0)
    product_part(0, late, False, True, 3)
    pull_last(0, 0)
    pull_last(1, 1)
    pull_done(0)
    swap(1)
    send_down(0)
    pull_last(1, 2)
    for i in range(1, len(blocks)):
        pull_last(0, i)
        swap(i + 1)
        pull_done(i)
        pull_last(1, i + 2)
        send_down(i)
    for side in (1, 0):
        m = partial[pl.ds(side * rows, rows), :]
        keep_affine(side, m + target[3, pl.ds(side * rows, rows), :], m, 3)
    send_affine(3)
    gradient(3)
    link_rows = half // LINK_CHUNKS
    merged = {}

    def link_part(h, c):
        return pl.ds(h * half + c * link_rows, link_rows)

    for c in range(LINK_CHUNKS):
        for h, to in ((0, X), (1, Y)):
            at = link_part(h, c)
            src = grad.at[pl.ds(2 * units + h * half + c * link_rows, link_rows)]
            remote(src, relay_in.at[at], device(to), "relay", ("relay", c)).start()
    for c in range(LINK_CHUNKS):
        for h, to in ((1, X), (0, Y)):
            src = grad.at[pl.ds(units + h * half + c * link_rows, link_rows)]
            dst = merged_in.at[link_part(h, c)]
            merged[h, c] = remote(src, dst, device(to), "merged", ("merged", c))

    for k, (low, high) in enumerate(((1, 2), (2, 1), (3, 3))):
        osend[k, :, :half] = osum[low, :, :half]
        osend[k, :, half:] = osum[high, :, half:]
    sums = [
        remote(osend.at[k], orecv.at[k], device(flip), "sums", ("sums", k))
        for k, flip in enumerate((X, Y, X))
    ]


    @pl.when(has_prev)
    def _():
        drive_up.wait_recv()

        @pl.loop(0, rows // 16)
        def _(i):
            at = pl.ds(pl.multiple_of(i * 16, 16), 16)
            prev_in[at, :] = pull[at, :] - step_input * prev_in[at, :]

    p_copy = local(x_ref.at[0], prev_in, "x")

    @pl.when(jnp.logical_not(has_prev))
    def _():
        p_copy.start()
        p_copy.wait()

    sums[0].start()
    sums[2].start()
    wait_sent("pull", pull.at[rows:])
    u_late = local(u_ref.at[0], pull.at[rows:], "u")
    u_late.start()

    @pl.when(has_next)
    def _():
        drive_up.wait_send()

    wait_received("affine", affine.at[:, : width // 2])
    u_late.wait()

    def finish_block(i):
        cols = blocks[i]

        @pl.when(has_next)
        def _():
            step_down[i].wait_recv()

            @pl.loop(0, rows // 32)
            def _(j):
                offset = pl.multiple_of(j * 32, 32)
                at = pl.ds(offset, 32)
                mults = pull[pl.ds(rows + offset, 32), cols]
                following = next_in[at, cols] - step_input * drive[at, cols]
                total = fit_weight * affine[at, cols] + penalty * following + mults
                fresh = jnp.maximum(0.0, total / (fit_weight + penalty))
                affine[at, cols] = fresh
                drive[at, cols] = mults + penalty * (following - fresh)

        @pl.when(jnp.logical_not(has_next))
        def _():
            @pl.loop(0, rows // 32)
            def _(j):
                offset = pl.multiple_of(j * 32, 32)
                at = pl.ds(offset, 32)
                affine[at, cols] = jnp.maximum(0.0, affine[at, cols])
                drive[at, cols] = pull[pl.ds(rows + offset, 32), cols]

    def merge(c):
        wait_received(("relay", c), relay_in.at[: 2 * link_rows])
        for h in (1, 0):
            start = units + h * half + c * link_rows
            at = pl.ds(start, link_rows)
            grad[at, :] = grad[at, :] + relay_in[link_part(h, c), :]
        for h in (1, 0):
            merged[h, c].start()

    def finish_weights(c):
        wait_received(("merged", c), merged_in.at[: 2 * link_rows])
        for h in (0, 1):
            at = link_part(h, c)
            total = own_grad[at, :] + direct_in[at, :] + merged_in[at, :]
            own_grad[at, :] = w[at, :] - (step_weight * fit_weight * scaling) * total

    def merge_offsets(_):
        wait_received("direct", direct_in)
        sums[2].wait_recv()
        osend[1] = osend[1] + orecv[2]
        sums[1].start()

    def finish_offsets(_):
        sums[0].wait_recv()
        sums[1].wait_recv()
        total = osum[0] + orecv[0] + orecv[1]
        total = jnp.sum(total, axis=0, keepdims=True)
        b_new[...] = b_ref[...] - (step_offset * fit_weight) * total

    ready, stage = [], width / 3
    for i, cols in enumerate(blocks):
        ready.append((cols.stop / stage + 0.2, finish_block, i))
    for c in range(LINK_CHUNKS):
        ready.append((1 + (c + 1) / LINK_CHUNKS, merge, c))
        ready.append((2 + (c + 1) / LINK_CHUNKS, finish_weights, c))
    ready.append((2.1, merge_offsets, 0))
    ready.append((2.6, finish_offsets, 0))
    def settle(_):
        wait_sent("own", w.at[: 2 * units])
        wait_sent("forward", w.at[:units])
        wait_sent("x", pull.at[:rows])
        wait_sent("target", target.at[:, :rows])
        wait_sent("affine", target.at[:, :rows])
        wait_sent("bias", bias.at[1:])
        wait_sent("direct", direct_in)
        wait_sent("relay", relay_in)
        wait_sent("sums", orecv)

    ready.append((blocks[-1].start / stage - 0.1, settle, 0))
    for _, work, i in sorted(ready, key=lambda entry: entry[0]):
        work(i)
    wait_sent("merged", merged_in)

    @pl.when(has_prev)
    def _():
        wait_sent("step", pull.at[:rows])

    counts = len(sends), len(receives), len(locals_)
    if counts != semaphore_counts(width):
        raise ValueError(counts)


def write_kernel(*refs):
    values, outs, sems = refs[:5], refs[5:10], refs[10]
    copies = [pltpu.make_async_copy(*pair, sems.at[i]) for i, pair in enumerate(zip(values, outs))]
    for copy in copies:
        copy.start()
    for copy in copies:
        copy.wait()


def body_fused(layer_inputs, weights, offsets, layer_outputs, multipliers):
    _, rows, width = layer_inputs.shape
    units = weights.shape[1]
    shapes = fused_shapes(rows, width, units)
    samples = rows * lax.axis_size("dp")
    anywhere = pl.BlockSpec(memory_space=pl.ANY)
    vmem = pl.BlockSpec(memory_space=pltpu.VMEM)
    args = (layer_inputs, weights, offsets, layer_outputs, multipliers)
    results = pl.pallas_call(
        functools.partial(fused_kernel, tuple(shapes), samples),
        out_shape=tuple(pltpu.VMEM(a.shape, a.dtype) for a in args),
        in_specs=[anywhere, anywhere, vmem, anywhere, anywhere],
        out_specs=[vmem] * 5,
        scratch_shapes=[pltpu.VMEM(shape, dtype) for shape, dtype in shapes.values()]
        + [pltpu.SemaphoreType.DMA((count,)) for count in semaphore_counts(width)],
        compiler_params=pltpu.CompilerParams(
            collective_id=0,
            has_side_effects=True,
            vmem_limit_bytes=fused_bytes(rows, width, units) + SPARE_BYTES,
        ),
        name="iteration",
    )(*args)
    return pl.pallas_call(
        write_kernel,
        out_shape=tuple(jax.ShapeDtypeStruct(a.shape, a.dtype) for a in args),
        in_specs=[vmem] * 5,
        out_specs=[anywhere] * 5,
        scratch_shapes=[pltpu.SemaphoreType.DMA((5,))],
        compiler_params=pltpu.CompilerParams(vmem_limit_bytes=SPARE_BYTES),
        name="write",
    )(*(pltpu.with_memory_space_constraint(r, pltpu.VMEM) for r in results))


def choose(mesh, layer_inputs, weights, *rest):
    if mesh.shape["dp"] != 8:
        return body_general(layer_inputs, weights, *rest)
    rows, width, units = layer_inputs.shape[1], layer_inputs.shape[2], weights.shape[1]
    tiles = rows % ROW_TILE, width % COLUMN_TILE, units % 256
    held = 4 * (3 * rows + units) * width
    total = fused_bytes(rows, width, units) + held + SPARE_BYTES
    if any(tiles) or total > VMEM_BYTES:
        return body_square(layer_inputs, weights, *rest)
    return body_fused(layer_inputs, weights, *rest)


def solution(mesh):
    specs = (
        P("depth", "dp", None),
        P("depth", "dp", None),
        P("depth", "dp"),
        P("depth", "dp", None),
        P("depth", "dp", None),
    )
    body = functools.partial(choose, mesh)
    return jax.shard_map(body, mesh=mesh, in_specs=specs, out_specs=specs, check_vma=False)
```

```python
import functools
import math

import jax
import jax.numpy as jnp
from jax import lax
from jax.experimental import pallas as pl
from jax.experimental.pallas import tpu as pltpu
from jax.sharding import PartitionSpec as P

fit_weight = 1.0
penalty = 1.0
step_input = 0.5
PRECISION = lax.Precision.HIGH


def passed_along(block, axis, distance):
    devices = range(lax.axis_size(axis))
    route = [(i - distance, i) for i in devices if i - distance in devices]
    return lax.ppermute(block, axis, route)


def swapped(block, bit):
    route = [(i, i ^ bit) for i in range(lax.axis_size("dp"))]
    return lax.ppermute(block, "dp", route)


def dot(a, b, dims):
    return lax.dot_general(a, b, (dims, ((), ())), precision=PRECISION)


def times_transposed(a, b):
    return dot(a, b, ((1,), (1,)))


def times(a, b):
    return dot(a, b, ((1,), (0,)))


def transposed_times(a, b):
    return dot(a, b, ((0,), (0,)))


def finish(inputs, outputs, mults, drive, prev_drive, affine, pulled_step, next_step):
    layer_index = lax.axis_index("depth")
    is_first = layer_index == 0
    is_last = layer_index == lax.axis_size("depth") - 1
    inputs_new = jnp.where(is_first, inputs, pulled_step - step_input * prev_drive)
    next_inputs = next_step - step_input * drive
    coupled = jnp.maximum(
        0.0, (fit_weight * affine + penalty * next_inputs + mults) / (fit_weight + penalty)
    )
    outputs_new = jnp.where(is_last, jnp.maximum(0.0, affine), coupled)
    mults_new = jnp.where(is_last, mults, mults + penalty * (next_inputs - outputs_new))
    return inputs_new, outputs_new, mults_new


def body_general(layer_inputs, weights, offsets, layer_outputs, multipliers):
    inputs, outputs, mults = layer_inputs[0], layer_outputs[0], multipliers[0]
    scaling = 1.0 / math.sqrt(inputs.shape[1])
    samples = inputs.shape[0] * lax.axis_size("dp")
    step_weight = 8.0 / math.sqrt(samples)
    step_offset = 0.5 / math.sqrt(samples)
    drive = mults - penalty * outputs
    prev_drive = passed_along(drive, "depth", 1)
    weight = lax.all_gather(weights[0], "dp", axis=0, tiled=True)
    offset = lax.all_gather(offsets, "dp", axis=1, tiled=True)
    affine = scaling * times_transposed(inputs, weight) + offset
    misfit = affine - outputs
    weight_grad = fit_weight * scaling * transposed_times(misfit, inputs)
    weight_sum = lax.psum_scatter(weight_grad, "dp", scatter_dimension=0, tiled=True)
    offset_sum = lax.psum_scatter(
        fit_weight * jnp.sum(misfit, axis=0), "dp", scatter_dimension=0, tiled=True
    )
    pulled = scaling * times(misfit, weight)
    pulled_step = inputs - step_input * (fit_weight * pulled + penalty * inputs)
    next_step = passed_along(pulled_step, "depth", -1)
    inputs_new, outputs_new, mults_new = finish(
        inputs, outputs, mults, drive, prev_drive, affine, pulled_step, next_step
    )
    weights_new = weights - step_weight * weight_sum[None]
    offsets_new = offsets - step_offset * offset_sum[None]
    return inputs_new[None], weights_new, offsets_new, outputs_new[None], mults_new[None]


def body_square(layer_inputs, weights, offsets, layer_outputs, multipliers):
    inputs, outputs, mults = layer_inputs[0], layer_outputs[0], multipliers[0]
    rows, width = inputs.shape
    units = weights.shape[1]
    half = units // 2
    scaling = 1.0 / math.sqrt(width)
    samples = rows * lax.axis_size("dp")
    step_weight = 8.0 / math.sqrt(samples)
    step_offset = 0.5 / math.sqrt(samples)
    me = lax.axis_index("dp")

    w_own = weights[0]
    low_own, high_own = w_own[:half], w_own[half:]
    low_own, high_own, inputs = lax.optimization_barrier((low_own, high_own, inputs))
    low_x, high_y = swapped(low_own, 2), swapped(high_own, 4)
    inputs_other = swapped(inputs, 1)
    inputs_other, outputs_late = lax.optimization_barrier((inputs_other, outputs))
    drive = mults - penalty * outputs
    prev_drive = passed_along(drive, "depth", 1)
    b_own = offsets
    b_x, b_y, b_d = swapped(b_own, 2), swapped(b_own, 4), swapped(b_own, 6)

    def columns(array, index):
        return lax.dynamic_slice(array, (0, index * units), (rows, units))

    def arranged(own, x, y, d):
        joined_a = jnp.concatenate([x[:, :half], y[:, half:]], axis=1)
        joined_b = jnp.concatenate([x[:, half:], y[:, :half]], axis=1)
        return own, joined_a, d, joined_b

    flips = (0, 2, 4, 6)
    out_mine = arranged(*[columns(outputs_late, me ^ f) for f in flips])
    out_sent = arranged(*[columns(outputs_late, me ^ f ^ 1) for f in flips])
    out_other = swapped(jnp.concatenate(out_sent, axis=1), 1)
    biases = arranged(b_own, b_x, b_y, b_d)
    both = jnp.concatenate([inputs, inputs_other], axis=0)

    def layer(n, w):
        affine = scaling * times_transposed(both, w) + biases[n]
        target = jnp.concatenate([out_mine[n], out_other[:, n * units : (n + 1) * units]], axis=0)
        return affine, affine - target

    affine_own, m = layer(0, w_own)
    g_own = transposed_times(m, both)
    o_own = jnp.sum(m, axis=0, keepdims=True)
    pulled = times(m, w_own)
    low_x, high_y, g_own, pulled, o_own = lax.optimization_barrier(
        (low_x, high_y, g_own, pulled, o_own)
    )

    low_d, high_d = swapped(low_x, 4), swapped(high_y, 2)
    w_a = jnp.concatenate([low_x, high_y], axis=0)
    affine_a, m = layer(1, w_a)
    g_a = transposed_times(m, both)
    o_a = jnp.sum(m, axis=0, keepdims=True)
    pulled = pulled + times(m, w_a)
    low_d, high_d, g_a, pulled, o_a, low_own, high_own = lax.optimization_barrier(
        (low_d, high_d, g_a, pulled, o_a, low_own, high_own)
    )

    high_x, low_y = swapped(high_own, 2), swapped(low_own, 4)
    w_d = jnp.concatenate([low_d, high_d], axis=0)
    affine_d, m = layer(2, w_d)
    g_d = transposed_times(m, both)
    o_d = jnp.sum(m, axis=0, keepdims=True)
    pulled = pulled + times(m, w_d)
    high_x, low_y, g_a, g_d, pulled, o_d, prev_drive = lax.optimization_barrier(
        (high_x, low_y, g_a, g_d, pulled, o_d, prev_drive)
    )

    x_low, y_high = swapped(g_a[:half], 2), swapped(g_a[half:], 4)
    from_x, from_y = swapped(g_d[:half], 2), swapped(g_d[half:], 4)
    w_b = jnp.concatenate([high_x, low_y], axis=0)
    affine_b, m = layer(3, w_b)
    pulled_other = swapped(pulled[rows:] + times(m[rows:], w_b), 1)
    pulled_mine = pulled[:rows] + times(m[:rows], w_b)
    pulled_all = scaling * (pulled_mine + pulled_other)
    pulled_step = inputs - step_input * (fit_weight * pulled_all + penalty * inputs)
    m, pulled_step = lax.optimization_barrier((m, pulled_step))
    next_step = passed_along(pulled_step, "depth", -1)
    g_b = transposed_times(m, both)
    o_b = jnp.sum(m, axis=0, keepdims=True)

    x_high = swapped(g_b[:half] + from_y, 2)
    y_low = swapped(g_b[half:] + from_x, 4)
    sum_low = g_own[:half] + x_low + y_low
    sum_high = g_own[half:] + x_high + y_high
    weight_step = step_weight * fit_weight * scaling
    weights_new = w_own - weight_step * jnp.concatenate([sum_low, sum_high], axis=0)
    o_x = jnp.concatenate([o_a[:, :half], o_b[:, :half]], axis=1)
    o_y = jnp.concatenate([o_b[:, half:], o_a[:, half:]], axis=1)
    offset_sum = o_own + swapped(o_x, 2) + swapped(o_y, 4) + swapped(o_d, 6)
    offsets_new = offsets - step_offset * fit_weight * offset_sum

    affines = (affine_own, affine_a, affine_d, affine_b)
    affine_other = swapped(jnp.concatenate([a[rows:] for a in affines], axis=1), 1)

    def by_owner(own, a, d, b):
        x = jnp.concatenate([a[:, :half], b[:, :half]], axis=1)
        y = jnp.concatenate([b[:, half:], a[:, half:]], axis=1)
        return own, x, y, d

    mine = by_owner(*[a[:rows] for a in affines])
    other = by_owner(*[affine_other[:, n * units : (n + 1) * units] for n in range(len(flips))])
    affine = jnp.zeros_like(outputs)
    for n, f in enumerate(flips):
        affine = lax.dynamic_update_slice(affine, mine[n], (0, (me ^ f) * units))
        affine = lax.dynamic_update_slice(affine, other[n], (0, (me ^ f ^ 1) * units))
    inputs_new, outputs_new, mults_new = finish(
        inputs, outputs, mults, drive, prev_drive, affine, pulled_step, next_step
    )
    return (
        inputs_new[None],
        weights_new[None],
        offsets_new,
        outputs_new[None],
        mults_new[None],
    )


MESH = pl.DeviceIdType.MESH
VMEM_BYTES = 67043328
SPARE_BYTES = 2**22
OWNERS = ((0, 0), (2, 4), (4, 2), (6, 6))
X, Y, DIAGONAL, PARTNER = 2, 4, 6, 1
ROW_TILE = 128
COLUMN_TILE = 256
LINK_CHUNKS = 4
EARLY_PART = 0.875


def fused_shapes(rows, width, units):
    f32, bf16 = jnp.float32, jnp.bfloat16
    return dict(
        pull=((2 * rows, width), f32),
        x_high=((2 * rows, width), bf16),
        x_low=((2 * rows, width), bf16),
        w=((4 * units, width), f32),
        w_high=((units, width), bf16),
        w_low=((units, width), bf16),
        target=((4, 2 * rows, units), f32),
        m_high=((2 * rows, units), bf16),
        m_low=((2 * rows, units), bf16),
        mt_high=((units, 2 * rows), bf16),
        mt_low=((units, 2 * rows), bf16),
        product=((2 * rows, units), f32),
        pull_in=((rows, width), f32),
        grad=((3 * units, width), f32),
        direct_in=((units, width), f32),
        relay_in=((units, width), f32),
        merged_in=((units, width), f32),
        next_in=((rows, width), f32),
        bias=((4, 8, units), f32),
        own_bias=((1, units), f32),
        osum=((4, 8, units), f32),
        osend=((3, 8, units), f32),
        orecv=((3, 8, units), f32),
    )


def fused_bytes(rows, width, units):
    shapes = fused_shapes(rows, width, units).values()
    return sum(math.prod(shape) * jnp.dtype(dtype).itemsize for shape, dtype in shapes)


def pull_blocks(width):
    narrow = COLUMN_TILE // 2
    widths = [narrow] * 2 + [COLUMN_TILE] * (width // COLUMN_TILE - 2) + [narrow] * 2
    return [slice(sum(widths[:i]), sum(widths[: i + 1])) for i in range(len(widths))]


def semaphore_counts(width):
    return 13, 18 + 2 * LINK_CHUNKS + 2 * len(pull_blocks(width)), 6


def fused_kernel(
    names, samples, x_ref, w_ref, b_ref, q_ref, u_ref, p_new, w_new, b_new, q_new, u_new, *scratch
):
    ref = dict(zip(names, scratch))
    send_sem, recv_sem, local_sem = scratch[len(names) :]
    pull, x_high, x_low, w = ref["pull"], ref["x_high"], ref["x_low"], ref["w"]
    w_high, w_low, target = ref["w_high"], ref["w_low"], ref["target"]
    m_high, m_low, mt_high, mt_low = ref["m_high"], ref["m_low"], ref["mt_high"], ref["mt_low"]
    pull_in, grad, partial = ref["pull_in"], ref["grad"], ref["product"]
    direct_in, relay_in, merged_in = ref["direct_in"], ref["relay_in"], ref["merged_in"]
    next_in = ref["next_in"]
    prev_in, own_grad, affine, drive = p_new.at[0], w_new.at[0], q_new.at[0], u_new.at[0]
    bias, osum, osend, orecv = ref["bias"], ref["osum"], ref["osend"], ref["orecv"]
    own_bias = ref["own_bias"]

    rows, width = affine.shape
    units = w_high.shape[0]
    half = units // 2
    scaling = 1.0 / math.sqrt(width)
    step_weight = 8.0 / math.sqrt(samples)
    step_offset = 0.5 / math.sqrt(samples)
    pull_factor = step_input * fit_weight * scaling
    keep_factor = 1.0 - step_input * penalty

    me, z = lax.axis_index("dp"), lax.axis_index("depth")
    has_prev, has_next = z > 0, z < lax.axis_size("depth") - 1
    bits = (me % 2, (me // 2) % 2, me // 4)

    def index_of(flip):
        return sum(((1 - b) if flip >> i & 1 else b) * 2**i for i, b in enumerate(bits))

    def device(flip):
        return (z, index_of(flip))

    above, below = (z + 1, me), (z - 1, me)
    sends, receives, locals_ = {}, {}, {}

    def slot(sems, taken, key):
        return sems.at[taken.setdefault(key, len(taken))]

    def remote(src, dst, to, sent, received):
        return pltpu.make_async_remote_copy(
            src_ref=src,
            dst_ref=dst,
            send_sem=slot(send_sem, sends, sent),
            recv_sem=slot(recv_sem, receives, received),
            device_id=to,
            device_id_type=MESH,
        )

    def local(src, dst, key):
        return pltpu.make_async_copy(src, dst, slot(local_sem, locals_, key))

    def wait_sent(key, buffer):
        pltpu.make_async_copy(buffer, buffer, slot(send_sem, sends, key)).wait()

    def wait_received(key, buffer):
        pltpu.make_async_copy(buffer, buffer, slot(recv_sem, receives, key)).wait()

    def columns(flip, h):
        return pl.ds(pl.multiple_of(index_of(flip) * units + h * half, half), half)

    def halves(h):
        return pl.ds(h * half, half)

    barrier = pltpu.get_barrier_semaphore()
    for flip in (PARTNER, X, Y):
        pl.semaphore_signal(barrier, inc=1, device_id=device(flip), device_id_type=MESH)

    @pl.when(has_prev)
    def _():
        pl.semaphore_signal(barrier, inc=1, device_id=below, device_id_type=MESH)

    @pl.when(has_next)
    def _():
        pl.semaphore_signal(barrier, inc=1, device_id=above, device_id_type=MESH)


    b_in = local(b_ref, own_bias, "b")
    b_in.start()
    w_in = local(w_ref.at[0], w.at[:units], "w")
    w_in.start()
    x_in = local(x_ref.at[0], pull.at[:rows], "x")
    x_in.start()

    depth = lax.axis_size("depth")
    pl.semaphore_wait(barrier, 3 + (z + depth - 1) // depth + 1 - (z + 1) // depth)

    b_in.wait()
    bias[0] = jnp.broadcast_to(own_bias[...], (8, units))
    bias_swap = [
        remote(bias.at[0], bias.at[flip // 2], device(flip), "bias", ("bias", flip))
        for flip in (X, Y)
    ]
    for copy in bias_swap:
        copy.start()
    w_in.wait()
    for piece, h, to in ((1, 0, X), (1, 1, Y), (2, 1, X), (2, 0, Y)):
        dst = w.at[pl.ds(piece * units + h * half, half)]
        remote(w.at[halves(h)], dst, device(to), "own", ("own", piece)).start()
    x_swap = remote(x_ref.at[0], pull.at[rows:], device(PARTNER), "x", "x")
    x_swap.start()

    def start_targets(n):
        for h, flip in enumerate(OWNERS[n]):
            src = q_ref.at[0, :, columns(flip, h)]
            local(src, target.at[n, :rows, halves(h)], "target").start()
            src = q_ref.at[0, :, columns(flip ^ PARTNER, h)]
            dst = target.at[n, rows:, halves(h)]
            remote(src, dst, device(PARTNER), "target", ("target", n)).start()

    start_targets(0)
    staged = grad.at[:rows]
    q_in, u_in = local(q_ref.at[0], staged, "q"), local(u_ref.at[0], drive, "u")
    q_in.start()
    u_in.start()
    for n in (1, 2, 3):
        start_targets(n)

    def split(value):
        high = value.astype(jnp.bfloat16)
        return high, (value - high.astype(jnp.float32)).astype(jnp.bfloat16)

    def split_rows(src, start, high, low, to, count, cols=slice(None)):
        step = 16 if cols == slice(None) else max(16, 16 * width // (cols.stop - cols.start) // 2)

        @pl.loop(0, count // step)
        def _(i):
            offset = pl.multiple_of(i * step, step)
            high_part, low_part = split(src[pl.ds(start + offset, step), cols])
            high[pl.ds(to + offset, step), cols] = high_part
            low[pl.ds(to + offset, step), cols] = low_part

    def dot(a, b, contract):
        return lax.dot_general(a, b, (contract, ((), ())), preferred_element_type=jnp.float32)

    def dot3(a, b, contract):
        return (
            dot(a[0], b[0], contract) + dot(a[1], b[0], contract) + dot(a[0], b[1], contract)
        )

    def product_part(side, cols, first, last, n):
        owners = OWNERS[n]
        at = pl.ds(side * rows, rows)
        value = dot3(
            (x_high[at, cols], x_low[at, cols]), (w_high[:, cols], w_low[:, cols]), ((1,), (1,))
        )
        if first:
            shift = [bias[owners[h] // 2, 0:1, h * half : (h + 1) * half] for h in (0, 1)]
            value = scaling * value + jnp.concatenate(shift, axis=1)
        if not last:
            partial[at, :] = value - target[n, at, :]
            return
        m = value - target[n, at, :] if first else scaling * value + partial[at, :]
        m_high[at, :], m_low[at, :] = split(m)
        if first:
            keep_affine(side, value, m, n)
        else:
            partial[at, :] = m

    def keep_affine(side, value, m, n):
        if side == 0:
            for h, flip in enumerate(OWNERS[n]):
                affine[:, columns(flip, h)] = value[:, h * half : (h + 1) * half]
        else:
            target[n, rows:, :] = value
        sums = jnp.sum(m.reshape(rows // 8, 8, units), axis=0)
        osum[n] = sums if side == 1 else osum[n] + sums

    def product(n):
        split_rows(w, n * units, w_high, w_low, 0, units)
        for side in (1, 0):
            product_part(side, slice(None), True, True, n)

    def pull_tile(at, cols):
        a = (m_high[at, :], m_low[at, :])
        return dot3(a, (w_high[:, cols], w_low[:, cols]), ((1,), (0,)))

    def column_loop(body):
        @pl.loop(0, width // COLUMN_TILE)
        def _(c):
            body(pl.ds(pl.multiple_of(c * COLUMN_TILE, COLUMN_TILE), COLUMN_TILE))

    def pull_add(n):
        for side in (1, 0):
            at = pl.ds(side * rows, rows)

            def body(cols):
                value = pull_tile(at, cols)
                if n > 0:
                    value += pull[at, cols]
                elif side == 0:
                    value -= (keep_factor / pull_factor) * pull[at, cols]
                pull[at, cols] = value

            column_loop(body)

    def gradient(n):
        for part, turned in ((m_high, mt_high), (m_low, mt_low)):

            @pl.loop(0, 2 * rows // ROW_TILE)
            def _(i):
                at = pl.ds(pl.multiple_of(i * ROW_TILE, ROW_TILE), ROW_TILE)
                turned[:, at] = part[at, :].astype(jnp.float32).T.astype(jnp.bfloat16)

        def body(cols):
            b = (x_high[:, cols], x_low[:, cols])
            value = dot3((mt_high[...], mt_low[...]), b, ((1,), (0,)))
            if n == 0:
                own_grad[:, cols] = value
            else:
                grad[pl.ds((n - 1) * units, units), cols] = value

        column_loop(body)

    def send_affine(n):
        for h, flip in enumerate(OWNERS[n]):
            src = target.at[n, rows:, halves(h)]
            dst = affine.at[:, columns(flip, h)]
            remote(src, dst, device(PARTNER), "affine", "affine").start()

    def wait_targets(n):
        wait_received(("target", n), target.at[n, rows:])

    x_in.wait()
    split_rows(pull, 0, x_high, x_low, 0, rows)
    x_swap.wait_recv()
    split_rows(pull, rows, x_high, x_low, rows, rows)
    whole = target.at[:, :rows]
    local(whole, whole, "target").wait()
    wait_targets(0)
    product(0)
    q_in.wait()
    u_in.wait()

    @pl.loop(0, rows // 16)
    def _(i):
        offset = pl.multiple_of(i * 16, 16)
        at = pl.ds(offset, 16)
        drive[at, :] = drive[at, :] - penalty * grad[pl.ds(offset, 16), :]

    pull_add(0)
    drive_up = remote(drive, prev_in, above, "drive", "drive")

    @pl.when(has_next)
    def _():
        drive_up.start()

    send_affine(0)
    gradient(0)

    for copy in bias_swap:
        copy.wait_recv()
    bias_on = remote(bias.at[1], bias.at[3], device(Y), "bias", ("bias", DIAGONAL))
    bias_on.start()
    wait_received(("own", 1), w.at[units : 2 * units])
    cut = int(width * EARLY_PART) // 128 * 128
    parts = (slice(0, cut), slice(cut, width))
    for k, cols in enumerate(parts):
        for h, to in ((1, X), (0, Y)):
            src = w.at[pl.ds(units + h * half, half), cols]
            dst = w.at[pl.ds(3 * units + h * half, half), cols]
            remote(src, dst, device(to), "forward", ("forward", k)).start()
    wait_targets(1)
    product(1)
    gradient(1)
    pull_add(1)
    send_affine(1)
    for h, to in ((0, X), (1, Y)):
        src = grad.at[halves(h)]
        remote(src, direct_in.at[halves(h)], device(to), "direct", "direct").start()

    wait_received(("own", 2), w.at[2 * units : 3 * units])
    wait_targets(2)
    product(2)
    gradient(2)
    pull_add(2)
    send_affine(2)

    wait_targets(3)
    early, late = parts
    bias_on.wait_recv()
    wait_received(("forward", 0), w.at[3 * units :, early])
    split_rows(w, 3 * units, w_high, w_low, 0, units, early)
    for side in (1, 0):
        product_part(side, early, True, False, 3)

    blocks = pull_blocks(width)
    pull_swap, step_down = [], []
    for i, cols in enumerate(blocks):
        ends = pull.at[rows:, cols], pull_in.at[:, cols]
        pull_swap.append(remote(*ends, device(PARTNER), "pull", ("pull", i)))
        ends = pull.at[:rows, cols], next_in.at[:, cols]
        step_down.append(remote(*ends, below, "step", ("step", i)))

    def pull_last(side, i):
        if i < len(blocks):
            at = pl.ds(side * rows, rows)
            pull[at, blocks[i]] = pull[at, blocks[i]] + pull_tile(at, blocks[i])

    def swap(i):
        if i < len(blocks):
            pull_swap[i].start()

    def pull_done(i):
        cols = blocks[i]
        pull_swap[i].wait_recv()
        pull[:rows, cols] = -pull_factor * (pull[:rows, cols] + pull_in[:, cols])

    def send_down(i):
        @pl.when(has_prev)
        def _():
            step_down[i].start()

    wait_received(("forward", 1), w.at[3 * units :, late])
    split_rows(w, 3 * units, w_high, w_low, 0, units, late)
    product_part(1, late, False, True, 3)
    pull_last(1, 0)
    swap(0)
    product_part(0, late, False, True, 3)
    pull_last(0, 0)
    pull_last(1, 1)
    pull_done(0)
    swap(1)
    send_down(0)
    pull_last(1, 2)
    for i in range(1, len(blocks)):
        pull_last(0, i)
        swap(i + 1)
        pull_done(i)
        pull_last(1, i + 2)
        send_down(i)
    for side in (1, 0):
        m = partial[pl.ds(side * rows, rows), :]
        keep_affine(side, m + target[3, pl.ds(side * rows, rows), :], m, 3)
    send_affine(3)
    gradient(3)
    link_rows = half // LINK_CHUNKS
    merged = {}

    def link_part(h, c):
        return pl.ds(h * half + c * link_rows, link_rows)

    for c in range(LINK_CHUNKS):
        for h, to in ((0, X), (1, Y)):
            at = link_part(h, c)
            src = grad.at[pl.ds(2 * units + h * half + c * link_rows, link_rows)]
            remote(src, relay_in.at[at], device(to), "relay", ("relay", c)).start()
    for c in range(LINK_CHUNKS):
        for h, to in ((1, X), (0, Y)):
            src = grad.at[pl.ds(units + h * half + c * link_rows, link_rows)]
            dst = merged_in.at[link_part(h, c)]
            merged[h, c] = remote(src, dst, device(to), "merged", ("merged", c))

    for k, (low, high) in enumerate(((1, 2), (2, 1), (3, 3))):
        osend[k, :, :half] = osum[low, :, :half]
        osend[k, :, half:] = osum[high, :, half:]
    sums = [
        remote(osend.at[k], orecv.at[k], device(flip), "sums", ("sums", k))
        for k, flip in enumerate((X, Y, X))
    ]


    @pl.when(has_prev)
    def _():
        drive_up.wait_recv()

        @pl.loop(0, rows // 16)
        def _(i):
            at = pl.ds(pl.multiple_of(i * 16, 16), 16)
            prev_in[at, :] = pull[at, :] - step_input * prev_in[at, :]

    p_copy = local(x_ref.at[0], prev_in, "x")

    @pl.when(jnp.logical_not(has_prev))
    def _():
        p_copy.start()
        p_copy.wait()

    sums[0].start()
    sums[2].start()
    wait_sent("pull", pull.at[rows:])
    u_late = local(u_ref.at[0], pull.at[rows:], "u")
    u_late.start()

    @pl.when(has_next)
    def _():
        drive_up.wait_send()

    wait_received("affine", affine.at[:, : width // 2])
    u_late.wait()

    def finish_block(i):
        cols = blocks[i]

        @pl.when(has_next)
        def _():
            step_down[i].wait_recv()

            @pl.loop(0, rows // 32)
            def _(j):
                offset = pl.multiple_of(j * 32, 32)
                at = pl.ds(offset, 32)
                mults = pull[pl.ds(rows + offset, 32), cols]
                following = next_in[at, cols] - step_input * drive[at, cols]
                total = fit_weight * affine[at, cols] + penalty * following + mults
                fresh = jnp.maximum(0.0, total / (fit_weight + penalty))
                affine[at, cols] = fresh
                drive[at, cols] = mults + penalty * (following - fresh)

        @pl.when(jnp.logical_not(has_next))
        def _():
            @pl.loop(0, rows // 32)
            def _(j):
                offset = pl.multiple_of(j * 32, 32)
                at = pl.ds(offset, 32)
                affine[at, cols] = jnp.maximum(0.0, affine[at, cols])
                drive[at, cols] = pull[pl.ds(rows + offset, 32), cols]

    def merge(c):
        wait_received(("relay", c), relay_in.at[: 2 * link_rows])
        for h in (1, 0):
            start = units + h * half + c * link_rows
            at = pl.ds(start, link_rows)
            grad[at, :] = grad[at, :] + relay_in[link_part(h, c), :]
        for h in (1, 0):
            merged[h, c].start()

    def finish_weights(c):
        wait_received(("merged", c), merged_in.at[: 2 * link_rows])
        for h in (0, 1):
            at = link_part(h, c)
            total = own_grad[at, :] + direct_in[at, :] + merged_in[at, :]
            own_grad[at, :] = w[at, :] - (step_weight * fit_weight * scaling) * total

    def merge_offsets(_):
        wait_received("direct", direct_in)
        sums[2].wait_recv()
        osend[1] = osend[1] + orecv[2]
        sums[1].start()

    def finish_offsets(_):
        sums[0].wait_recv()
        sums[1].wait_recv()
        total = osum[0] + orecv[0] + orecv[1]
        total = jnp.sum(total, axis=0, keepdims=True)
        b_new[...] = own_bias[...] - (step_offset * fit_weight) * total

    ready, stage = [], width / 3
    for i, cols in enumerate(blocks):
        ready.append((cols.stop / stage + 0.2, finish_block, i))
    for c in range(LINK_CHUNKS):
        ready.append((1 + (c + 1) / LINK_CHUNKS, merge, c))
        ready.append((2 + (c + 1) / LINK_CHUNKS, finish_weights, c))
    ready.append((2.1, merge_offsets, 0))
    ready.append((2.6, finish_offsets, 0))
    def settle(_):
        wait_sent("own", w.at[: 2 * units])
        wait_sent("forward", w.at[:units])
        wait_sent("x", pull.at[:rows])
        wait_sent("target", target.at[:, :rows])
        wait_sent("affine", target.at[:, :rows])
        wait_sent("bias", bias.at[1:])
        wait_sent("direct", direct_in)
        wait_sent("relay", relay_in)
        wait_sent("sums", orecv)

    ready.append((blocks[-1].start / stage - 0.1, settle, 0))
    for _, work, i in sorted(ready, key=lambda entry: entry[0]):
        work(i)
    wait_sent("merged", merged_in)

    @pl.when(has_prev)
    def _():
        wait_sent("step", pull.at[:rows])

    counts = len(sends), len(receives), len(locals_)
    if counts != semaphore_counts(width):
        raise ValueError(counts)


def write_kernel(*refs):
    values, outs, sems = refs[:5], refs[5:10], refs[10]
    copies = [pltpu.make_async_copy(*pair, sems.at[i]) for i, pair in enumerate(zip(values, outs))]
    for copy in copies:
        copy.start()
    for copy in copies:
        copy.wait()


def body_fused(layer_inputs, weights, offsets, layer_outputs, multipliers):
    _, rows, width = layer_inputs.shape
    units = weights.shape[1]
    shapes = fused_shapes(rows, width, units)
    samples = rows * lax.axis_size("dp")
    anywhere = pl.BlockSpec(memory_space=pl.ANY)
    vmem = pl.BlockSpec(memory_space=pltpu.VMEM)
    args = (layer_inputs, weights, offsets, layer_outputs, multipliers)
    results = pl.pallas_call(
        functools.partial(fused_kernel, tuple(shapes), samples),
        out_shape=tuple(pltpu.VMEM(a.shape, a.dtype) for a in args),
        in_specs=[anywhere] * 5,
        out_specs=[vmem] * 5,
        scratch_shapes=[pltpu.VMEM(shape, dtype) for shape, dtype in shapes.values()]
        + [pltpu.SemaphoreType.DMA((count,)) for count in semaphore_counts(width)],
        compiler_params=pltpu.CompilerParams(
            collective_id=0,
            has_side_effects=True,
            vmem_limit_bytes=fused_bytes(rows, width, units) + SPARE_BYTES,
        ),
        name="iteration",
    )(*args)
    return pl.pallas_call(
        write_kernel,
        out_shape=tuple(jax.ShapeDtypeStruct(a.shape, a.dtype) for a in args),
        in_specs=[vmem] * 5,
        out_specs=[anywhere] * 5,
        scratch_shapes=[pltpu.SemaphoreType.DMA((5,))],
        compiler_params=pltpu.CompilerParams(vmem_limit_bytes=SPARE_BYTES),
        name="write",
    )(*(pltpu.with_memory_space_constraint(r, pltpu.VMEM) for r in results))


def choose(mesh, layer_inputs, weights, *rest):
    if mesh.shape["dp"] != 8:
        return body_general(layer_inputs, weights, *rest)
    rows, width, units = layer_inputs.shape[1], layer_inputs.shape[2], weights.shape[1]
    tiles = rows % ROW_TILE, width % COLUMN_TILE, units % 256
    held = 4 * (3 * rows + units) * width
    total = fused_bytes(rows, width, units) + held + SPARE_BYTES
    if any(tiles) or total > VMEM_BYTES:
        return body_square(layer_inputs, weights, *rest)
    return body_fused(layer_inputs, weights, *rest)


def solution(mesh):
    specs = (
        P("depth", "dp", None),
        P("depth", "dp", None),
        P("depth", "dp"),
        P("depth", "dp", None),
        P("depth", "dp", None),
    )
    body = functools.partial(choose, mesh)
    return jax.shard_map(body, mesh=mesh, in_specs=specs, out_specs=specs, check_vma=False)
```

```python
import functools
import math

import jax
import jax.numpy as jnp
from jax import lax
from jax.experimental import pallas as pl
from jax.experimental.pallas import tpu as pltpu
from jax.sharding import PartitionSpec as P

fit_weight = 1.0
penalty = 1.0
step_input = 0.5
PRECISION = lax.Precision.HIGH


def passed_along(block, axis, distance):
    devices = range(lax.axis_size(axis))
    route = [(i - distance, i) for i in devices if i - distance in devices]
    return lax.ppermute(block, axis, route)


def swapped(block, bit):
    route = [(i, i ^ bit) for i in range(lax.axis_size("dp"))]
    return lax.ppermute(block, "dp", route)


def dot(a, b, dims):
    return lax.dot_general(a, b, (dims, ((), ())), precision=PRECISION)


def times_transposed(a, b):
    return dot(a, b, ((1,), (1,)))


def times(a, b):
    return dot(a, b, ((1,), (0,)))


def transposed_times(a, b):
    return dot(a, b, ((0,), (0,)))


def finish(inputs, outputs, mults, drive, prev_drive, affine, pulled_step, next_step):
    layer_index = lax.axis_index("depth")
    is_first = layer_index == 0
    is_last = layer_index == lax.axis_size("depth") - 1
    inputs_new = jnp.where(is_first, inputs, pulled_step - step_input * prev_drive)
    next_inputs = next_step - step_input * drive
    coupled = jnp.maximum(
        0.0, (fit_weight * affine + penalty * next_inputs + mults) / (fit_weight + penalty)
    )
    outputs_new = jnp.where(is_last, jnp.maximum(0.0, affine), coupled)
    mults_new = jnp.where(is_last, mults, mults + penalty * (next_inputs - outputs_new))
    return inputs_new, outputs_new, mults_new


def body_general(layer_inputs, weights, offsets, layer_outputs, multipliers):
    inputs, outputs, mults = layer_inputs[0], layer_outputs[0], multipliers[0]
    scaling = 1.0 / math.sqrt(inputs.shape[1])
    samples = inputs.shape[0] * lax.axis_size("dp")
    step_weight = 8.0 / math.sqrt(samples)
    step_offset = 0.5 / math.sqrt(samples)
    drive = mults - penalty * outputs
    prev_drive = passed_along(drive, "depth", 1)
    weight = lax.all_gather(weights[0], "dp", axis=0, tiled=True)
    offset = lax.all_gather(offsets, "dp", axis=1, tiled=True)
    affine = scaling * times_transposed(inputs, weight) + offset
    misfit = affine - outputs
    weight_grad = fit_weight * scaling * transposed_times(misfit, inputs)
    weight_sum = lax.psum_scatter(weight_grad, "dp", scatter_dimension=0, tiled=True)
    offset_sum = lax.psum_scatter(
        fit_weight * jnp.sum(misfit, axis=0), "dp", scatter_dimension=0, tiled=True
    )
    pulled = scaling * times(misfit, weight)
    pulled_step = inputs - step_input * (fit_weight * pulled + penalty * inputs)
    next_step = passed_along(pulled_step, "depth", -1)
    inputs_new, outputs_new, mults_new = finish(
        inputs, outputs, mults, drive, prev_drive, affine, pulled_step, next_step
    )
    weights_new = weights - step_weight * weight_sum[None]
    offsets_new = offsets - step_offset * offset_sum[None]
    return inputs_new[None], weights_new, offsets_new, outputs_new[None], mults_new[None]


def body_square(layer_inputs, weights, offsets, layer_outputs, multipliers):
    inputs, outputs, mults = layer_inputs[0], layer_outputs[0], multipliers[0]
    rows, width = inputs.shape
    units = weights.shape[1]
    half = units // 2
    scaling = 1.0 / math.sqrt(width)
    samples = rows * lax.axis_size("dp")
    step_weight = 8.0 / math.sqrt(samples)
    step_offset = 0.5 / math.sqrt(samples)
    me = lax.axis_index("dp")

    w_own = weights[0]
    low_own, high_own = w_own[:half], w_own[half:]
    low_own, high_own, inputs = lax.optimization_barrier((low_own, high_own, inputs))
    low_x, high_y = swapped(low_own, 2), swapped(high_own, 4)
    inputs_other = swapped(inputs, 1)
    inputs_other, outputs_late = lax.optimization_barrier((inputs_other, outputs))
    drive = mults - penalty * outputs
    prev_drive = passed_along(drive, "depth", 1)
    b_own = offsets
    b_x, b_y, b_d = swapped(b_own, 2), swapped(b_own, 4), swapped(b_own, 6)

    def columns(array, index):
        return lax.dynamic_slice(array, (0, index * units), (rows, units))

    def arranged(own, x, y, d):
        joined_a = jnp.concatenate([x[:, :half], y[:, half:]], axis=1)
        joined_b = jnp.concatenate([x[:, half:], y[:, :half]], axis=1)
        return own, joined_a, d, joined_b

    flips = (0, 2, 4, 6)
    out_mine = arranged(*[columns(outputs_late, me ^ f) for f in flips])
    out_sent = arranged(*[columns(outputs_late, me ^ f ^ 1) for f in flips])
    out_other = swapped(jnp.concatenate(out_sent, axis=1), 1)
    biases = arranged(b_own, b_x, b_y, b_d)
    both = jnp.concatenate([inputs, inputs_other], axis=0)

    def layer(n, w):
        affine = scaling * times_transposed(both, w) + biases[n]
        target = jnp.concatenate([out_mine[n], out_other[:, n * units : (n + 1) * units]], axis=0)
        return affine, affine - target

    affine_own, m = layer(0, w_own)
    g_own = transposed_times(m, both)
    o_own = jnp.sum(m, axis=0, keepdims=True)
    pulled = times(m, w_own)
    low_x, high_y, g_own, pulled, o_own = lax.optimization_barrier(
        (low_x, high_y, g_own, pulled, o_own)
    )

    low_d, high_d = swapped(low_x, 4), swapped(high_y, 2)
    w_a = jnp.concatenate([low_x, high_y], axis=0)
    affine_a, m = layer(1, w_a)
    g_a = transposed_times(m, both)
    o_a = jnp.sum(m, axis=0, keepdims=True)
    pulled = pulled + times(m, w_a)
    low_d, high_d, g_a, pulled, o_a, low_own, high_own = lax.optimization_barrier(
        (low_d, high_d, g_a, pulled, o_a, low_own, high_own)
    )

    high_x, low_y = swapped(high_own, 2), swapped(low_own, 4)
    w_d = jnp.concatenate([low_d, high_d], axis=0)
    affine_d, m = layer(2, w_d)
    g_d = transposed_times(m, both)
    o_d = jnp.sum(m, axis=0, keepdims=True)
    pulled = pulled + times(m, w_d)
    high_x, low_y, g_a, g_d, pulled, o_d, prev_drive = lax.optimization_barrier(
        (high_x, low_y, g_a, g_d, pulled, o_d, prev_drive)
    )

    x_low, y_high = swapped(g_a[:half], 2), swapped(g_a[half:], 4)
    from_x, from_y = swapped(g_d[:half], 2), swapped(g_d[half:], 4)
    w_b = jnp.concatenate([high_x, low_y], axis=0)
    affine_b, m = layer(3, w_b)
    pulled_other = swapped(pulled[rows:] + times(m[rows:], w_b), 1)
    pulled_mine = pulled[:rows] + times(m[:rows], w_b)
    pulled_all = scaling * (pulled_mine + pulled_other)
    pulled_step = inputs - step_input * (fit_weight * pulled_all + penalty * inputs)
    m, pulled_step = lax.optimization_barrier((m, pulled_step))
    next_step = passed_along(pulled_step, "depth", -1)
    g_b = transposed_times(m, both)
    o_b = jnp.sum(m, axis=0, keepdims=True)

    x_high = swapped(g_b[:half] + from_y, 2)
    y_low = swapped(g_b[half:] + from_x, 4)
    sum_low = g_own[:half] + x_low + y_low
    sum_high = g_own[half:] + x_high + y_high
    weight_step = step_weight * fit_weight * scaling
    weights_new = w_own - weight_step * jnp.concatenate([sum_low, sum_high], axis=0)
    o_x = jnp.concatenate([o_a[:, :half], o_b[:, :half]], axis=1)
    o_y = jnp.concatenate([o_b[:, half:], o_a[:, half:]], axis=1)
    offset_sum = o_own + swapped(o_x, 2) + swapped(o_y, 4) + swapped(o_d, 6)
    offsets_new = offsets - step_offset * fit_weight * offset_sum

    affines = (affine_own, affine_a, affine_d, affine_b)
    affine_other = swapped(jnp.concatenate([a[rows:] for a in affines], axis=1), 1)

    def by_owner(own, a, d, b):
        x = jnp.concatenate([a[:, :half], b[:, :half]], axis=1)
        y = jnp.concatenate([b[:, half:], a[:, half:]], axis=1)
        return own, x, y, d

    mine = by_owner(*[a[:rows] for a in affines])
    other = by_owner(*[affine_other[:, n * units : (n + 1) * units] for n in range(len(flips))])
    affine = jnp.zeros_like(outputs)
    for n, f in enumerate(flips):
        affine = lax.dynamic_update_slice(affine, mine[n], (0, (me ^ f) * units))
        affine = lax.dynamic_update_slice(affine, other[n], (0, (me ^ f ^ 1) * units))
    inputs_new, outputs_new, mults_new = finish(
        inputs, outputs, mults, drive, prev_drive, affine, pulled_step, next_step
    )
    return (
        inputs_new[None],
        weights_new[None],
        offsets_new,
        outputs_new[None],
        mults_new[None],
    )


MESH = pl.DeviceIdType.MESH
VMEM_BYTES = 67043328
SPARE_BYTES = 2**22
OWNERS = ((0, 0), (2, 4), (4, 2), (6, 6))
X, Y, DIAGONAL, PARTNER = 2, 4, 6, 1
ROW_TILE = 128
COLUMN_TILE = 256
LINK_CHUNKS = 4
EARLY_PART = 0.875


def fused_shapes(rows, width, units):
    f32, bf16 = jnp.float32, jnp.bfloat16
    return dict(
        pull=((2 * rows, width), f32),
        x_high=((2 * rows, width), bf16),
        x_low=((2 * rows, width), bf16),
        w=((4 * units, width), f32),
        w_high=((units, width), bf16),
        w_low=((units, width), bf16),
        target=((4, 2 * rows, units), f32),
        m_high=((2 * rows, units), bf16),
        m_low=((2 * rows, units), bf16),
        mt_high=((units, 2 * rows), bf16),
        mt_low=((units, 2 * rows), bf16),
        product=((2 * rows, units), f32),
        pull_in=((rows, width), f32),
        grad=((3 * units, width), f32),
        direct_in=((units, width), f32),
        relay_in=((units, width), f32),
        merged_in=((units, width), f32),
        next_in=((rows, width), f32),
        bias=((4, 8, units), f32),
        own_bias=((1, units), f32),
        osum=((4, 8, units), f32),
        osend=((3, 8, units), f32),
        orecv=((3, 8, units), f32),
    )


def fused_bytes(rows, width, units):
    shapes = fused_shapes(rows, width, units).values()
    return sum(math.prod(shape) * jnp.dtype(dtype).itemsize for shape, dtype in shapes)


def pull_blocks(width):
    narrow = COLUMN_TILE // 2
    widths = [COLUMN_TILE] * (width // COLUMN_TILE - 1) + [narrow] * 2
    return [slice(sum(widths[:i]), sum(widths[: i + 1])) for i in range(len(widths))]


def semaphore_counts(width):
    return 13, 18 + 2 * LINK_CHUNKS + 2 * len(pull_blocks(width)), 6


def fused_kernel(
    names, samples, x_ref, w_ref, b_ref, q_ref, u_ref, p_new, w_new, b_new, q_new, u_new, *scratch
):
    ref = dict(zip(names, scratch))
    send_sem, recv_sem, local_sem = scratch[len(names) :]
    pull, x_high, x_low, w = ref["pull"], ref["x_high"], ref["x_low"], ref["w"]
    w_high, w_low, target = ref["w_high"], ref["w_low"], ref["target"]
    m_high, m_low, mt_high, mt_low = ref["m_high"], ref["m_low"], ref["mt_high"], ref["mt_low"]
    pull_in, grad, partial = ref["pull_in"], ref["grad"], ref["product"]
    direct_in, relay_in, merged_in = ref["direct_in"], ref["relay_in"], ref["merged_in"]
    next_in = ref["next_in"]
    prev_in, own_grad, affine, drive = p_new.at[0], w_new.at[0], q_new.at[0], u_new.at[0]
    bias, osum, osend, orecv = ref["bias"], ref["osum"], ref["osend"], ref["orecv"]
    own_bias = ref["own_bias"]

    rows, width = affine.shape
    units = w_high.shape[0]
    half = units // 2
    scaling = 1.0 / math.sqrt(width)
    step_weight = 8.0 / math.sqrt(samples)
    step_offset = 0.5 / math.sqrt(samples)
    pull_factor = step_input * fit_weight * scaling
    keep_factor = 1.0 - step_input * penalty

    me, z = lax.axis_index("dp"), lax.axis_index("depth")
    has_prev, has_next = z > 0, z < lax.axis_size("depth") - 1
    bits = (me % 2, (me // 2) % 2, me // 4)

    def index_of(flip):
        return sum(((1 - b) if flip >> i & 1 else b) * 2**i for i, b in enumerate(bits))

    def device(flip):
        return (z, index_of(flip))

    above, below = (z + 1, me), (z - 1, me)
    sends, receives, locals_ = {}, {}, {}

    def slot(sems, taken, key):
        return sems.at[taken.setdefault(key, len(taken))]

    def remote(src, dst, to, sent, received):
        return pltpu.make_async_remote_copy(
            src_ref=src,
            dst_ref=dst,
            send_sem=slot(send_sem, sends, sent),
            recv_sem=slot(recv_sem, receives, received),
            device_id=to,
            device_id_type=MESH,
        )

    def local(src, dst, key):
        return pltpu.make_async_copy(src, dst, slot(local_sem, locals_, key))

    def wait_sent(key, buffer):
        pltpu.make_async_copy(buffer, buffer, slot(send_sem, sends, key)).wait()

    def wait_received(key, buffer):
        pltpu.make_async_copy(buffer, buffer, slot(recv_sem, receives, key)).wait()

    def columns(flip, h):
        return pl.ds(pl.multiple_of(index_of(flip) * units + h * half, half), half)

    def halves(h):
        return pl.ds(h * half, half)

    barrier = pltpu.get_barrier_semaphore()
    for flip in (PARTNER, X, Y):
        pl.semaphore_signal(barrier, inc=1, device_id=device(flip), device_id_type=MESH)

    @pl.when(has_prev)
    def _():
        pl.semaphore_signal(barrier, inc=1, device_id=below, device_id_type=MESH)

    @pl.when(has_next)
    def _():
        pl.semaphore_signal(barrier, inc=1, device_id=above, device_id_type=MESH)


    b_in = local(b_ref, own_bias, "b")
    b_in.start()
    w_in = local(w_ref.at[0], w.at[:units], "w")
    w_in.start()
    x_in = local(x_ref.at[0], pull.at[:rows], "x")
    x_in.start()

    depth = lax.axis_size("depth")
    pl.semaphore_wait(barrier, 3 + (z + depth - 1) // depth + 1 - (z + 1) // depth)

    b_in.wait()
    bias[0] = jnp.broadcast_to(own_bias[...], (8, units))
    bias_swap = [
        remote(bias.at[0], bias.at[flip // 2], device(flip), "bias", ("bias", flip))
        for flip in (X, Y)
    ]
    for copy in bias_swap:
        copy.start()
    w_in.wait()
    for piece, h, to in ((1, 0, X), (1, 1, Y), (2, 1, X), (2, 0, Y)):
        dst = w.at[pl.ds(piece * units + h * half, half)]
        remote(w.at[halves(h)], dst, device(to), "own", ("own", piece)).start()
    x_swap = remote(x_ref.at[0], pull.at[rows:], device(PARTNER), "x", "x")
    x_swap.start()

    def start_targets(n):
        for h, flip in enumerate(OWNERS[n]):
            src = q_ref.at[0, :, columns(flip, h)]
            local(src, target.at[n, :rows, halves(h)], "target").start()
            src = q_ref.at[0, :, columns(flip ^ PARTNER, h)]
            dst = target.at[n, rows:, halves(h)]
            remote(src, dst, device(PARTNER), "target", ("target", n)).start()

    start_targets(0)
    staged = grad.at[:rows]
    q_in, u_in = local(q_ref.at[0], staged, "q"), local(u_ref.at[0], drive, "u")
    q_in.start()
    u_in.start()
    for n in (1, 2, 3):
        start_targets(n)

    def split(value):
        high = value.astype(jnp.bfloat16)
        return high, (value - high.astype(jnp.float32)).astype(jnp.bfloat16)

    def split_rows(src, start, high, low, to, count, cols=slice(None)):
        step = 16 if cols == slice(None) else max(16, 16 * width // (cols.stop - cols.start) // 2)

        @pl.loop(0, count // step)
        def _(i):
            offset = pl.multiple_of(i * step, step)
            high_part, low_part = split(src[pl.ds(start + offset, step), cols])
            high[pl.ds(to + offset, step), cols] = high_part
            low[pl.ds(to + offset, step), cols] = low_part

    def dot(a, b, contract):
        return lax.dot_general(a, b, (contract, ((), ())), preferred_element_type=jnp.float32)

    def dot3(a, b, contract):
        return (
            dot(a[0], b[0], contract) + dot(a[1], b[0], contract) + dot(a[0], b[1], contract)
        )

    def product_part(side, cols, first, last, n):
        owners = OWNERS[n]
        at = pl.ds(side * rows, rows)
        value = dot3(
            (x_high[at, cols], x_low[at, cols]), (w_high[:, cols], w_low[:, cols]), ((1,), (1,))
        )
        if first:
            shift = [bias[owners[h] // 2, 0:1, h * half : (h + 1) * half] for h in (0, 1)]
            value = scaling * value + jnp.concatenate(shift, axis=1)
        if not last:
            partial[at, :] = value - target[n, at, :]
            return
        m = value - target[n, at, :] if first else scaling * value + partial[at, :]
        m_high[at, :], m_low[at, :] = split(m)
        if first:
            keep_affine(side, value, m, n)
        else:
            partial[at, :] = m

    def keep_affine(side, value, m, n):
        if side == 0:
            for h, flip in enumerate(OWNERS[n]):
                affine[:, columns(flip, h)] = value[:, h * half : (h + 1) * half]
        else:
            target[n, rows:, :] = value
        sums = jnp.sum(m.reshape(rows // 8, 8, units), axis=0)
        osum[n] = sums if side == 1 else osum[n] + sums

    def product(n):
        split_rows(w, n * units, w_high, w_low, 0, units)
        for side in (1, 0):
            product_part(side, slice(None), True, True, n)

    def pull_tile(at, cols):
        a = (m_high[at, :], m_low[at, :])
        return dot3(a, (w_high[:, cols], w_low[:, cols]), ((1,), (0,)))

    def column_loop(body):
        @pl.loop(0, width // COLUMN_TILE)
        def _(c):
            body(pl.ds(pl.multiple_of(c * COLUMN_TILE, COLUMN_TILE), COLUMN_TILE))

    def pull_add(n):
        for side in (1, 0):
            at = pl.ds(side * rows, rows)

            def body(cols):
                value = pull_tile(at, cols)
                if n > 0:
                    value += pull[at, cols]
                elif side == 0:
                    value -= (keep_factor / pull_factor) * pull[at, cols]
                pull[at, cols] = value

            column_loop(body)

    def gradient(n):
        for part, turned in ((m_high, mt_high), (m_low, mt_low)):

            @pl.loop(0, 2 * rows // ROW_TILE)
            def _(i):
                at = pl.ds(pl.multiple_of(i * ROW_TILE, ROW_TILE), ROW_TILE)
                turned[:, at] = part[at, :].astype(jnp.float32).T.astype(jnp.bfloat16)

        def body(cols):
            b = (x_high[:, cols], x_low[:, cols])
            value = dot3((mt_high[...], mt_low[...]), b, ((1,), (0,)))
            if n == 0:
                own_grad[:, cols] = value
            else:
                grad[pl.ds((n - 1) * units, units), cols] = value

        column_loop(body)

    def send_affine(n):
        for h, flip in enumerate(OWNERS[n]):
            src = target.at[n, rows:, halves(h)]
            dst = affine.at[:, columns(flip, h)]
            remote(src, dst, device(PARTNER), "affine", "affine").start()

    def wait_targets(n):
        wait_received(("target", n), target.at[n, rows:])

    x_in.wait()
    split_rows(pull, 0, x_high, x_low, 0, rows)
    x_swap.wait_recv()
    split_rows(pull, rows, x_high, x_low, rows, rows)
    whole = target.at[:, :rows]
    local(whole, whole, "target").wait()
    wait_targets(0)
    product(0)
    q_in.wait()
    u_in.wait()

    @pl.loop(0, rows // 16)
    def _(i):
        offset = pl.multiple_of(i * 16, 16)
        at = pl.ds(offset, 16)
        drive[at, :] = drive[at, :] - penalty * grad[pl.ds(offset, 16), :]

    pull_add(0)
    drive_up = remote(drive, prev_in, above, "drive", "drive")

    @pl.when(has_next)
    def _():
        drive_up.start()

    send_affine(0)
    gradient(0)

    for copy in bias_swap:
        copy.wait_recv()
    bias_on = remote(bias.at[1], bias.at[3], device(Y), "bias", ("bias", DIAGONAL))
    bias_on.start()
    wait_received(("own", 1), w.at[units : 2 * units])
    cut = int(width * EARLY_PART) // 128 * 128
    parts = (slice(0, cut), slice(cut, width))
    for k, cols in enumerate(parts):
        for h, to in ((1, X), (0, Y)):
            src = w.at[pl.ds(units + h * half, half), cols]
            dst = w.at[pl.ds(3 * units + h * half, half), cols]
            remote(src, dst, device(to), "forward", ("forward", k)).start()
    wait_targets(1)
    product(1)
    gradient(1)
    pull_add(1)
    send_affine(1)
    for h, to in ((0, X), (1, Y)):
        src = grad.at[halves(h)]
        remote(src, direct_in.at[halves(h)], device(to), "direct", "direct").start()

    wait_received(("own", 2), w.at[2 * units : 3 * units])
    wait_targets(2)
    product(2)
    gradient(2)
    pull_add(2)
    send_affine(2)

    wait_targets(3)
    early, late = parts
    bias_on.wait_recv()
    wait_received(("forward", 0), w.at[3 * units :, early])
    split_rows(w, 3 * units, w_high, w_low, 0, units, early)
    for side in (1, 0):
        product_part(side, early, True, False, 3)

    blocks = pull_blocks(width)
    pull_swap, step_down = [], []
    for i, cols in enumerate(blocks):
        ends = pull.at[rows:, cols], pull_in.at[:, cols]
        pull_swap.append(remote(*ends, device(PARTNER), "pull", ("pull", i)))
        ends = pull.at[:rows, cols], next_in.at[:, cols]
        step_down.append(remote(*ends, below, "step", ("step", i)))

    def pull_last(side, i):
        if i < len(blocks):
            at = pl.ds(side * rows, rows)
            pull[at, blocks[i]] = pull[at, blocks[i]] + pull_tile(at, blocks[i])

    def swap(i):
        if i < len(blocks):
            pull_swap[i].start()

    def pull_done(i):
        cols = blocks[i]
        pull_swap[i].wait_recv()
        pull[:rows, cols] = -pull_factor * (pull[:rows, cols] + pull_in[:, cols])

    def send_down(i):
        @pl.when(has_prev)
        def _():
            step_down[i].start()

    wait_received(("forward", 1), w.at[3 * units :, late])
    split_rows(w, 3 * units, w_high, w_low, 0, units, late)
    @pl.when(bits[0] == 0)
    def _():
        product_part(0, late, False, True, 3)
        pull_last(0, 0)
        pull_done(0)
        send_down(0)
        product_part(1, late, False, True, 3)
        pull_last(1, 0)
        swap(0)
        pull_last(0, 1)
        pull_last(1, 1)
        swap(1)
        pull_done(1)
        send_down(1)

    @pl.when(bits[0] == 1)
    def _():
        product_part(1, late, False, True, 3)
        pull_last(1, 0)
        swap(0)
        product_part(0, late, False, True, 3)
        pull_last(1, 1)
        pull_last(0, 0)
        swap(1)
        pull_last(0, 1)
        pull_done(0)
        send_down(0)
        pull_done(1)
        send_down(1)

    pull_last(1, 2)
    swap(2)
    for i in range(2, len(blocks)):
        pull_last(1, i + 1)
        pull_last(0, i)
        swap(i + 1)
        pull_done(i)
        send_down(i)
    for side in (1, 0):
        m = partial[pl.ds(side * rows, rows), :]
        keep_affine(side, m + target[3, pl.ds(side * rows, rows), :], m, 3)
    send_affine(3)
    gradient(3)
    link_rows = half // LINK_CHUNKS
    merged = {}

    def link_part(h, c):
        return pl.ds(h * half + c * link_rows, link_rows)

    for c in range(LINK_CHUNKS):
        for h, to in ((0, X), (1, Y)):
            at = link_part(h, c)
            src = grad.at[pl.ds(2 * units + h * half + c * link_rows, link_rows)]
            remote(src, relay_in.at[at], device(to), "relay", ("relay", c)).start()
    for c in range(LINK_CHUNKS):
        for h, to in ((1, X), (0, Y)):
            src = grad.at[pl.ds(units + h * half + c * link_rows, link_rows)]
            dst = merged_in.at[link_part(h, c)]
            merged[h, c] = remote(src, dst, device(to), "merged", ("merged", c))

    for k, (low, high) in enumerate(((1, 2), (2, 1), (3, 3))):
        osend[k, :, :half] = osum[low, :, :half]
        osend[k, :, half:] = osum[high, :, half:]
    sums = [
        remote(osend.at[k], orecv.at[k], device(flip), "sums", ("sums", k))
        for k, flip in enumerate((X, Y, X))
    ]


    @pl.when(has_prev)
    def _():
        drive_up.wait_recv()

        @pl.loop(0, rows // 16)
        def _(i):
            at = pl.ds(pl.multiple_of(i * 16, 16), 16)
            prev_in[at, :] = pull[at, :] - step_input * prev_in[at, :]

    p_copy = local(x_ref.at[0], prev_in, "x")

    @pl.when(jnp.logical_not(has_prev))
    def _():
        p_copy.start()
        p_copy.wait()

    sums[0].start()
    sums[2].start()
    wait_sent("pull", pull.at[rows:])
    u_late = local(u_ref.at[0], pull.at[rows:], "u")
    u_late.start()

    @pl.when(has_next)
    def _():
        drive_up.wait_send()

    wait_received("affine", affine.at[:, : width // 2])
    u_late.wait()

    def finish_block(i):
        cols = blocks[i]

        @pl.when(has_next)
        def _():
            step_down[i].wait_recv()

            @pl.loop(0, rows // 32)
            def _(j):
                offset = pl.multiple_of(j * 32, 32)
                at = pl.ds(offset, 32)
                mults = pull[pl.ds(rows + offset, 32), cols]
                following = next_in[at, cols] - step_input * drive[at, cols]
                total = fit_weight * affine[at, cols] + penalty * following + mults
                fresh = jnp.maximum(0.0, total / (fit_weight + penalty))
                affine[at, cols] = fresh
                drive[at, cols] = mults + penalty * (following - fresh)

        @pl.when(jnp.logical_not(has_next))
        def _():
            @pl.loop(0, rows // 32)
            def _(j):
                offset = pl.multiple_of(j * 32, 32)
                at = pl.ds(offset, 32)
                affine[at, cols] = jnp.maximum(0.0, affine[at, cols])
                drive[at, cols] = pull[pl.ds(rows + offset, 32), cols]

    def merge(c):
        wait_received(("relay", c), relay_in.at[: 2 * link_rows])
        for h in (1, 0):
            start = units + h * half + c * link_rows
            at = pl.ds(start, link_rows)
            grad[at, :] = grad[at, :] + relay_in[link_part(h, c), :]
        for h in (1, 0):
            merged[h, c].start()

    def finish_weights(c):
        wait_received(("merged", c), merged_in.at[: 2 * link_rows])
        for h in (0, 1):
            at = link_part(h, c)
            total = own_grad[at, :] + direct_in[at, :] + merged_in[at, :]
            own_grad[at, :] = w[at, :] - (step_weight * fit_weight * scaling) * total

    def merge_offsets(_):
        wait_received("direct", direct_in)
        sums[2].wait_recv()
        osend[1] = osend[1] + orecv[2]
        sums[1].start()

    def finish_offsets(_):
        sums[0].wait_recv()
        sums[1].wait_recv()
        total = osum[0] + orecv[0] + orecv[1]
        total = jnp.sum(total, axis=0, keepdims=True)
        b_new[...] = own_bias[...] - (step_offset * fit_weight) * total

    ready, stage = [], width / 3
    for i, cols in enumerate(blocks):
        ready.append((cols.stop / stage + 0.2, finish_block, i))
    for c in range(LINK_CHUNKS):
        ready.append((1 + (c + 1) / LINK_CHUNKS, merge, c))
        ready.append((2 + (c + 1) / LINK_CHUNKS, finish_weights, c))
    ready.append((2.1, merge_offsets, 0))
    ready.append((2.6, finish_offsets, 0))
    def settle(_):
        wait_sent("own", w.at[: 2 * units])
        wait_sent("forward", w.at[:units])
        wait_sent("x", pull.at[:rows])
        wait_sent("target", target.at[:, :rows])
        wait_sent("affine", target.at[:, :rows])
        wait_sent("bias", bias.at[1:])
        wait_sent("direct", direct_in)
        wait_sent("relay", relay_in)
        wait_sent("sums", orecv)

    ready.append((blocks[-1].start / stage - 0.1, settle, 0))
    for _, work, i in sorted(ready, key=lambda entry: entry[0]):
        work(i)
    wait_sent("merged", merged_in)

    @pl.when(has_prev)
    def _():
        wait_sent("step", pull.at[:rows])

    counts = len(sends), len(receives), len(locals_)
    if counts != semaphore_counts(width):
        raise ValueError(counts)


def write_kernel(*refs):
    values, outs, sems = refs[:5], refs[5:10], refs[10]
    copies = [pltpu.make_async_copy(*pair, sems.at[i]) for i, pair in enumerate(zip(values, outs))]
    for copy in copies:
        copy.start()
    for copy in copies:
        copy.wait()


def body_fused(layer_inputs, weights, offsets, layer_outputs, multipliers):
    _, rows, width = layer_inputs.shape
    units = weights.shape[1]
    shapes = fused_shapes(rows, width, units)
    samples = rows * lax.axis_size("dp")
    anywhere = pl.BlockSpec(memory_space=pl.ANY)
    vmem = pl.BlockSpec(memory_space=pltpu.VMEM)
    args = (layer_inputs, weights, offsets, layer_outputs, multipliers)
    results = pl.pallas_call(
        functools.partial(fused_kernel, tuple(shapes), samples),
        out_shape=tuple(pltpu.VMEM(a.shape, a.dtype) for a in args),
        in_specs=[anywhere] * 5,
        out_specs=[vmem] * 5,
        scratch_shapes=[pltpu.VMEM(shape, dtype) for shape, dtype in shapes.values()]
        + [pltpu.SemaphoreType.DMA((count,)) for count in semaphore_counts(width)],
        compiler_params=pltpu.CompilerParams(
            collective_id=0,
            has_side_effects=True,
            vmem_limit_bytes=fused_bytes(rows, width, units) + SPARE_BYTES,
        ),
        name="iteration",
    )(*args)
    return pl.pallas_call(
        write_kernel,
        out_shape=tuple(jax.ShapeDtypeStruct(a.shape, a.dtype) for a in args),
        in_specs=[vmem] * 5,
        out_specs=[anywhere] * 5,
        scratch_shapes=[pltpu.SemaphoreType.DMA((5,))],
        compiler_params=pltpu.CompilerParams(vmem_limit_bytes=SPARE_BYTES),
        name="write",
    )(*(pltpu.with_memory_space_constraint(r, pltpu.VMEM) for r in results))


def choose(mesh, layer_inputs, weights, *rest):
    if mesh.shape["dp"] != 8:
        return body_general(layer_inputs, weights, *rest)
    rows, width, units = layer_inputs.shape[1], layer_inputs.shape[2], weights.shape[1]
    tiles = rows % ROW_TILE, width % COLUMN_TILE, units % 256
    held = 4 * (3 * rows + units) * width
    total = fused_bytes(rows, width, units) + held + SPARE_BYTES
    if any(tiles) or total > VMEM_BYTES:
        return body_square(layer_inputs, weights, *rest)
    return body_fused(layer_inputs, weights, *rest)


def solution(mesh):
    specs = (
        P("depth", "dp", None),
        P("depth", "dp", None),
        P("depth", "dp"),
        P("depth", "dp", None),
        P("depth", "dp", None),
    )
    body = functools.partial(choose, mesh)
    return jax.shard_map(body, mesh=mesh, in_specs=specs, out_specs=specs, check_vma=False)
```

```python
import functools
import math

import jax
import jax.numpy as jnp
from jax import lax
from jax.experimental import pallas as pl
from jax.experimental.pallas import tpu as pltpu
from jax.sharding import PartitionSpec as P

fit_weight = 1.0
penalty = 1.0
step_input = 0.5
PRECISION = lax.Precision.HIGH


def passed_along(block, axis, distance):
    devices = range(lax.axis_size(axis))
    route = [(i - distance, i) for i in devices if i - distance in devices]
    return lax.ppermute(block, axis, route)


def swapped(block, bit):
    route = [(i, i ^ bit) for i in range(lax.axis_size("dp"))]
    return lax.ppermute(block, "dp", route)


def dot(a, b, dims):
    return lax.dot_general(a, b, (dims, ((), ())), precision=PRECISION)


def times_transposed(a, b):
    return dot(a, b, ((1,), (1,)))


def times(a, b):
    return dot(a, b, ((1,), (0,)))


def transposed_times(a, b):
    return dot(a, b, ((0,), (0,)))


def finish(inputs, outputs, mults, drive, prev_drive, affine, pulled_step, next_step):
    layer_index = lax.axis_index("depth")
    is_first = layer_index == 0
    is_last = layer_index == lax.axis_size("depth") - 1
    inputs_new = jnp.where(is_first, inputs, pulled_step - step_input * prev_drive)
    next_inputs = next_step - step_input * drive
    coupled = jnp.maximum(
        0.0, (fit_weight * affine + penalty * next_inputs + mults) / (fit_weight + penalty)
    )
    outputs_new = jnp.where(is_last, jnp.maximum(0.0, affine), coupled)
    mults_new = jnp.where(is_last, mults, mults + penalty * (next_inputs - outputs_new))
    return inputs_new, outputs_new, mults_new


def body_general(layer_inputs, weights, offsets, layer_outputs, multipliers):
    inputs, outputs, mults = layer_inputs[0], layer_outputs[0], multipliers[0]
    scaling = 1.0 / math.sqrt(inputs.shape[1])
    samples = inputs.shape[0] * lax.axis_size("dp")
    step_weight = 8.0 / math.sqrt(samples)
    step_offset = 0.5 / math.sqrt(samples)
    drive = mults - penalty * outputs
    prev_drive = passed_along(drive, "depth", 1)
    weight = lax.all_gather(weights[0], "dp", axis=0, tiled=True)
    offset = lax.all_gather(offsets, "dp", axis=1, tiled=True)
    affine = scaling * times_transposed(inputs, weight) + offset
    misfit = affine - outputs
    weight_grad = fit_weight * scaling * transposed_times(misfit, inputs)
    weight_sum = lax.psum_scatter(weight_grad, "dp", scatter_dimension=0, tiled=True)
    offset_sum = lax.psum_scatter(
        fit_weight * jnp.sum(misfit, axis=0), "dp", scatter_dimension=0, tiled=True
    )
    pulled = scaling * times(misfit, weight)
    pulled_step = inputs - step_input * (fit_weight * pulled + penalty * inputs)
    next_step = passed_along(pulled_step, "depth", -1)
    inputs_new, outputs_new, mults_new = finish(
        inputs, outputs, mults, drive, prev_drive, affine, pulled_step, next_step
    )
    weights_new = weights - step_weight * weight_sum[None]
    offsets_new = offsets - step_offset * offset_sum[None]
    return inputs_new[None], weights_new, offsets_new, outputs_new[None], mults_new[None]


def body_square(layer_inputs, weights, offsets, layer_outputs, multipliers):
    inputs, outputs, mults = layer_inputs[0], layer_outputs[0], multipliers[0]
    rows, width = inputs.shape
    units = weights.shape[1]
    half = units // 2
    scaling = 1.0 / math.sqrt(width)
    samples = rows * lax.axis_size("dp")
    step_weight = 8.0 / math.sqrt(samples)
    step_offset = 0.5 / math.sqrt(samples)
    me = lax.axis_index("dp")

    w_own = weights[0]
    low_own, high_own = w_own[:half], w_own[half:]
    low_own, high_own, inputs = lax.optimization_barrier((low_own, high_own, inputs))
    low_x, high_y = swapped(low_own, 2), swapped(high_own, 4)
    inputs_other = swapped(inputs, 1)
    inputs_other, outputs_late = lax.optimization_barrier((inputs_other, outputs))
    drive = mults - penalty * outputs
    prev_drive = passed_along(drive, "depth", 1)
    b_own = offsets
    b_x, b_y, b_d = swapped(b_own, 2), swapped(b_own, 4), swapped(b_own, 6)

    def columns(array, index):
        return lax.dynamic_slice(array, (0, index * units), (rows, units))

    def arranged(own, x, y, d):
        joined_a = jnp.concatenate([x[:, :half], y[:, half:]], axis=1)
        joined_b = jnp.concatenate([x[:, half:], y[:, :half]], axis=1)
        return own, joined_a, d, joined_b

    flips = (0, 2, 4, 6)
    out_mine = arranged(*[columns(outputs_late, me ^ f) for f in flips])
    out_sent = arranged(*[columns(outputs_late, me ^ f ^ 1) for f in flips])
    out_other = swapped(jnp.concatenate(out_sent, axis=1), 1)
    biases = arranged(b_own, b_x, b_y, b_d)
    both = jnp.concatenate([inputs, inputs_other], axis=0)

    def layer(n, w):
        affine = scaling * times_transposed(both, w) + biases[n]
        target = jnp.concatenate([out_mine[n], out_other[:, n * units : (n + 1) * units]], axis=0)
        return affine, affine - target

    affine_own, m = layer(0, w_own)
    g_own = transposed_times(m, both)
    o_own = jnp.sum(m, axis=0, keepdims=True)
    pulled = times(m, w_own)
    low_x, high_y, g_own, pulled, o_own = lax.optimization_barrier(
        (low_x, high_y, g_own, pulled, o_own)
    )

    low_d, high_d = swapped(low_x, 4), swapped(high_y, 2)
    w_a = jnp.concatenate([low_x, high_y], axis=0)
    affine_a, m = layer(1, w_a)
    g_a = transposed_times(m, both)
    o_a = jnp.sum(m, axis=0, keepdims=True)
    pulled = pulled + times(m, w_a)
    low_d, high_d, g_a, pulled, o_a, low_own, high_own = lax.optimization_barrier(
        (low_d, high_d, g_a, pulled, o_a, low_own, high_own)
    )

    high_x, low_y = swapped(high_own, 2), swapped(low_own, 4)
    w_d = jnp.concatenate([low_d, high_d], axis=0)
    affine_d, m = layer(2, w_d)
    g_d = transposed_times(m, both)
    o_d = jnp.sum(m, axis=0, keepdims=True)
    pulled = pulled + times(m, w_d)
    high_x, low_y, g_a, g_d, pulled, o_d, prev_drive = lax.optimization_barrier(
        (high_x, low_y, g_a, g_d, pulled, o_d, prev_drive)
    )

    x_low, y_high = swapped(g_a[:half], 2), swapped(g_a[half:], 4)
    from_x, from_y = swapped(g_d[:half], 2), swapped(g_d[half:], 4)
    w_b = jnp.concatenate([high_x, low_y], axis=0)
    affine_b, m = layer(3, w_b)
    pulled_other = swapped(pulled[rows:] + times(m[rows:], w_b), 1)
    pulled_mine = pulled[:rows] + times(m[:rows], w_b)
    pulled_all = scaling * (pulled_mine + pulled_other)
    pulled_step = inputs - step_input * (fit_weight * pulled_all + penalty * inputs)
    m, pulled_step = lax.optimization_barrier((m, pulled_step))
    next_step = passed_along(pulled_step, "depth", -1)
    g_b = transposed_times(m, both)
    o_b = jnp.sum(m, axis=0, keepdims=True)

    x_high = swapped(g_b[:half] + from_y, 2)
    y_low = swapped(g_b[half:] + from_x, 4)
    sum_low = g_own[:half] + x_low + y_low
    sum_high = g_own[half:] + x_high + y_high
    weight_step = step_weight * fit_weight * scaling
    weights_new = w_own - weight_step * jnp.concatenate([sum_low, sum_high], axis=0)
    o_x = jnp.concatenate([o_a[:, :half], o_b[:, :half]], axis=1)
    o_y = jnp.concatenate([o_b[:, half:], o_a[:, half:]], axis=1)
    offset_sum = o_own + swapped(o_x, 2) + swapped(o_y, 4) + swapped(o_d, 6)
    offsets_new = offsets - step_offset * fit_weight * offset_sum

    affines = (affine_own, affine_a, affine_d, affine_b)
    affine_other = swapped(jnp.concatenate([a[rows:] for a in affines], axis=1), 1)

    def by_owner(own, a, d, b):
        x = jnp.concatenate([a[:, :half], b[:, :half]], axis=1)
        y = jnp.concatenate([b[:, half:], a[:, half:]], axis=1)
        return own, x, y, d

    mine = by_owner(*[a[:rows] for a in affines])
    other = by_owner(*[affine_other[:, n * units : (n + 1) * units] for n in range(len(flips))])
    affine = jnp.zeros_like(outputs)
    for n, f in enumerate(flips):
        affine = lax.dynamic_update_slice(affine, mine[n], (0, (me ^ f) * units))
        affine = lax.dynamic_update_slice(affine, other[n], (0, (me ^ f ^ 1) * units))
    inputs_new, outputs_new, mults_new = finish(
        inputs, outputs, mults, drive, prev_drive, affine, pulled_step, next_step
    )
    return (
        inputs_new[None],
        weights_new[None],
        offsets_new,
        outputs_new[None],
        mults_new[None],
    )


MESH = pl.DeviceIdType.MESH
VMEM_BYTES = 67043328
SPARE_BYTES = 2**22
OWNERS = ((0, 0), (2, 4), (4, 2), (6, 6))
X, Y, DIAGONAL, PARTNER = 2, 4, 6, 1
ROW_TILE = 128
COLUMN_TILE = 256
LINK_CHUNKS = 4
EARLY_PART = 0.875


def fused_shapes(rows, width, units):
    f32, bf16 = jnp.float32, jnp.bfloat16
    return dict(
        pull=((2 * rows, width), f32),
        x_high=((2 * rows, width), bf16),
        x_low=((2 * rows, width), bf16),
        w=((4 * units, width), f32),
        w_high=((units, width), bf16),
        w_low=((units, width), bf16),
        target=((4, 2 * rows, units), f32),
        m_high=((2 * rows, units), bf16),
        m_low=((2 * rows, units), bf16),
        mt_high=((units, 2 * rows), bf16),
        mt_low=((units, 2 * rows), bf16),
        product=((2 * rows, units), f32),
        pull_in=((rows, width), f32),
        grad=((3 * units, width), f32),
        direct_in=((units, width), f32),
        relay_in=((units, width), f32),
        merged_in=((units, width), f32),
        next_in=((rows, width), f32),
        bias=((4, 8, units), f32),
        own_bias=((1, units), f32),
        osum=((4, 8, units), f32),
        osend=((3, 8, units), f32),
        orecv=((3, 8, units), f32),
    )


def fused_bytes(rows, width, units):
    shapes = fused_shapes(rows, width, units).values()
    return sum(math.prod(shape) * jnp.dtype(dtype).itemsize for shape, dtype in shapes)


def pull_blocks(width):
    narrow = COLUMN_TILE // 2
    widths = [COLUMN_TILE] * (width // COLUMN_TILE - 1) + [narrow] * 2
    return [slice(sum(widths[:i]), sum(widths[: i + 1])) for i in range(len(widths))]


def semaphore_counts(width):
    return 13, 19 + 2 * LINK_CHUNKS + 2 * len(pull_blocks(width)), 6


def fused_kernel(
    names, samples, x_ref, w_ref, b_ref, q_ref, u_ref, p_new, w_new, b_new, q_new, u_new, *scratch
):
    ref = dict(zip(names, scratch))
    send_sem, recv_sem, local_sem = scratch[len(names) :]
    pull, x_high, x_low, w = ref["pull"], ref["x_high"], ref["x_low"], ref["w"]
    w_high, w_low, target = ref["w_high"], ref["w_low"], ref["target"]
    m_high, m_low, mt_high, mt_low = ref["m_high"], ref["m_low"], ref["mt_high"], ref["mt_low"]
    pull_in, grad, partial = ref["pull_in"], ref["grad"], ref["product"]
    direct_in, relay_in, merged_in = ref["direct_in"], ref["relay_in"], ref["merged_in"]
    next_in = ref["next_in"]
    prev_in, own_grad, affine, drive = p_new.at[0], w_new.at[0], q_new.at[0], u_new.at[0]
    bias, osum, osend, orecv = ref["bias"], ref["osum"], ref["osend"], ref["orecv"]
    own_bias = ref["own_bias"]

    rows, width = affine.shape
    units = w_high.shape[0]
    half = units // 2
    scaling = 1.0 / math.sqrt(width)
    step_weight = 8.0 / math.sqrt(samples)
    step_offset = 0.5 / math.sqrt(samples)
    pull_factor = step_input * fit_weight * scaling
    keep_factor = 1.0 - step_input * penalty

    me, z = lax.axis_index("dp"), lax.axis_index("depth")
    has_prev, has_next = z > 0, z < lax.axis_size("depth") - 1
    bits = (me % 2, (me // 2) % 2, me // 4)

    def index_of(flip):
        return sum(((1 - b) if flip >> i & 1 else b) * 2**i for i, b in enumerate(bits))

    def device(flip):
        return (z, index_of(flip))

    above, below = (z + 1, me), (z - 1, me)
    sends, receives, locals_ = {}, {}, {}

    def slot(sems, taken, key):
        return sems.at[taken.setdefault(key, len(taken))]

    def remote(src, dst, to, sent, received):
        return pltpu.make_async_remote_copy(
            src_ref=src,
            dst_ref=dst,
            send_sem=slot(send_sem, sends, sent),
            recv_sem=slot(recv_sem, receives, received),
            device_id=to,
            device_id_type=MESH,
        )

    def local(src, dst, key):
        return pltpu.make_async_copy(src, dst, slot(local_sem, locals_, key))

    def wait_sent(key, buffer):
        pltpu.make_async_copy(buffer, buffer, slot(send_sem, sends, key)).wait()

    def wait_received(key, buffer):
        pltpu.make_async_copy(buffer, buffer, slot(recv_sem, receives, key)).wait()

    def columns(flip, h):
        return pl.ds(pl.multiple_of(index_of(flip) * units + h * half, half), half)

    def halves(h):
        return pl.ds(h * half, half)

    barrier = pltpu.get_barrier_semaphore()
    for flip in (PARTNER, X, Y):
        pl.semaphore_signal(barrier, inc=1, device_id=device(flip), device_id_type=MESH)

    @pl.when(has_prev)
    def _():
        pl.semaphore_signal(barrier, inc=1, device_id=below, device_id_type=MESH)

    @pl.when(has_next)
    def _():
        pl.semaphore_signal(barrier, inc=1, device_id=above, device_id_type=MESH)


    b_in = local(b_ref, own_bias, "b")
    b_in.start()
    w_in = local(w_ref.at[0], w.at[:units], "w")
    w_in.start()
    x_in = local(x_ref.at[0], pull.at[:rows], "x")
    x_in.start()

    depth = lax.axis_size("depth")
    pl.semaphore_wait(barrier, 3 + (z + depth - 1) // depth + 1 - (z + 1) // depth)

    b_in.wait()
    bias[0] = jnp.broadcast_to(own_bias[...], (8, units))
    bias_swap = [
        remote(bias.at[0], bias.at[flip // 2], device(flip), "bias", ("bias", flip))
        for flip in (X, Y)
    ]
    for copy in bias_swap:
        copy.start()
    w_in.wait()
    for piece, h, to in ((1, 0, X), (1, 1, Y), (2, 1, X), (2, 0, Y)):
        dst = w.at[pl.ds(piece * units + h * half, half)]
        remote(w.at[halves(h)], dst, device(to), "own", ("own", piece)).start()
    x_swap = remote(x_ref.at[0], pull.at[rows:], device(PARTNER), "x", "x")
    x_swap.start()

    def start_targets(n):
        for h, flip in enumerate(OWNERS[n]):
            src = q_ref.at[0, :, columns(flip, h)]
            local(src, target.at[n, :rows, halves(h)], "target").start()
            src = q_ref.at[0, :, columns(flip ^ PARTNER, h)]
            dst = target.at[n, rows:, halves(h)]
            remote(src, dst, device(PARTNER), "target", ("target", n)).start()

    start_targets(0)
    staged = grad.at[:rows]
    q_in, u_in = local(q_ref.at[0], staged, "q"), local(u_ref.at[0], drive, "u")
    q_in.start()
    u_in.start()
    for n in (1, 2, 3):
        start_targets(n)

    def split(value):
        high = value.astype(jnp.bfloat16)
        return high, (value - high.astype(jnp.float32)).astype(jnp.bfloat16)

    def split_rows(src, start, high, low, to, count, cols=slice(None)):
        step = 16 if cols == slice(None) else max(16, 16 * width // (cols.stop - cols.start) // 2)

        @pl.loop(0, count // step)
        def _(i):
            offset = pl.multiple_of(i * step, step)
            high_part, low_part = split(src[pl.ds(start + offset, step), cols])
            high[pl.ds(to + offset, step), cols] = high_part
            low[pl.ds(to + offset, step), cols] = low_part

    def dot(a, b, contract):
        return lax.dot_general(a, b, (contract, ((), ())), preferred_element_type=jnp.float32)

    def dot3(a, b, contract):
        return (
            dot(a[0], b[0], contract) + dot(a[1], b[0], contract) + dot(a[0], b[1], contract)
        )

    def product_part(side, cols, first, last, n):
        owners = OWNERS[n]
        at = pl.ds(side * rows, rows) if isinstance(side, int) else side
        value = dot3(
            (x_high[at, cols], x_low[at, cols]), (w_high[:, cols], w_low[:, cols]), ((1,), (1,))
        )
        if first:
            shift = [bias[owners[h] // 2, 0:1, h * half : (h + 1) * half] for h in (0, 1)]
            value = scaling * value + jnp.concatenate(shift, axis=1)
        if not last:
            partial[at, :] = value - target[n, at, :]
            return
        m = value - target[n, at, :] if first else scaling * value + partial[at, :]
        m_high[at, :], m_low[at, :] = split(m)
        if first:
            keep_affine(side, value, m, n)
        else:
            partial[at, :] = m

    def keep_affine(side, value, m, n):
        if side == 0:
            for h, flip in enumerate(OWNERS[n]):
                affine[:, columns(flip, h)] = value[:, h * half : (h + 1) * half]
        else:
            target[n, rows:, :] = value
        sums = jnp.sum(m.reshape(rows // 8, 8, units), axis=0)
        osum[n] = sums if side == 1 else osum[n] + sums

    def product(n):
        split_rows(w, n * units, w_high, w_low, 0, units)
        for side in (1, 0):
            product_part(side, slice(None), True, True, n)

    def pull_tile(at, cols):
        a = (m_high[at, :], m_low[at, :])
        return dot3(a, (w_high[:, cols], w_low[:, cols]), ((1,), (0,)))

    def column_loop(body):
        @pl.loop(0, width // COLUMN_TILE)
        def _(c):
            body(pl.ds(pl.multiple_of(c * COLUMN_TILE, COLUMN_TILE), COLUMN_TILE))

    def pull_add(n):
        for side in (1, 0):
            at = pl.ds(side * rows, rows)

            def body(cols):
                value = pull_tile(at, cols)
                if n > 0:
                    value += pull[at, cols]
                elif side == 0:
                    value -= (keep_factor / pull_factor) * pull[at, cols]
                pull[at, cols] = value

            column_loop(body)

    def gradient(n):
        for part, turned in ((m_high, mt_high), (m_low, mt_low)):

            @pl.loop(0, 2 * rows // ROW_TILE)
            def _(i):
                at = pl.ds(pl.multiple_of(i * ROW_TILE, ROW_TILE), ROW_TILE)
                turned[:, at] = part[at, :].astype(jnp.float32).T.astype(jnp.bfloat16)

        def body(cols):
            b = (x_high[:, cols], x_low[:, cols])
            value = dot3((mt_high[...], mt_low[...]), b, ((1,), (0,)))
            if n == 0:
                own_grad[:, cols] = value
            else:
                grad[pl.ds((n - 1) * units, units), cols] = value

        column_loop(body)

    def send_affine(n):
        for h, flip in enumerate(OWNERS[n]):
            src = target.at[n, rows:, halves(h)]
            dst = affine.at[:, columns(flip, h)]
            remote(src, dst, device(PARTNER), "affine", "affine").start()

    def wait_targets(n):
        wait_received(("target", n), target.at[n, rows:])

    x_in.wait()
    split_rows(pull, 0, x_high, x_low, 0, rows)
    x_swap.wait_recv()
    split_rows(pull, rows, x_high, x_low, rows, rows)
    whole = target.at[:, :rows]
    local(whole, whole, "target").wait()
    wait_targets(0)
    product(0)
    q_in.wait()
    u_in.wait()

    @pl.loop(0, rows // 16)
    def _(i):
        offset = pl.multiple_of(i * 16, 16)
        at = pl.ds(offset, 16)
        drive[at, :] = drive[at, :] - penalty * grad[pl.ds(offset, 16), :]

    pull_add(0)
    drive_up = remote(drive, prev_in, above, "drive", "drive")

    @pl.when(has_next)
    def _():
        drive_up.start()

    send_affine(0)
    gradient(0)

    for copy in bias_swap:
        copy.wait_recv()
    bias_on = remote(bias.at[1], bias.at[3], device(Y), "bias", ("bias", DIAGONAL))
    bias_on.start()
    wait_received(("own", 1), w.at[units : 2 * units])
    cut = int(width * EARLY_PART) // 128 * 128
    parts = (slice(0, cut), slice(cut, width))
    for k, cols in enumerate(parts):
        for h, to in ((1, X), (0, Y)):
            src = w.at[pl.ds(units + h * half, half), cols]
            dst = w.at[pl.ds(3 * units + h * half, half), cols]
            remote(src, dst, device(to), "forward", ("forward", k)).start()
    wait_targets(1)
    product(1)
    gradient(1)
    pull_add(1)
    send_affine(1)
    for h, to in ((0, X), (1, Y)):
        src = grad.at[halves(h)]
        remote(src, direct_in.at[halves(h)], device(to), "direct", "direct").start()

    wait_received(("own", 2), w.at[2 * units : 3 * units])
    wait_targets(2)
    product(2)
    gradient(2)
    pull_add(2)
    send_affine(2)

    wait_targets(3)
    early, late = parts
    bias_on.wait_recv()
    wait_received(("forward", 0), w.at[3 * units :, early])
    split_rows(w, 3 * units, w_high, w_low, 0, units, early)
    for side in (1, 0):
        product_part(side, early, True, False, 3)

    blocks = pull_blocks(width)
    pull_swap, step_down = [], []
    row_halves = slice(0, rows // 2), slice(rows // 2, rows)
    for i, cols in enumerate(blocks):
        ends = pull.at[rows:, cols], pull_in.at[:, cols]
        pull_swap.append(remote(*ends, device(PARTNER), "pull", ("pull", i)))
        step_down.append([])
        for k, at in enumerate(row_halves if i == 0 else (slice(0, rows),)):
            ends = pull.at[at, cols], next_in.at[at, cols]
            step_down[i].append(remote(*ends, below, "step", ("step", i, k)))

    def pull_last(side, i):
        if i < len(blocks):
            at = pl.ds(side * rows, rows)
            pull[at, blocks[i]] = pull[at, blocks[i]] + pull_tile(at, blocks[i])

    def swap(i):
        if i < len(blocks):
            pull_swap[i].start()

    def pull_done(i):
        cols = blocks[i]
        pull_swap[i].wait_recv()
        pull[:rows, cols] = -pull_factor * (pull[:rows, cols] + pull_in[:, cols])

    def send_down(i):
        @pl.when(has_prev)
        def _():
            for copy in step_down[i]:
                copy.start()

    wait_received(("forward", 1), w.at[3 * units :, late])
    split_rows(w, 3 * units, w_high, w_low, 0, units, late)
    @pl.when(bits[0] == 0)
    def _():
        for k, at in enumerate(row_halves):
            product_part(at, late, False, True, 3)
            value = pull[at, blocks[0]] + pull_tile(at, blocks[0])
            if k == 0:
                pull_swap[0].wait_recv()
            pull[at, blocks[0]] = -pull_factor * (value + pull_in[at, blocks[0]])

            @pl.when(has_prev)
            def _():
                step_down[0][k].start()

        product_part(1, late, False, True, 3)
        pull_last(1, 0)
        swap(0)
        pull_last(0, 1)
        pull_last(1, 1)
        swap(1)
        pull_done(1)
        send_down(1)

    @pl.when(bits[0] == 1)
    def _():
        product_part(1, late, False, True, 3)
        pull_last(1, 0)
        swap(0)
        product_part(0, late, False, True, 3)
        pull_last(1, 1)
        pull_last(0, 0)
        swap(1)
        pull_last(0, 1)
        pull_done(0)
        send_down(0)
        pull_done(1)
        send_down(1)

    pull_last(1, 2)
    swap(2)
    for i in range(2, len(blocks)):
        pull_last(1, i + 1)
        pull_last(0, i)
        swap(i + 1)
        pull_done(i)
        send_down(i)
    for side in (1, 0):
        m = partial[pl.ds(side * rows, rows), :]
        keep_affine(side, m + target[3, pl.ds(side * rows, rows), :], m, 3)
    send_affine(3)
    gradient(3)
    link_rows = half // LINK_CHUNKS
    merged = {}

    def link_part(h, c):
        return pl.ds(h * half + c * link_rows, link_rows)

    for c in range(LINK_CHUNKS):
        for h, to in ((0, X), (1, Y)):
            at = link_part(h, c)
            src = grad.at[pl.ds(2 * units + h * half + c * link_rows, link_rows)]
            remote(src, relay_in.at[at], device(to), "relay", ("relay", c)).start()
    for c in range(LINK_CHUNKS):
        for h, to in ((1, X), (0, Y)):
            src = grad.at[pl.ds(units + h * half + c * link_rows, link_rows)]
            dst = merged_in.at[link_part(h, c)]
            merged[h, c] = remote(src, dst, device(to), "merged", ("merged", c))

    for k, (low, high) in enumerate(((1, 2), (2, 1), (3, 3))):
        osend[k, :, :half] = osum[low, :, :half]
        osend[k, :, half:] = osum[high, :, half:]
    sums = [
        remote(osend.at[k], orecv.at[k], device(flip), "sums", ("sums", k))
        for k, flip in enumerate((X, Y, X))
    ]


    @pl.when(has_prev)
    def _():
        drive_up.wait_recv()

        @pl.loop(0, rows // 16)
        def _(i):
            at = pl.ds(pl.multiple_of(i * 16, 16), 16)
            prev_in[at, :] = pull[at, :] - step_input * prev_in[at, :]

    p_copy = local(x_ref.at[0], prev_in, "x")

    @pl.when(jnp.logical_not(has_prev))
    def _():
        p_copy.start()
        p_copy.wait()

    sums[0].start()
    sums[2].start()
    wait_sent("pull", pull.at[rows:])
    u_late = local(u_ref.at[0], pull.at[rows:], "u")
    u_late.start()

    @pl.when(has_next)
    def _():
        drive_up.wait_send()

    wait_received("affine", affine.at[:, : width // 2])
    u_late.wait()

    def finish_block(i):
        cols = blocks[i]

        @pl.when(has_next)
        def _():
            for copy in step_down[i]:
                copy.wait_recv()

            @pl.loop(0, rows // 32)
            def _(j):
                offset = pl.multiple_of(j * 32, 32)
                at = pl.ds(offset, 32)
                mults = pull[pl.ds(rows + offset, 32), cols]
                following = next_in[at, cols] - step_input * drive[at, cols]
                total = fit_weight * affine[at, cols] + penalty * following + mults
                fresh = jnp.maximum(0.0, total / (fit_weight + penalty))
                affine[at, cols] = fresh
                drive[at, cols] = mults + penalty * (following - fresh)

        @pl.when(jnp.logical_not(has_next))
        def _():
            @pl.loop(0, rows // 32)
            def _(j):
                offset = pl.multiple_of(j * 32, 32)
                at = pl.ds(offset, 32)
                affine[at, cols] = jnp.maximum(0.0, affine[at, cols])
                drive[at, cols] = pull[pl.ds(rows + offset, 32), cols]

    def merge(c):
        wait_received(("relay", c), relay_in.at[: 2 * link_rows])
        for h in (1, 0):
            start = units + h * half + c * link_rows
            at = pl.ds(start, link_rows)
            grad[at, :] = grad[at, :] + relay_in[link_part(h, c), :]
        for h in (1, 0):
            merged[h, c].start()

    def finish_weights(c):
        wait_received(("merged", c), merged_in.at[: 2 * link_rows])
        for h in (0, 1):
            at = link_part(h, c)
            total = own_grad[at, :] + direct_in[at, :] + merged_in[at, :]
            own_grad[at, :] = w[at, :] - (step_weight * fit_weight * scaling) * total

    def merge_offsets(_):
        wait_received("direct", direct_in)
        sums[2].wait_recv()
        osend[1] = osend[1] + orecv[2]
        sums[1].start()

    def finish_offsets(_):
        sums[0].wait_recv()
        sums[1].wait_recv()
        total = osum[0] + orecv[0] + orecv[1]
        total = jnp.sum(total, axis=0, keepdims=True)
        b_new[...] = own_bias[...] - (step_offset * fit_weight) * total

    ready, stage = [], width / 3
    for i, cols in enumerate(blocks):
        ready.append((cols.stop / stage + 0.2, finish_block, i))
    for c in range(LINK_CHUNKS):
        ready.append((1 + (c + 1) / LINK_CHUNKS, merge, c))
        ready.append((2 + (c + 1) / LINK_CHUNKS, finish_weights, c))
    ready.append((2.1, merge_offsets, 0))
    ready.append((2.6, finish_offsets, 0))
    def settle(_):
        wait_sent("own", w.at[: 2 * units])
        wait_sent("forward", w.at[:units])
        wait_sent("x", pull.at[:rows])
        wait_sent("target", target.at[:, :rows])
        wait_sent("affine", target.at[:, :rows])
        wait_sent("bias", bias.at[1:])
        wait_sent("direct", direct_in)
        wait_sent("relay", relay_in)
        wait_sent("sums", orecv)

    ready.append((blocks[-1].start / stage - 0.1, settle, 0))
    for _, work, i in sorted(ready, key=lambda entry: entry[0]):
        work(i)
    wait_sent("merged", merged_in)

    @pl.when(has_prev)
    def _():
        wait_sent("step", pull.at[:rows])

    counts = len(sends), len(receives), len(locals_)
    if counts != semaphore_counts(width):
        raise ValueError(counts)


def write_kernel(*refs):
    values, outs, sems = refs[:5], refs[5:10], refs[10]
    copies = [pltpu.make_async_copy(*pair, sems.at[i]) for i, pair in enumerate(zip(values, outs))]
    for copy in copies:
        copy.start()
    for copy in copies:
        copy.wait()


def body_fused(layer_inputs, weights, offsets, layer_outputs, multipliers):
    _, rows, width = layer_inputs.shape
    units = weights.shape[1]
    shapes = fused_shapes(rows, width, units)
    samples = rows * lax.axis_size("dp")
    anywhere = pl.BlockSpec(memory_space=pl.ANY)
    vmem = pl.BlockSpec(memory_space=pltpu.VMEM)
    args = (layer_inputs, weights, offsets, layer_outputs, multipliers)
    results = pl.pallas_call(
        functools.partial(fused_kernel, tuple(shapes), samples),
        out_shape=tuple(pltpu.VMEM(a.shape, a.dtype) for a in args),
        in_specs=[anywhere] * 5,
        out_specs=[vmem] * 5,
        scratch_shapes=[pltpu.VMEM(shape, dtype) for shape, dtype in shapes.values()]
        + [pltpu.SemaphoreType.DMA((count,)) for count in semaphore_counts(width)],
        compiler_params=pltpu.CompilerParams(
            collective_id=0,
            has_side_effects=True,
            vmem_limit_bytes=fused_bytes(rows, width, units) + SPARE_BYTES,
        ),
        name="iteration",
    )(*args)
    return pl.pallas_call(
        write_kernel,
        out_shape=tuple(jax.ShapeDtypeStruct(a.shape, a.dtype) for a in args),
        in_specs=[vmem] * 5,
        out_specs=[anywhere] * 5,
        scratch_shapes=[pltpu.SemaphoreType.DMA((5,))],
        compiler_params=pltpu.CompilerParams(vmem_limit_bytes=SPARE_BYTES),
        name="write",
    )(*(pltpu.with_memory_space_constraint(r, pltpu.VMEM) for r in results))


def choose(mesh, layer_inputs, weights, *rest):
    if mesh.shape["dp"] != 8:
        return body_general(layer_inputs, weights, *rest)
    rows, width, units = layer_inputs.shape[1], layer_inputs.shape[2], weights.shape[1]
    tiles = rows % ROW_TILE, width % COLUMN_TILE, units % 256
    held = 4 * (3 * rows + units) * width
    total = fused_bytes(rows, width, units) + held + SPARE_BYTES
    if any(tiles) or total > VMEM_BYTES:
        return body_square(layer_inputs, weights, *rest)
    return body_fused(layer_inputs, weights, *rest)


def solution(mesh):
    specs = (
        P("depth", "dp", None),
        P("depth", "dp", None),
        P("depth", "dp"),
        P("depth", "dp", None),
        P("depth", "dp", None),
    )
    body = functools.partial(choose, mesh)
    return jax.shard_map(body, mesh=mesh, in_specs=specs, out_specs=specs, check_vma=False)
```

```python
import functools
import math

import jax
import jax.numpy as jnp
from jax import lax
from jax.experimental import pallas as pl
from jax.experimental.pallas import tpu as pltpu
from jax.sharding import PartitionSpec as P

fit_weight = 1.0
penalty = 1.0
step_input = 0.5
PRECISION = lax.Precision.HIGH


def passed_along(block, axis, distance):
    devices = range(lax.axis_size(axis))
    route = [(i - distance, i) for i in devices if i - distance in devices]
    return lax.ppermute(block, axis, route)


def swapped(block, bit):
    route = [(i, i ^ bit) for i in range(lax.axis_size("dp"))]
    return lax.ppermute(block, "dp", route)


def dot(a, b, dims):
    return lax.dot_general(a, b, (dims, ((), ())), precision=PRECISION)


def times_transposed(a, b):
    return dot(a, b, ((1,), (1,)))


def times(a, b):
    return dot(a, b, ((1,), (0,)))


def transposed_times(a, b):
    return dot(a, b, ((0,), (0,)))


def finish(inputs, outputs, mults, drive, prev_drive, affine, pulled_step, next_step):
    layer_index = lax.axis_index("depth")
    is_first = layer_index == 0
    is_last = layer_index == lax.axis_size("depth") - 1
    inputs_new = jnp.where(is_first, inputs, pulled_step - step_input * prev_drive)
    next_inputs = next_step - step_input * drive
    coupled = jnp.maximum(
        0.0, (fit_weight * affine + penalty * next_inputs + mults) / (fit_weight + penalty)
    )
    outputs_new = jnp.where(is_last, jnp.maximum(0.0, affine), coupled)
    mults_new = jnp.where(is_last, mults, mults + penalty * (next_inputs - outputs_new))
    return inputs_new, outputs_new, mults_new


def body_general(layer_inputs, weights, offsets, layer_outputs, multipliers):
    inputs, outputs, mults = layer_inputs[0], layer_outputs[0], multipliers[0]
    scaling = 1.0 / math.sqrt(inputs.shape[1])
    samples = inputs.shape[0] * lax.axis_size("dp")
    step_weight = 8.0 / math.sqrt(samples)
    step_offset = 0.5 / math.sqrt(samples)
    drive = mults - penalty * outputs
    prev_drive = passed_along(drive, "depth", 1)
    weight = lax.all_gather(weights[0], "dp", axis=0, tiled=True)
    offset = lax.all_gather(offsets, "dp", axis=1, tiled=True)
    affine = scaling * times_transposed(inputs, weight) + offset
    misfit = affine - outputs
    weight_grad = fit_weight * scaling * transposed_times(misfit, inputs)
    weight_sum = lax.psum_scatter(weight_grad, "dp", scatter_dimension=0, tiled=True)
    offset_sum = lax.psum_scatter(
        fit_weight * jnp.sum(misfit, axis=0), "dp", scatter_dimension=0, tiled=True
    )
    pulled = scaling * times(misfit, weight)
    pulled_step = inputs - step_input * (fit_weight * pulled + penalty * inputs)
    next_step = passed_along(pulled_step, "depth", -1)
    inputs_new, outputs_new, mults_new = finish(
        inputs, outputs, mults, drive, prev_drive, affine, pulled_step, next_step
    )
    weights_new = weights - step_weight * weight_sum[None]
    offsets_new = offsets - step_offset * offset_sum[None]
    return inputs_new[None], weights_new, offsets_new, outputs_new[None], mults_new[None]


def body_square(layer_inputs, weights, offsets, layer_outputs, multipliers):
    inputs, outputs, mults = layer_inputs[0], layer_outputs[0], multipliers[0]
    rows, width = inputs.shape
    units = weights.shape[1]
    half = units // 2
    scaling = 1.0 / math.sqrt(width)
    samples = rows * lax.axis_size("dp")
    step_weight = 8.0 / math.sqrt(samples)
    step_offset = 0.5 / math.sqrt(samples)
    me = lax.axis_index("dp")

    w_own = weights[0]
    low_own, high_own = w_own[:half], w_own[half:]
    low_own, high_own, inputs = lax.optimization_barrier((low_own, high_own, inputs))
    low_x, high_y = swapped(low_own, 2), swapped(high_own, 4)
    inputs_other = swapped(inputs, 1)
    inputs_other, outputs_late = lax.optimization_barrier((inputs_other, outputs))
    drive = mults - penalty * outputs
    prev_drive = passed_along(drive, "depth", 1)
    b_own = offsets
    b_x, b_y, b_d = swapped(b_own, 2), swapped(b_own, 4), swapped(b_own, 6)

    def columns(array, index):
        return lax.dynamic_slice(array, (0, index * units), (rows, units))

    def arranged(own, x, y, d):
        joined_a = jnp.concatenate([x[:, :half], y[:, half:]], axis=1)
        joined_b = jnp.concatenate([x[:, half:], y[:, :half]], axis=1)
        return own, joined_a, d, joined_b

    flips = (0, 2, 4, 6)
    out_mine = arranged(*[columns(outputs_late, me ^ f) for f in flips])
    out_sent = arranged(*[columns(outputs_late, me ^ f ^ 1) for f in flips])
    out_other = swapped(jnp.concatenate(out_sent, axis=1), 1)
    biases = arranged(b_own, b_x, b_y, b_d)
    both = jnp.concatenate([inputs, inputs_other], axis=0)

    def layer(n, w):
        affine = scaling * times_transposed(both, w) + biases[n]
        target = jnp.concatenate([out_mine[n], out_other[:, n * units : (n + 1) * units]], axis=0)
        return affine, affine - target

    affine_own, m = layer(0, w_own)
    g_own = transposed_times(m, both)
    o_own = jnp.sum(m, axis=0, keepdims=True)
    pulled = times(m, w_own)
    low_x, high_y, g_own, pulled, o_own = lax.optimization_barrier(
        (low_x, high_y, g_own, pulled, o_own)
    )

    low_d, high_d = swapped(low_x, 4), swapped(high_y, 2)
    w_a = jnp.concatenate([low_x, high_y], axis=0)
    affine_a, m = layer(1, w_a)
    g_a = transposed_times(m, both)
    o_a = jnp.sum(m, axis=0, keepdims=True)
    pulled = pulled + times(m, w_a)
    low_d, high_d, g_a, pulled, o_a, low_own, high_own = lax.optimization_barrier(
        (low_d, high_d, g_a, pulled, o_a, low_own, high_own)
    )

    high_x, low_y = swapped(high_own, 2), swapped(low_own, 4)
    w_d = jnp.concatenate([low_d, high_d], axis=0)
    affine_d, m = layer(2, w_d)
    g_d = transposed_times(m, both)
    o_d = jnp.sum(m, axis=0, keepdims=True)
    pulled = pulled + times(m, w_d)
    high_x, low_y, g_a, g_d, pulled, o_d, prev_drive = lax.optimization_barrier(
        (high_x, low_y, g_a, g_d, pulled, o_d, prev_drive)
    )

    x_low, y_high = swapped(g_a[:half], 2), swapped(g_a[half:], 4)
    from_x, from_y = swapped(g_d[:half], 2), swapped(g_d[half:], 4)
    w_b = jnp.concatenate([high_x, low_y], axis=0)
    affine_b, m = layer(3, w_b)
    pulled_other = swapped(pulled[rows:] + times(m[rows:], w_b), 1)
    pulled_mine = pulled[:rows] + times(m[:rows], w_b)
    pulled_all = scaling * (pulled_mine + pulled_other)
    pulled_step = inputs - step_input * (fit_weight * pulled_all + penalty * inputs)
    m, pulled_step = lax.optimization_barrier((m, pulled_step))
    next_step = passed_along(pulled_step, "depth", -1)
    g_b = transposed_times(m, both)
    o_b = jnp.sum(m, axis=0, keepdims=True)

    x_high = swapped(g_b[:half] + from_y, 2)
    y_low = swapped(g_b[half:] + from_x, 4)
    sum_low = g_own[:half] + x_low + y_low
    sum_high = g_own[half:] + x_high + y_high
    weight_step = step_weight * fit_weight * scaling
    weights_new = w_own - weight_step * jnp.concatenate([sum_low, sum_high], axis=0)
    o_x = jnp.concatenate([o_a[:, :half], o_b[:, :half]], axis=1)
    o_y = jnp.concatenate([o_b[:, half:], o_a[:, half:]], axis=1)
    offset_sum = o_own + swapped(o_x, 2) + swapped(o_y, 4) + swapped(o_d, 6)
    offsets_new = offsets - step_offset * fit_weight * offset_sum

    affines = (affine_own, affine_a, affine_d, affine_b)
    affine_other = swapped(jnp.concatenate([a[rows:] for a in affines], axis=1), 1)

    def by_owner(own, a, d, b):
        x = jnp.concatenate([a[:, :half], b[:, :half]], axis=1)
        y = jnp.concatenate([b[:, half:], a[:, half:]], axis=1)
        return own, x, y, d

    mine = by_owner(*[a[:rows] for a in affines])
    other = by_owner(*[affine_other[:, n * units : (n + 1) * units] for n in range(len(flips))])
    affine = jnp.zeros_like(outputs)
    for n, f in enumerate(flips):
        affine = lax.dynamic_update_slice(affine, mine[n], (0, (me ^ f) * units))
        affine = lax.dynamic_update_slice(affine, other[n], (0, (me ^ f ^ 1) * units))
    inputs_new, outputs_new, mults_new = finish(
        inputs, outputs, mults, drive, prev_drive, affine, pulled_step, next_step
    )
    return (
        inputs_new[None],
        weights_new[None],
        offsets_new,
        outputs_new[None],
        mults_new[None],
    )


MESH = pl.DeviceIdType.MESH
VMEM_BYTES = 67043328
SPARE_BYTES = 2**22
OWNERS = ((0, 0), (2, 4), (4, 2), (6, 6))
X, Y, DIAGONAL, PARTNER = 2, 4, 6, 1
ROW_TILE = 128
COLUMN_TILE = 256
LINK_CHUNKS = 2
EARLY_PART = 0.875


def fused_shapes(rows, width, units):
    f32, bf16 = jnp.float32, jnp.bfloat16
    return dict(
        pull=((2 * rows, width), f32),
        x_high=((2 * rows, width), bf16),
        x_low=((2 * rows, width), bf16),
        w=((4 * units, width), f32),
        w_high=((units, width), bf16),
        w_low=((units, width), bf16),
        target=((4, 2 * rows, units), f32),
        m_high=((2 * rows, units), bf16),
        m_low=((2 * rows, units), bf16),
        mt_high=((units, 2 * rows), bf16),
        mt_low=((units, 2 * rows), bf16),
        product=((2 * rows, units), f32),
        pull_in=((rows, width), f32),
        grad=((3 * units, width), f32),
        direct_in=((units, width), f32),
        relay_in=((units, width), f32),
        merged_in=((units, width), f32),
        next_in=((rows, width), f32),
        bias=((4, 8, units), f32),
        own_bias=((1, units), f32),
        osum=((4, 8, units), f32),
        osend=((3, 8, units), f32),
        orecv=((3, 8, units), f32),
    )


def fused_bytes(rows, width, units):
    shapes = fused_shapes(rows, width, units).values()
    return sum(math.prod(shape) * jnp.dtype(dtype).itemsize for shape, dtype in shapes)


def pull_blocks(width):
    narrow = COLUMN_TILE // 2
    widths = [COLUMN_TILE] * (width // COLUMN_TILE - 1) + [narrow] * 2
    return [slice(sum(widths[:i]), sum(widths[: i + 1])) for i in range(len(widths))]


def semaphore_counts(width):
    return 13, 19 + 2 * LINK_CHUNKS + 2 * len(pull_blocks(width)), 6


def fused_kernel(
    names, samples, x_ref, w_ref, b_ref, q_ref, u_ref, p_new, w_new, b_new, q_new, u_new, *scratch
):
    ref = dict(zip(names, scratch))
    send_sem, recv_sem, local_sem = scratch[len(names) :]
    pull, x_high, x_low, w = ref["pull"], ref["x_high"], ref["x_low"], ref["w"]
    w_high, w_low, target = ref["w_high"], ref["w_low"], ref["target"]
    m_high, m_low, mt_high, mt_low = ref["m_high"], ref["m_low"], ref["mt_high"], ref["mt_low"]
    pull_in, grad, partial = ref["pull_in"], ref["grad"], ref["product"]
    direct_in, relay_in, merged_in = ref["direct_in"], ref["relay_in"], ref["merged_in"]
    next_in = ref["next_in"]
    prev_in, own_grad, affine, drive = p_new.at[0], w_new.at[0], q_new.at[0], u_new.at[0]
    bias, osum, osend, orecv = ref["bias"], ref["osum"], ref["osend"], ref["orecv"]
    own_bias = ref["own_bias"]

    rows, width = affine.shape
    units = w_high.shape[0]
    half = units // 2
    scaling = 1.0 / math.sqrt(width)
    step_weight = 8.0 / math.sqrt(samples)
    step_offset = 0.5 / math.sqrt(samples)
    pull_factor = step_input * fit_weight * scaling
    keep_factor = 1.0 - step_input * penalty

    me, z = lax.axis_index("dp"), lax.axis_index("depth")
    has_prev, has_next = z > 0, z < lax.axis_size("depth") - 1
    bits = (me % 2, (me // 2) % 2, me // 4)

    def index_of(flip):
        return sum(((1 - b) if flip >> i & 1 else b) * 2**i for i, b in enumerate(bits))

    def device(flip):
        return (z, index_of(flip))

    above, below = (z + 1, me), (z - 1, me)
    sends, receives, locals_ = {}, {}, {}

    def slot(sems, taken, key):
        return sems.at[taken.setdefault(key, len(taken))]

    def remote(src, dst, to, sent, received):
        return pltpu.make_async_remote_copy(
            src_ref=src,
            dst_ref=dst,
            send_sem=slot(send_sem, sends, sent),
            recv_sem=slot(recv_sem, receives, received),
            device_id=to,
            device_id_type=MESH,
        )

    def local(src, dst, key):
        return pltpu.make_async_copy(src, dst, slot(local_sem, locals_, key))

    def wait_sent(key, buffer):
        pltpu.make_async_copy(buffer, buffer, slot(send_sem, sends, key)).wait()

    def wait_received(key, buffer):
        pltpu.make_async_copy(buffer, buffer, slot(recv_sem, receives, key)).wait()

    def columns(flip, h):
        return pl.ds(pl.multiple_of(index_of(flip) * units + h * half, half), half)

    def halves(h):
        return pl.ds(h * half, half)

    barrier = pltpu.get_barrier_semaphore()
    for flip in (PARTNER, X, Y):
        pl.semaphore_signal(barrier, inc=1, device_id=device(flip), device_id_type=MESH)

    @pl.when(has_prev)
    def _():
        pl.semaphore_signal(barrier, inc=1, device_id=below, device_id_type=MESH)

    @pl.when(has_next)
    def _():
        pl.semaphore_signal(barrier, inc=1, device_id=above, device_id_type=MESH)


    b_in = local(b_ref, own_bias, "b")
    b_in.start()
    w_in = local(w_ref.at[0], w.at[:units], "w")
    w_in.start()
    x_in = local(x_ref.at[0], pull.at[:rows], "x")
    x_in.start()

    depth = lax.axis_size("depth")
    pl.semaphore_wait(barrier, 3 + (z + depth - 1) // depth + 1 - (z + 1) // depth)

    b_in.wait()
    bias[0] = jnp.broadcast_to(own_bias[...], (8, units))
    bias_swap = [
        remote(bias.at[0], bias.at[flip // 2], device(flip), "bias", ("bias", flip))
        for flip in (X, Y)
    ]
    for copy in bias_swap:
        copy.start()
    w_in.wait()
    for piece, h, to in ((1, 0, X), (1, 1, Y), (2, 1, X), (2, 0, Y)):
        dst = w.at[pl.ds(piece * units + h * half, half)]
        remote(w.at[halves(h)], dst, device(to), "own", ("own", piece)).start()
    x_swap = remote(x_ref.at[0], pull.at[rows:], device(PARTNER), "x", "x")
    x_swap.start()

    def start_targets(n):
        for h, flip in enumerate(OWNERS[n]):
            src = q_ref.at[0, :, columns(flip, h)]
            local(src, target.at[n, :rows, halves(h)], "target").start()
            src = q_ref.at[0, :, columns(flip ^ PARTNER, h)]
            dst = target.at[n, rows:, halves(h)]
            remote(src, dst, device(PARTNER), "target", ("target", n)).start()

    start_targets(0)
    staged = grad.at[:rows]
    q_in, u_in = local(q_ref.at[0], staged, "q"), local(u_ref.at[0], drive, "u")
    q_in.start()
    u_in.start()
    for n in (1, 2, 3):
        start_targets(n)

    def split(value):
        high = value.astype(jnp.bfloat16)
        return high, (value - high.astype(jnp.float32)).astype(jnp.bfloat16)

    def split_rows(src, start, high, low, to, count, cols=slice(None)):
        step = 16 if cols == slice(None) else max(16, 16 * width // (cols.stop - cols.start) // 2)

        @pl.loop(0, count // step)
        def _(i):
            offset = pl.multiple_of(i * step, step)
            high_part, low_part = split(src[pl.ds(start + offset, step), cols])
            high[pl.ds(to + offset, step), cols] = high_part
            low[pl.ds(to + offset, step), cols] = low_part

    def dot(a, b, contract):
        return lax.dot_general(a, b, (contract, ((), ())), preferred_element_type=jnp.float32)

    def dot3(a, b, contract):
        return (
            dot(a[0], b[0], contract) + dot(a[1], b[0], contract) + dot(a[0], b[1], contract)
        )

    def product_part(side, cols, first, last, n):
        owners = OWNERS[n]
        at = pl.ds(side * rows, rows) if isinstance(side, int) else side
        value = dot3(
            (x_high[at, cols], x_low[at, cols]), (w_high[:, cols], w_low[:, cols]), ((1,), (1,))
        )
        if first:
            shift = [bias[owners[h] // 2, 0:1, h * half : (h + 1) * half] for h in (0, 1)]
            value = scaling * value + jnp.concatenate(shift, axis=1)
        if not last:
            partial[at, :] = value - target[n, at, :]
            return
        m = value - target[n, at, :] if first else scaling * value + partial[at, :]
        m_high[at, :], m_low[at, :] = split(m)
        if first:
            keep_affine(side, value, m, n)
        else:
            partial[at, :] = m

    def keep_affine(side, value, m, n):
        if side == 0:
            for h, flip in enumerate(OWNERS[n]):
                affine[:, columns(flip, h)] = value[:, h * half : (h + 1) * half]
        else:
            target[n, rows:, :] = value
        sums = jnp.sum(m.reshape(rows // 8, 8, units), axis=0)
        osum[n] = sums if side == 1 else osum[n] + sums

    def product(n):
        split_rows(w, n * units, w_high, w_low, 0, units)
        for side in (1, 0):
            product_part(side, slice(None), True, True, n)

    def pull_tile(at, cols):
        a = (m_high[at, :], m_low[at, :])
        return dot3(a, (w_high[:, cols], w_low[:, cols]), ((1,), (0,)))

    def column_loop(body):
        @pl.loop(0, width // COLUMN_TILE)
        def _(c):
            body(pl.ds(pl.multiple_of(c * COLUMN_TILE, COLUMN_TILE), COLUMN_TILE))

    def pull_add(n):
        for side in (1, 0):
            at = pl.ds(side * rows, rows)

            def body(cols):
                value = pull_tile(at, cols)
                if n > 0:
                    value += pull[at, cols]
                elif side == 0:
                    value -= (keep_factor / pull_factor) * pull[at, cols]
                pull[at, cols] = value

            column_loop(body)

    def gradient(n):
        for part, turned in ((m_high, mt_high), (m_low, mt_low)):

            @pl.loop(0, 2 * rows // ROW_TILE)
            def _(i):
                at = pl.ds(pl.multiple_of(i * ROW_TILE, ROW_TILE), ROW_TILE)
                turned[:, at] = part[at, :].astype(jnp.float32).T.astype(jnp.bfloat16)

        def body(cols):
            b = (x_high[:, cols], x_low[:, cols])
            value = dot3((mt_high[...], mt_low[...]), b, ((1,), (0,)))
            if n == 0:
                own_grad[:, cols] = value
            else:
                grad[pl.ds((n - 1) * units, units), cols] = value

        column_loop(body)

    def send_affine(n):
        for h, flip in enumerate(OWNERS[n]):
            src = target.at[n, rows:, halves(h)]
            dst = affine.at[:, columns(flip, h)]
            remote(src, dst, device(PARTNER), "affine", "affine").start()

    def wait_targets(n):
        wait_received(("target", n), target.at[n, rows:])

    x_in.wait()
    split_rows(pull, 0, x_high, x_low, 0, rows)
    x_swap.wait_recv()
    split_rows(pull, rows, x_high, x_low, rows, rows)
    whole = target.at[:, :rows]
    local(whole, whole, "target").wait()
    wait_targets(0)
    product(0)
    q_in.wait()
    u_in.wait()

    @pl.loop(0, rows // 16)
    def _(i):
        offset = pl.multiple_of(i * 16, 16)
        at = pl.ds(offset, 16)
        drive[at, :] = drive[at, :] - penalty * grad[pl.ds(offset, 16), :]

    pull_add(0)
    drive_up = remote(drive, prev_in, above, "drive", "drive")

    @pl.when(has_next)
    def _():
        drive_up.start()

    send_affine(0)
    gradient(0)

    for copy in bias_swap:
        copy.wait_recv()
    bias_on = remote(bias.at[1], bias.at[3], device(Y), "bias", ("bias", DIAGONAL))
    bias_on.start()
    wait_received(("own", 1), w.at[units : 2 * units])
    cut = int(width * EARLY_PART) // 128 * 128
    parts = (slice(0, cut), slice(cut, width))
    for k, cols in enumerate(parts):
        for h, to in ((1, X), (0, Y)):
            src = w.at[pl.ds(units + h * half, half), cols]
            dst = w.at[pl.ds(3 * units + h * half, half), cols]
            remote(src, dst, device(to), "forward", ("forward", k)).start()
    wait_targets(1)
    product(1)
    gradient(1)
    pull_add(1)
    send_affine(1)
    for h, to in ((0, X), (1, Y)):
        src = grad.at[halves(h)]
        remote(src, direct_in.at[halves(h)], device(to), "direct", "direct").start()

    wait_received(("own", 2), w.at[2 * units : 3 * units])
    wait_targets(2)
    product(2)
    gradient(2)
    pull_add(2)
    send_affine(2)

    wait_targets(3)
    early, late = parts
    bias_on.wait_recv()
    wait_received(("forward", 0), w.at[3 * units :, early])
    split_rows(w, 3 * units, w_high, w_low, 0, units, early)
    for side in (1, 0):
        product_part(side, early, True, False, 3)

    blocks = pull_blocks(width)
    pull_swap, step_down = [], []
    row_halves = slice(0, rows // 2), slice(rows // 2, rows)
    for i, cols in enumerate(blocks):
        ends = pull.at[rows:, cols], pull_in.at[:, cols]
        pull_swap.append(remote(*ends, device(PARTNER), "pull", ("pull", i)))
        step_down.append([])
        for k, at in enumerate(row_halves if i == 0 else (slice(0, rows),)):
            ends = pull.at[at, cols], next_in.at[at, cols]
            step_down[i].append(remote(*ends, below, "step", ("step", i, k)))

    def pull_last(side, i):
        if i < len(blocks):
            at = pl.ds(side * rows, rows)
            pull[at, blocks[i]] = pull[at, blocks[i]] + pull_tile(at, blocks[i])

    def swap(i):
        if i < len(blocks):
            pull_swap[i].start()

    def pull_done(i):
        cols = blocks[i]
        pull_swap[i].wait_recv()
        pull[:rows, cols] = -pull_factor * (pull[:rows, cols] + pull_in[:, cols])

    def send_down(i):
        @pl.when(has_prev)
        def _():
            for copy in step_down[i]:
                copy.start()

    wait_received(("forward", 1), w.at[3 * units :, late])
    split_rows(w, 3 * units, w_high, w_low, 0, units, late)
    @pl.when(bits[0] == 0)
    def _():
        for k, at in enumerate(row_halves):
            product_part(at, late, False, True, 3)
            value = pull[at, blocks[0]] + pull_tile(at, blocks[0])
            if k == 0:
                pull_swap[0].wait_recv()
            pull[at, blocks[0]] = -pull_factor * (value + pull_in[at, blocks[0]])

            @pl.when(has_prev)
            def _():
                step_down[0][k].start()

        product_part(1, late, False, True, 3)
        pull_last(1, 0)
        swap(0)
        pull_last(0, 1)
        pull_last(1, 1)
        swap(1)
        pull_done(1)
        send_down(1)

    @pl.when(bits[0] == 1)
    def _():
        product_part(1, late, False, True, 3)
        pull_last(1, 0)
        swap(0)
        product_part(0, late, False, True, 3)
        pull_last(1, 1)
        pull_last(0, 0)
        swap(1)
        pull_last(0, 1)
        pull_done(0)
        send_down(0)
        pull_done(1)
        send_down(1)

    pull_last(1, 2)
    swap(2)
    for i in range(2, len(blocks)):
        pull_last(1, i + 1)
        pull_last(0, i)
        swap(i + 1)
        pull_done(i)
        send_down(i)
    for side in (1, 0):
        m = partial[pl.ds(side * rows, rows), :]
        keep_affine(side, m + target[3, pl.ds(side * rows, rows), :], m, 3)
    send_affine(3)
    gradient(3)
    link_rows = half // LINK_CHUNKS
    merged = {}

    def link_part(h, c):
        return pl.ds(h * half + c * link_rows, link_rows)

    for c in range(LINK_CHUNKS):
        for h, to in ((0, X), (1, Y)):
            at = link_part(h, c)
            src = grad.at[pl.ds(2 * units + h * half + c * link_rows, link_rows)]
            remote(src, relay_in.at[at], device(to), "relay", ("relay", c)).start()
    for c in range(LINK_CHUNKS):
        for h, to in ((1, X), (0, Y)):
            src = grad.at[pl.ds(units + h * half + c * link_rows, link_rows)]
            dst = merged_in.at[link_part(h, c)]
            merged[h, c] = remote(src, dst, device(to), "merged", ("merged", c))

    for k, (low, high) in enumerate(((1, 2), (2, 1), (3, 3))):
        osend[k, :, :half] = osum[low, :, :half]
        osend[k, :, half:] = osum[high, :, half:]
    sums = [
        remote(osend.at[k], orecv.at[k], device(flip), "sums", ("sums", k))
        for k, flip in enumerate((X, Y, X))
    ]


    @pl.when(has_prev)
    def _():
        drive_up.wait_recv()

        @pl.loop(0, rows // 16)
        def _(i):
            at = pl.ds(pl.multiple_of(i * 16, 16), 16)
            prev_in[at, :] = pull[at, :] - step_input * prev_in[at, :]

    p_copy = local(x_ref.at[0], prev_in, "x")

    @pl.when(jnp.logical_not(has_prev))
    def _():
        p_copy.start()
        p_copy.wait()

    sums[0].start()
    sums[2].start()
    wait_sent("pull", pull.at[rows:])
    u_late = local(u_ref.at[0], pull.at[rows:], "u")
    u_late.start()

    @pl.when(has_next)
    def _():
        drive_up.wait_send()

    wait_received("affine", affine.at[:, : width // 2])
    u_late.wait()

    def finish_block(i):
        cols = blocks[i]

        @pl.when(has_next)
        def _():
            for copy in step_down[i]:
                copy.wait_recv()

            @pl.loop(0, rows // 32)
            def _(j):
                offset = pl.multiple_of(j * 32, 32)
                at = pl.ds(offset, 32)
                mults = pull[pl.ds(rows + offset, 32), cols]
                following = next_in[at, cols] - step_input * drive[at, cols]
                total = fit_weight * affine[at, cols] + penalty * following + mults
                fresh = jnp.maximum(0.0, total / (fit_weight + penalty))
                affine[at, cols] = fresh
                drive[at, cols] = mults + penalty * (following - fresh)

        @pl.when(jnp.logical_not(has_next))
        def _():
            @pl.loop(0, rows // 32)
            def _(j):
                offset = pl.multiple_of(j * 32, 32)
                at = pl.ds(offset, 32)
                affine[at, cols] = jnp.maximum(0.0, affine[at, cols])
                drive[at, cols] = pull[pl.ds(rows + offset, 32), cols]

    def merge(c):
        wait_received(("relay", c), relay_in.at[: 2 * link_rows])
        for h in (1, 0):
            start = units + h * half + c * link_rows
            at = pl.ds(start, link_rows)
            grad[at, :] = grad[at, :] + relay_in[link_part(h, c), :]
        for h in (1, 0):
            merged[h, c].start()

    def finish_weights(c):
        wait_received(("merged", c), merged_in.at[: 2 * link_rows])
        for h in (0, 1):
            at = link_part(h, c)
            total = own_grad[at, :] + direct_in[at, :] + merged_in[at, :]
            own_grad[at, :] = w[at, :] - (step_weight * fit_weight * scaling) * total

    def merge_offsets(_):
        wait_received("direct", direct_in)
        sums[2].wait_recv()
        osend[1] = osend[1] + orecv[2]
        sums[1].start()

    def finish_offsets(_):
        sums[0].wait_recv()
        sums[1].wait_recv()
        total = osum[0] + orecv[0] + orecv[1]
        total = jnp.sum(total, axis=0, keepdims=True)
        b_new[...] = own_bias[...] - (step_offset * fit_weight) * total

    ready, stage = [], width / 3
    for i, cols in enumerate(blocks):
        ready.append((cols.stop / stage + 0.2, finish_block, i))
    for c in range(LINK_CHUNKS):
        ready.append((1 + (c + 1) / LINK_CHUNKS, merge, c))
        ready.append((2 + (c + 1) / LINK_CHUNKS, finish_weights, c))
    ready.append((2.1, merge_offsets, 0))
    ready.append((2.6, finish_offsets, 0))
    def settle(_):
        wait_sent("own", w.at[: 2 * units])
        wait_sent("forward", w.at[:units])
        wait_sent("x", pull.at[:rows])
        wait_sent("target", target.at[:, :rows])
        wait_sent("affine", target.at[:, :rows])
        wait_sent("bias", bias.at[1:])
        wait_sent("direct", direct_in)
        wait_sent("relay", relay_in)
        wait_sent("sums", orecv)

    ready.append((blocks[-1].start / stage - 0.1, settle, 0))
    for _, work, i in sorted(ready, key=lambda entry: entry[0]):
        work(i)
    wait_sent("merged", merged_in)

    @pl.when(has_prev)
    def _():
        wait_sent("step", pull.at[:rows])

    counts = len(sends), len(receives), len(locals_)
    if counts != semaphore_counts(width):
        raise ValueError(counts)


def write_kernel(*refs):
    values, outs, sems = refs[:5], refs[5:10], refs[10]
    copies = [pltpu.make_async_copy(*pair, sems.at[i]) for i, pair in enumerate(zip(values, outs))]
    for copy in copies:
        copy.start()
    for copy in copies:
        copy.wait()


def body_fused(layer_inputs, weights, offsets, layer_outputs, multipliers):
    _, rows, width = layer_inputs.shape
    units = weights.shape[1]
    shapes = fused_shapes(rows, width, units)
    samples = rows * lax.axis_size("dp")
    anywhere = pl.BlockSpec(memory_space=pl.ANY)
    vmem = pl.BlockSpec(memory_space=pltpu.VMEM)
    args = (layer_inputs, weights, offsets, layer_outputs, multipliers)
    results = pl.pallas_call(
        functools.partial(fused_kernel, tuple(shapes), samples),
        out_shape=tuple(pltpu.VMEM(a.shape, a.dtype) for a in args),
        in_specs=[anywhere] * 5,
        out_specs=[vmem] * 5,
        scratch_shapes=[pltpu.VMEM(shape, dtype) for shape, dtype in shapes.values()]
        + [pltpu.SemaphoreType.DMA((count,)) for count in semaphore_counts(width)],
        compiler_params=pltpu.CompilerParams(
            collective_id=0,
            has_side_effects=True,
            vmem_limit_bytes=fused_bytes(rows, width, units) + SPARE_BYTES,
        ),
        name="iteration",
    )(*args)
    return pl.pallas_call(
        write_kernel,
        out_shape=tuple(jax.ShapeDtypeStruct(a.shape, a.dtype) for a in args),
        in_specs=[vmem] * 5,
        out_specs=[anywhere] * 5,
        scratch_shapes=[pltpu.SemaphoreType.DMA((5,))],
        compiler_params=pltpu.CompilerParams(vmem_limit_bytes=SPARE_BYTES),
        name="write",
    )(*(pltpu.with_memory_space_constraint(r, pltpu.VMEM) for r in results))


def choose(mesh, layer_inputs, weights, *rest):
    if mesh.shape["dp"] != 8:
        return body_general(layer_inputs, weights, *rest)
    rows, width, units = layer_inputs.shape[1], layer_inputs.shape[2], weights.shape[1]
    tiles = rows % ROW_TILE, width % COLUMN_TILE, units % 256
    held = 4 * (3 * rows + units) * width
    total = fused_bytes(rows, width, units) + held + SPARE_BYTES
    if any(tiles) or total > VMEM_BYTES:
        return body_square(layer_inputs, weights, *rest)
    return body_fused(layer_inputs, weights, *rest)


def solution(mesh):
    specs = (
        P("depth", "dp", None),
        P("depth", "dp", None),
        P("depth", "dp"),
        P("depth", "dp", None),
        P("depth", "dp", None),
    )
    body = functools.partial(choose, mesh)
    return jax.shard_map(body, mesh=mesh, in_specs=specs, out_specs=specs, check_vma=False)
```
